128 devices in a mesh: strike: 8 (over z, x_hi), normal: 16 (over x_lo, y, core).
Axes of the slice: x: 4 (x_hi: 2, x_lo: 2; x = x_hi * 2 + x_lo), y: 4, z: 4, core: 2. Of those that a mesh axis runs over, the one named last changes fastest.
Arguments:
- velocity: float32 [3, 256, 256, 384], P(None, 'strike', 'normal'), may hold values from -6 to 6
- stress: float32 [6, 256, 256, 384], P(None, 'strike', 'normal'), may hold values from -6 to 6
- modulus: float32 [256, 256, 384], P('strike', 'normal'), may hold values from 0.5 to 2
- buoyancy: float32 [256, 256, 384], P('strike', 'normal'), may hold values from 0.5 to 1.5
- fault_state: float32 [256, 384], P(('strike', 'normal')), may hold values from -0.3 to 0.3
- fault_mask: int32 [256, 384], P(('strike', 'normal')), may hold values 0 or 1
- region_ids: int32 [256, 384], P(('strike', 'normal')), may hold values from 0 to 3
- friction_table: float32 [4, 4], replicated, may hold values from 0.2 to 2
Outputs:
- velocity_out: float32 [3, 256, 256, 384], P(None, 'strike', 'normal')
- stress_out: float32 [6, 256, 256, 384], P(None, 'strike', 'normal')
- slip_rate: float32 [256, 384], P(('strike', 'normal'))
- state_out: float32 [256, 384], P(('strike', 'normal'))
The draws below stay inside these ranges and needn't reach their ends.
Inputs may be any that keep to these rules, and one draw needn't show every extreme that they name: `region_ids`: region ids index the columns of friction_table.
All inputs are finite; a program needn't handle non-finite values. No bound on the sum of `fault_mask` on one device may be relied on, other than what follows from the above.
Results may differ from the reference program's by a relative error of at most 0.0003.
Values sent between devices are 32-bit elements; how exact they have to be, the bound alone decides.
No kernel may reach another device: no remote copies, remote signals or barrier semaphores. Data moves between devices by JAX's collectives and lax.ppermute only.
A program may use at most 128 MiB of HBM per device.

```python
import math
import jax
import jax.numpy as jnp
from jax import lax

NZ = 384
STEPS = 2
NEWTON = 4
REGIONS = 4
NX = 256
NY = 256


def touch_ends(entries, rng, least, high):
    longest = entries.shape.index(max(entries.shape))
    spots = []
    for shift in (0, 1):
        where = [jax.random.randint(jax.random.fold_in(rng, axis), (), 0, length) for axis, length in enumerate(entries.shape)]
        where[longest] = (where[longest] + shift) % entries.shape[longest]
        spots.append(tuple(where))
    return entries.at[spots[0]].set(least).at[spots[1]].set(high)


def steps_of(rng, shape, pieces, low, largest):
    loudness = 1.0
    for axis_at, parts in pieces:
        heights = jax.random.uniform(jax.random.fold_in(jax.random.fold_in(rng, 6), axis_at), (parts,), jnp.float32, low / len(pieces), largest / len(pieces))
        loudness = loudness * jnp.repeat(jnp.exp(heights), shape[axis_at] // parts).reshape((-1,) + (1,) * (len(shape) - 1 - axis_at))
    return loudness


def normal_values(own_key, shape, spread, limit, shards=(), dtype=jnp.bfloat16):
    values = jax.random.normal(own_key, shape, jnp.float32) * spread
    if len(shards) > 0:
        values = steps_of(own_key, shape, shards, -0.22, 0.18) * values
    return jnp.clip(values, min=-limit, max=limit).astype(dtype)


def setup_inputs(seed: int = 0) -> dict:
    streams_of = jax.random.split(jax.random.key(seed), 9)
    return {
        "velocity": normal_values(streams_of[0], (3, NX, NY, NZ), 1.0, 6.0, ((1, 8), (2, 16)), jnp.float32),
        "stress": normal_values(streams_of[1], (6, NX, NY, NZ), 1.0, 6.0, ((1, 8), (2, 16)), jnp.float32),
        "modulus": jnp.clip(jnp.exp(math.log(2.0) - 1.3862944 * jax.random.uniform(streams_of[2], (NX, NY, NZ), jnp.float32) ** steps_of(streams_of[2], (NX, NY, NZ), ((0, 8), (1, 16)), -0.2, 0.2)), 0.5, 2.0),
        "buoyancy": jnp.clip(jnp.exp(math.log(1.5) - 1.0986123 * jax.random.uniform(streams_of[3], (NX, NY, NZ), jnp.float32) ** steps_of(streams_of[3], (NX, NY, NZ), ((0, 8), (1, 16)), -0.2, 0.2)), 0.5, 1.5),
        "fault_state": jnp.clip(jax.random.uniform(streams_of[4], (NX, NZ), jnp.float32, -0.3, 0.3) * steps_of(streams_of[4], (NX, NZ), ((0, 128),), -0.4, 0.0), -0.3, 0.3),
        "fault_mask": touch_ends((jax.random.randint(streams_of[5], (NX, NZ), 0, 4) < 3).astype(jnp.int32), jax.random.fold_in(streams_of[5], 1), 0, 1),
        "region_ids": touch_ends(jax.random.randint(streams_of[6], (NX, NZ), 0, REGIONS), jax.random.fold_in(streams_of[6], 1), 0, REGIONS - 1).astype(jnp.int32),
        "friction_table": jnp.clip(jnp.exp(jax.random.uniform(streams_of[7], (4, REGIONS), jnp.float32, math.log(0.2), math.log(2.0))), 0.2, 2.0),
    }


inner_coef = 9.0 / 8.0
outer_coef = -1.0 / 24.0
time_step = 0.1
impedance = 1.0

def inverse_sinh(values):
    magnitude = jnp.abs(values)
    root = jnp.sqrt(1.0 + magnitude * magnitude)
    result = jnp.log1p(magnitude + magnitude * magnitude / (1.0 + root))
    return jnp.where(values < 0.0, -result, result)

def shifted(padded_values, dimension, offset):
    length = padded_values.shape[dimension] - 4
    return lax.slice_in_dim(padded_values, 2 + offset, 2 + offset + length, axis=dimension)

def forward_diff(padded_values, dimension):
    return inner_coef * (shifted(padded_values, dimension, 1) - shifted(padded_values, dimension, 0)) + outer_coef * (shifted(padded_values, dimension, 2) - shifted(padded_values, dimension, -1))

def backward_diff(padded_values, dimension):
    return inner_coef * (shifted(padded_values, dimension, 0) - shifted(padded_values, dimension, -1)) + outer_coef * (shifted(padded_values, dimension, 1) - shifted(padded_values, dimension, -2))

def padded(values, dimension):
    widths = [(0, 0)] * values.ndim
    widths[dimension] = (2, 2)
    return jnp.pad(values, widths)

def accelerate(sxx_x, sxy_x, sxz_x, syy_y, sxy_y, syz_y, sxz, syz, szz):
    accel_x = forward_diff(sxx_x, 0) + backward_diff(sxy_y, 1) + backward_diff(padded(sxz, 2), 2)
    accel_y = backward_diff(sxy_x, 0) + forward_diff(syy_y, 1) + backward_diff(padded(syz, 2), 2)
    accel_z = backward_diff(sxz_x, 0) + backward_diff(syz_y, 1) + forward_diff(padded(szz, 2), 2)
    return jnp.stack((accel_x, accel_y, accel_z))

def strain_rates(vx_x, vy_x, vz_x, vx_y, vy_y, vz_y, vel_x, vel_y, vel_z):
    exx = backward_diff(vx_x, 0)
    eyy = backward_diff(vy_y, 1)
    ezz = backward_diff(padded(vel_z, 2), 2)
    trace = exx + eyy + ezz
    rate_xy = forward_diff(vx_y, 1) + forward_diff(vy_x, 0)
    rate_xz = forward_diff(padded(vel_x, 2), 2) + forward_diff(vz_x, 0)
    rate_yz = forward_diff(padded(vel_y, 2), 2) + forward_diff(vz_y, 1)
    return jnp.stack((trace + 2.0 * exx, trace + 2.0 * eyy, trace + 2.0 * ezz, rate_xy, rate_xz, rate_yz))

def friction(minus, plus, traction, state_now, mask_now, params):
    direct_effect = params[0]
    evolution_b = params[1]
    inverse_length = params[2]
    normal_stress = params[3]
    locked = traction + impedance * (plus - minus)
    scale_c = 0.5 * jnp.exp(state_now / direct_effect)
    weight = normal_stress * direct_effect
    rate = jnp.zeros_like(locked)
    for newton_step in range(NEWTON):
        argument = scale_c * rate
        residue = locked - impedance * rate - weight * inverse_sinh(argument)
        slope = impedance + weight * scale_c / jnp.sqrt(1.0 + argument * argument)
        rate = rate + residue / slope
    rate = rate * mask_now
    traction_new = locked - impedance * rate
    middle = 0.5 * (minus + plus)
    state_new = state_now + time_step * inverse_length * (jnp.exp(-state_now / evolution_b) - jnp.abs(rate))
    return (rate, traction_new, middle - 0.5 * rate, middle + 0.5 * rate, state_new)

def reference(velocity, stress, modulus, buoyancy, fault_state, fault_mask, region_ids, friction_table):
    center = NY // 2
    params = friction_table[:, region_ids]
    mask_now = fault_mask.astype(jnp.float32)
    state_now = fault_state
    rate = jnp.zeros_like(fault_state)
    for time_index in range(STEPS):
        accel = accelerate(padded(stress[0], 0), padded(stress[3], 0), padded(stress[4], 0), padded(stress[1], 1), padded(stress[3], 1), padded(stress[5], 1), stress[4], stress[5], stress[2])
        velocity = velocity + time_step * buoyancy * accel
        vel_x = velocity[0]
        rate, traction_new, minus_new, plus_new, state_now = friction(vel_x[:, center - 1, :], vel_x[:, center, :], stress[3][:, center - 1, :], state_now, mask_now, params)
        vel_x = vel_x.at[:, center - 1, :].set(minus_new).at[:, center, :].set(plus_new)
        velocity = velocity.at[0].set(vel_x)
        rates = strain_rates(padded(velocity[0], 0), padded(velocity[1], 0), padded(velocity[2], 0), padded(velocity[0], 1), padded(velocity[1], 1), padded(velocity[2], 1), velocity[0], velocity[1], velocity[2])
        stress = stress + time_step * modulus * rates
        stress = stress.at[3, :, center - 1, :].set(traction_new)
    return (velocity, stress, rate, state_now)
```

```python
import jax
import jax.numpy as jnp
from jax import lax
from jax.sharding import PartitionSpec as P

STEPS = 2
NEWTON = 4

C1 = 9.0 / 8.0
C2 = -1.0 / 24.0
DT = 0.1
ETA = 1.0


def shift_up(x, axis):
    count = lax.axis_size(axis)
    return lax.ppermute(x, axis, [(i, (i + 1) % count) for i in range(count)])


def shift_down(x, axis):
    count = lax.axis_size(axis)
    return lax.ppermute(x, axis, [((i + 1) % count, i) for i in range(count)])


def swap_odd(x, axis):
    count = lax.axis_size(axis)
    pairs = []
    for i in range(1, count, 2):
        j = (i + 1) % count
        pairs += [(i, j), (j, i)]
    return lax.ppermute(x, axis, pairs)


def inverse_sinh(values):
    magnitude = jnp.abs(values)
    root = jnp.sqrt(1.0 + magnitude * magnitude)
    result = jnp.log1p(magnitude + magnitude * magnitude / (1.0 + root))
    return jnp.where(values < 0.0, -result, result)


def sl(f, dim, lo, hi):
    return lax.slice_in_dim(f, lo, hi, axis=dim)


def ext(f, low, high, dim):
    return jnp.concatenate([low, f, high], axis=dim)


def dplus(g, dim):
    n = g.shape[dim] - 3
    at = lambda o: sl(g, dim, 1 + o, 1 + o + n)
    return C1 * (at(1) - at(0)) + C2 * (at(2) - at(-1))


def dminus(g, dim):
    n = g.shape[dim] - 3
    at = lambda o: sl(g, dim, 2 + o, 2 + o + n)
    return C1 * (at(0) - at(-1)) + C2 * (at(1) - at(-2))


def zpad(f, lo, hi):
    return jnp.pad(f, ((0, 0), (0, 0), (lo, hi)))


def friction(minus, plus, traction, state_now, mask_now, params):
    a, b, inv_len, sigma = params
    locked = traction + ETA * (plus - minus)
    c = 0.5 * jnp.exp(state_now / a)
    weight = sigma * a
    rate = jnp.zeros_like(locked)
    for _ in range(NEWTON):
        arg = c * rate
        residue = locked - ETA * rate - weight * inverse_sinh(arg)
        slope = ETA + weight * c / jnp.sqrt(1.0 + arg * arg)
        rate = rate + residue / slope
    rate = rate * mask_now
    middle = 0.5 * (minus + plus)
    state_new = state_now + DT * inv_len * (jnp.exp(-state_now / b) - jnp.abs(rate))
    return rate, locked - ETA * rate, middle - 0.5 * rate, middle + 0.5 * rate, state_new


def local(velocity, stress, modulus, buoyancy, fault_state, fault_mask, region_ids, friction_table):
    members = lax.axis_size("normal")
    position = lax.axis_index("normal")
    strike = lax.axis_index("strike")
    last_strike = lax.axis_size("strike") - 1
    odd = position % 2 == 1
    on_minus = position == members // 2 - 1
    on_plus = position == members // 2
    nx, ny = velocity.shape[1], velocity.shape[2]

    own = jnp.stack(
        (fault_state, fault_mask.astype(jnp.float32), region_ids.astype(jnp.float32))
    )
    rows = own.shape[1]
    spread = jnp.broadcast_to(own[None], (members,) + own.shape)
    gathered = lax.all_to_all(spread, "normal", 0, 0, tiled=True)
    gathered = jnp.transpose(gathered, (1, 0, 2, 3)).reshape(3, members * rows, -1)
    state_now, mask_now, regions = gathered[0], gathered[1], gathered[2]
    params = []
    for k in range(4):
        p = jnp.zeros_like(regions)
        for r in range(friction_table.shape[1]):
            p = jnp.where(regions == r, friction_table[k, r], p)
        params.append(p)

    vx, vy, vz = velocity[0], velocity[1], velocity[2]
    sxx, syy, szz, sxy, sxz, syz = (stress[i] for i in range(6))

    def exchange(up, down, axis, dim, first, last):
        low = shift_up(jnp.concatenate(up, dim), axis)
        high = shift_down(jnp.concatenate(down, dim), axis)
        return jnp.where(first, 0.0, low), jnp.where(last, 0.0, high)

    for _ in range(STEPS):
        xl, xh = exchange(
            (sl(sxx, 0, nx - 1, nx), sl(sxy, 0, nx - 2, nx), sl(sxz, 0, nx - 2, nx)),
            (sl(sxx, 0, 0, 2), sl(sxy, 0, 0, 1), sl(sxz, 0, 0, 1)),
            "strike", 0, strike == 0, strike == last_strike,
        )
        yl, yh = exchange(
            (sl(syy, 1, ny - 1, ny), sl(sxy, 1, ny - 2, ny), sl(syz, 1, ny - 2, ny)),
            (sl(syy, 1, 0, 2), sl(sxy, 1, 0, 1), sl(syz, 1, 0, 1)),
            "normal", 1, position == 0, position == members - 1,
        )
        ax = (
            dplus(ext(sxx, xl[0:1], xh[0:2], 0), 0)
            + dminus(ext(sxy, yl[:, 1:3], yh[:, 2:3], 1), 1)
            + dminus(zpad(sxz, 2, 1), 2)
        )
        ay = (
            dminus(ext(sxy, xl[1:3], xh[2:3], 0), 0)
            + dplus(ext(syy, yl[:, 0:1], yh[:, 0:2], 1), 1)
            + dminus(zpad(syz, 2, 1), 2)
        )
        az = (
            dminus(ext(sxz, xl[3:5], xh[3:4], 0), 0)
            + dminus(ext(syz, yl[:, 3:5], yh[:, 3:4], 1), 1)
            + dplus(zpad(szz, 1, 2), 2)
        )
        step = DT * buoyancy
        vx, vy, vz = vx + step * ax, vy + step * ay, vz + step * az

        mine = jnp.where(odd, vx[:, ny - 1], vx[:, 0])
        other = swap_odd(mine, "normal")
        minus = jnp.where(odd, mine, other)
        plus = jnp.where(odd, other, mine)
        traction = jnp.where(odd, sxy[:, ny - 1], yl[:, 2])
        rate, traction_new, minus_new, plus_new, state_now = friction(
            minus, plus, traction, state_now, mask_now, params
        )
        row_at = lax.broadcasted_iota(jnp.int32, (1, ny, 1), 1)
        vx = jnp.where(on_minus & (row_at == ny - 1), minus_new[:, None], vx)
        vx = jnp.where(on_plus & (row_at == 0), plus_new[:, None], vx)

        xl, xh = exchange(
            (sl(vx, 0, nx - 2, nx), sl(vy, 0, nx - 1, nx), sl(vz, 0, nx - 1, nx)),
            (sl(vx, 0, 0, 1), sl(vy, 0, 0, 2), sl(vz, 0, 0, 2)),
            "strike", 0, strike == 0, strike == last_strike,
        )
        yl, yh = exchange(
            (sl(vy, 1, ny - 2, ny), sl(vx, 1, ny - 1, ny), sl(vz, 1, ny - 1, ny)),
            (sl(vy, 1, 0, 1), sl(vx, 1, 0, 2), sl(vz, 1, 0, 2)),
            "normal", 1, position == 0, position == members - 1,
        )
        exx = dminus(ext(vx, xl[0:2], xh[0:1], 0), 0)
        eyy = dminus(ext(vy, yl[:, 0:2], yh[:, 0:1], 1), 1)
        ezz = dminus(zpad(vz, 2, 1), 2)
        trace = exx + eyy + ezz
        exy = dplus(ext(vx, yl[:, 2:3], yh[:, 1:3], 1), 1) + dplus(
            ext(vy, xl[2:3], xh[1:3], 0), 0
        )
        exz = dplus(zpad(vx, 1, 2), 2) + dplus(ext(vz, xl[3:4], xh[3:5], 0), 0)
        eyz = dplus(zpad(vy, 1, 2), 2) + dplus(ext(vz, yl[:, 3:4], yh[:, 3:5], 1), 1)
        scale = DT * modulus
        sxx = sxx + scale * (trace + 2.0 * exx)
        syy = syy + scale * (trace + 2.0 * eyy)
        szz = szz + scale * (trace + 2.0 * ezz)
        sxy = sxy + scale * exy
        sxz = sxz + scale * exz
        syz = syz + scale * eyz
        sxy = jnp.where(on_minus & (row_at == ny - 1), traction_new[:, None], sxy)

    back = jnp.stack((rate, state_now)).reshape(2, members, rows, -1).transpose(1, 0, 2, 3)
    back = lax.all_to_all(back, "normal", 0, 0, tiled=True)[members // 2]
    return (
        jnp.stack((vx, vy, vz)),
        jnp.stack((sxx, syy, szz, sxy, sxz, syz)),
        back[0],
        back[1],
    )


def solution(mesh):
    block = P(None, "strike", "normal", None)
    part = P("strike", "normal", None)
    row = P(("strike", "normal"), None)
    return jax.shard_map(
        local,
        mesh=mesh,
        in_specs=(block, block, part, part, row, row, row, P()),
        out_specs=(block, block, row, row),
        check_vma=False,
    )
```

```python
import functools

import jax
import jax.numpy as jnp
from jax import lax
from jax.experimental import pallas as pl
from jax.experimental.pallas import tpu as pltpu
from jax.sharding import PartitionSpec as P

STEPS = 2
NEWTON = 4

C1 = 9.0 / 8.0
C2 = -1.0 / 24.0
DT = 0.1
ETA = 1.0

F32 = jnp.float32
SXX, SYY, SZZ, SXY, SXZ, SYZ = range(6)


def shift_up(x, axis):
    count = lax.axis_size(axis)
    return lax.ppermute(x, axis, [(i, (i + 1) % count) for i in range(count)])


def shift_down(x, axis):
    count = lax.axis_size(axis)
    return lax.ppermute(x, axis, [((i + 1) % count, i) for i in range(count)])


def swap_odd(x, axis):
    count = lax.axis_size(axis)
    pairs = []
    for i in range(1, count, 2):
        j = (i + 1) % count
        pairs += [(i, j), (j, i)]
    return lax.ppermute(x, axis, pairs)


VMEM = pl.BlockSpec(memory_space=pltpu.VMEM)
SMEM = pl.BlockSpec(memory_space=pltpu.SMEM)
ANY = pl.BlockSpec(memory_space=pl.ANY)


def call(body, ins, outs, args, scratch=(), aliases=None, cost=None, name=None):
    shapes = [
        pltpu.VMEM(shape, F32) if spec is VMEM else jax.ShapeDtypeStruct(shape, F32)
        for shape, spec in outs
    ]
    return pl.pallas_call(
        body,
        out_shape=shapes,
        in_specs=ins,
        out_specs=[spec for _, spec in outs],
        scratch_shapes=list(scratch),
        input_output_aliases=aliases or {},
        compiler_params=pltpu.CompilerParams(vmem_limit_bytes=16 << 20),
        cost_estimate=cost,
        name=name,
    )(*args)


LANES = 128


def masked(shape, offset, value):
    i = lax.broadcasted_iota(jnp.int32, shape, 0)
    n = shape[0]
    keep = i >= -offset if offset < 0 else i < n - offset
    return jnp.where(keep, jnp.asarray(value, F32), 0.0)


class Coefs:
    def __init__(self, ny):
        self.ny = ny
        self.t = {}
        for offset, value in ((-1, C1), (1, C2), (-2, C2), (1, C1), (2, C2), (-1, C2)):
            self.t[offset, value] = masked((ny, LANES), offset, value)
        self.lane = lax.broadcasted_iota(jnp.int32, (ny, LANES), 1)

    def y(self, f, offset, value):
        return pltpu.roll(f, (-offset) % self.ny, 0) * self.t[offset, value]

    def y_minus(self, fs):
        return [
            C1 * f - self.y(f, -1, C1) + self.y(f, 1, C2) - self.y(f, -2, C2) for f in fs
        ]

    def y_plus(self, fs):
        return [
            self.y(f, 1, C1) - C1 * f + self.y(f, 2, C2) - self.y(f, -1, C2) for f in fs
        ]

    def z(self, fs, offset):
        rolls = [pltpu.roll(f, (-offset) % LANES, 1) for f in fs]
        keep = self.lane < LANES - offset if offset > 0 else self.lane >= -offset
        out = []
        for k, r in enumerate(rolls):
            j = k + 1 if offset > 0 else k - 1
            out.append(jnp.where(keep, r, rolls[j] if 0 <= j < len(fs) else 0.0))
        return out

    def z_minus(self, fs):
        return [
            C1 * (f - b) + C2 * (c - d)
            for f, b, c, d in zip(fs, self.z(fs, -1), self.z(fs, 1), self.z(fs, -2))
        ]

    def z_plus(self, fs):
        return [
            C1 * (b - f) + C2 * (c - d)
            for f, b, c, d in zip(fs, self.z(fs, 1), self.z(fs, 2), self.z(fs, -1))
        ]


def add(*lists):
    return [functools.reduce(lambda p, q: p + q, parts) for parts in zip(*lists)]


def tile(k):
    return slice(k * LANES, (k + 1) * LANES)


def to_tiles(source, target, sems):
    return [
        pltpu.make_async_copy(source.at[:, tile(k)], target.at[k], sems.at[k])
        for k in range(target.shape[0])
    ]


def from_tiles(source, target, sems):
    return [
        pltpu.make_async_copy(source.at[k], target.at[:, tile(k)], sems.at[k])
        for k in range(source.shape[0])
    ]


def run(copies):
    for c in copies:
        c.start()
    for c in copies:
        c.wait()


MINUS = ((0, C1), (-1, -C1), (1, C2), (-2, -C2))
PLUS = ((1, C1), (0, -C1), (2, C2), (-1, -C2))


def slab(ref, comp, at):
    if comp is None:
        return [ref[k, at, :] for k in range(ref.shape[0])]
    return [ref[comp, k, at, :] for k in range(ref.shape[1])]


def x_terms(ref, comp, x, nx, ny, static, pairs):
    total = None
    for offset, coef in pairs:
        if static and not 0 <= x + offset < nx:
            continue
        start = (x + offset) * ny
        if not static:
            start = pl.multiple_of(start, 8)
        term = [coef * f for f in slab(ref, comp, pl.ds(start, ny))]
        total = term if total is None else add(total, term)
    return total


def over_x(nx, body):
    for x in (0, 1, nx - 2, nx - 1):
        body(x, True)

    def step(x, carry):
        body(x, False)
        return carry

    lax.fori_loop(2, nx - 2, step, 0)


def velocity_body(nx, ny, first, s, v_in, b_in, v, *refs):
    tiles = s.shape[1]
    if first:
        bd, sem = refs
        copies = to_tiles(b_in, bd, sem.at[3])
        for c in range(3):
            copies += to_tiles(v_in.at[c], v.at[c], sem.at[c])
        run(copies)
    cf = Coefs(ny)

    def body(x, static):
        start = x * ny if static else pl.multiple_of(x * ny, 8)
        at = pl.ds(start, ny)
        xt = functools.partial(x_terms, s, x=x, nx=nx, ny=ny, static=static)
        sxy, sxz, syz = slab(s, SXY, at), slab(s, SXZ, at), slab(s, SYZ, at)
        a = (
            add(xt(SXX, pairs=PLUS), cf.y_minus(sxy), cf.z_minus(sxz)),
            add(xt(SXY, pairs=MINUS), cf.y_plus(slab(s, SYY, at)), cf.z_minus(syz)),
            add(xt(SXZ, pairs=MINUS), cf.y_minus(syz), cf.z_plus(slab(s, SZZ, at))),
        )
        src = v if first else v_in
        for k in range(tiles):
            if first:
                w = DT * bd[k, at, :]
                bd[k, at, :] = w
            else:
                w = b_in[k, at, :]
            for c in range(3):
                v[c, k, at, :] = src[c, k, at, :] + w * a[c][k]

    over_x(nx, body)


def stress_body(nx, ny, first, last, *refs):
    refs = list(refs)
    v, s_in, m_in = refs[:3]
    refs = refs[3:]
    s = refs.pop(0)
    md = refs.pop(0) if first else m_in
    v_out = refs.pop(0) if last else None
    sem = refs.pop(0) if first or last else None
    tiles = s.shape[1]
    if first:
        run(to_tiles(m_in, md, sem.at[0]))
    if last:
        out = []
        for c in range(3):
            out += from_tiles(v.at[c], v_out.at[c], sem.at[c])
        for c in out:
            c.start()
    cf = Coefs(ny)

    def body(x, static):
        start = x * ny if static else pl.multiple_of(x * ny, 8)
        at = pl.ds(start, ny)
        xt = functools.partial(x_terms, v, x=x, nx=nx, ny=ny, static=static)
        vx, vy, vz = slab(v, 0, at), slab(v, 1, at), slab(v, 2, at)
        exx = xt(0, pairs=MINUS)
        eyy = cf.y_minus(vy)
        ezz = cf.z_minus(vz)
        exy = add(xt(1, pairs=PLUS), cf.y_plus(vx))
        exz = add(xt(2, pairs=PLUS), cf.z_plus(vx))
        eyz = add(cf.z_plus(vy), cf.y_plus(vz))
        tr = add(exx, eyy, ezz)
        for k in range(tiles):
            w = md[k, at, :]
            if first:
                w = DT * w
                md[k, at, :] = w
            s[SXX, k, at, :] = s_in[SXX, k, at, :] + w * (tr[k] + 2.0 * exx[k])
            s[SYY, k, at, :] = s_in[SYY, k, at, :] + w * (tr[k] + 2.0 * eyy[k])
            s[SZZ, k, at, :] = s_in[SZZ, k, at, :] + w * (tr[k] + 2.0 * ezz[k])
            s[SXY, k, at, :] = s_in[SXY, k, at, :] + w * exy[k]
            s[SXZ, k, at, :] = s_in[SXZ, k, at, :] + w * exz[k]
            s[SYZ, k, at, :] = s_in[SYZ, k, at, :] + w * eyz[k]

    over_x(nx, body)
    if last:
        for c in out:
            c.wait()


class Edges:
    def __init__(self, nx, ny):
        self.nx, self.ny = nx, ny

    def x(self, i):
        return pl.ds(i * self.ny, self.ny)

    def y(self, i):
        return pl.ds(i, self.nx, stride=self.ny)


def minus_edges(n, low, high):
    return (
        (0, -C1 * low[1] - C2 * low[0]),
        (1, -C2 * low[1]),
        (n - 1, C2 * high[0]),
    )


def plus_edges(n, low, high):
    return (
        (0, -C2 * low[0]),
        (n - 1, C1 * high[0] + C2 * high[1]),
        (n - 2, C2 * high[0]),
    )


def sides():
    out = []
    for axis in ("strike", "normal"):
        i = lax.axis_index(axis)
        last = lax.axis_size(axis) - 1
        out += [jnp.where(i > 0, 1.0, 0.0).astype(F32), jnp.where(i < last, 1.0, 0.0).astype(F32)]
    return out


def add_rows(ref, comp, w, at, factor, value):
    ref[comp, :, at, :] = ref[comp, :, at, :] + w[:, at, :] * (factor * value if factor != 1.0 else value)


def pack_stress_x(s, e, up, down):
    nx = e.nx
    for k, (c, i) in enumerate(
        ((SXX, nx - 1), (SXY, nx - 2), (SXY, nx - 1), (SXZ, nx - 2), (SXZ, nx - 1))
    ):
        up[k] = s[c, :, e.x(i), :]
    for k, (c, i) in enumerate(((SXX, 0), (SXX, 1), (SXY, 0), (SXZ, 0))):
        down[k] = s[c, :, e.x(i), :]


def pack_stress_y(s, e, up, down):
    ny = e.ny
    for k, (c, i) in enumerate(
        ((SYY, ny - 1), (SXY, ny - 2), (SXY, ny - 1), (SYZ, ny - 2), (SYZ, ny - 1))
    ):
        up[k] = s[c, :, e.y(i), :]
    for k, (c, i) in enumerate(((SYY, 0), (SYY, 1), (SXY, 0), (SYZ, 0))):
        down[k] = s[c, :, e.y(i), :]


def load_body(nx, ny, stress, s, xu, xd, yu, yd, sem):
    e = Edges(nx, ny)
    order = (SXX, SXY, SXZ, SYY, SYZ, SZZ)
    copies = {c: to_tiles(stress.at[c], s.at[c], sem.at[c]) for c in order}

    def wait(*comps):
        for c in comps:
            for copy in copies[c]:
                copy.wait()

    for c in order:
        for copy in copies[c]:
            copy.start()
    wait(SXX, SXY, SXZ)
    pack_stress_x(s, e, xu, xd)
    wait(SYY, SYZ)
    pack_stress_y(s, e, yu, yd)
    wait(SZZ)


def velocity_edges_body(nx, ny, v_in, w, s, xl, xh, yl, yh, v, yu, yd, mine, traction):
    del v_in
    e = Edges(nx, ny)
    fxl, fxh, fyl, fyh = sides()
    a = [xl[k] * fxl for k in range(5)]
    b = [xh[k] * fxh for k in range(4)]
    for comp, terms in (
        (0, plus_edges(nx, a[0:1], b[0:2])),
        (1, minus_edges(nx, a[1:3], b[2:3])),
        (2, minus_edges(nx, a[3:5], b[3:4])),
    ):
        for i, value in terms:
            add_rows(v, comp, w, e.x(i), 1.0, value)
    a = [yl[k] * fyl for k in range(5)]
    b = [yh[k] * fyh for k in range(4)]
    for comp, terms in (
        (1, plus_edges(ny, a[0:1], b[0:2])),
        (0, minus_edges(ny, a[1:3], b[2:3])),
        (2, minus_edges(ny, a[3:5], b[3:4])),
    ):
        for i, value in terms:
            add_rows(v, comp, w, e.y(i), 1.0, value)
    odd = lax.rem(lax.axis_index("normal"), 2) == 1
    mine[...] = jnp.where(odd, v[0, :, e.y(ny - 1), :], v[0, :, e.y(0), :])
    traction[...] = jnp.where(odd, s[SXY, :, e.y(ny - 1), :], yl[2])
    for k, (c, i) in enumerate(((1, ny - 2), (1, ny - 1), (0, ny - 1), (2, ny - 1))):
        yu[k] = v[c, :, e.y(i), :]
    for k, (c, i) in enumerate(((1, 0), (0, 0), (0, 1), (2, 0), (2, 1))):
        yd[k] = v[c, :, e.y(i), :]


def inverse_sinh(values):
    magnitude = jnp.abs(values)
    root = jnp.sqrt(1.0 + magnitude * magnitude)
    result = jnp.log1p(magnitude + magnitude * magnitude / (1.0 + root))
    return jnp.where(values < 0.0, -result, result)


def fault_body(nx, ny, last, *refs):
    mine, other, traction, par, st_in, v_in, v, xu, xd, st, minus_o, plus_o, trac_o = refs[:13]
    del v_in
    e = Edges(nx, ny)
    position = lax.axis_index("normal")
    members = lax.axis_size("normal")
    odd = lax.rem(position, 2) == 1
    on_minus = position == members // 2 - 1
    on_plus = position == members // 2
    m, o = mine[...], other[...]
    minus = jnp.where(odd, m, o)
    plus = jnp.where(odd, o, m)
    mask, a, b, inv_len, sigma = (par[k] for k in range(5))
    state = st_in[...]
    locked = traction[...] + ETA * (plus - minus)
    c = 0.5 * jnp.exp(state / a)
    weight = sigma * a
    rate = jnp.zeros_like(locked)
    for _ in range(NEWTON):
        arg = c * rate
        residue = locked - ETA * rate - weight * inverse_sinh(arg)
        slope = ETA + weight * c / jnp.sqrt(1.0 + arg * arg)
        rate = rate + residue / slope
    rate = rate * mask
    state = state + DT * inv_len * (jnp.exp(-state / b) - jnp.abs(rate))
    st[...] = state
    trac_o[...] = locked - ETA * rate
    middle = 0.5 * (minus + plus)
    minus = middle - 0.5 * rate
    plus = middle + 0.5 * rate
    minus_o[...] = minus
    plus_o[...] = plus
    v[0, :, e.y(ny - 1), :] = jnp.where(on_minus, minus, v[0, :, e.y(ny - 1), :])
    v[0, :, e.y(0), :] = jnp.where(on_plus, plus, v[0, :, e.y(0), :])
    for k, (comp, i) in enumerate(((0, nx - 2), (0, nx - 1), (1, nx - 1), (2, nx - 1))):
        xu[k] = v[comp, :, e.x(i), :]
    for k, (comp, i) in enumerate(((0, 0), (1, 0), (1, 1), (2, 0), (2, 1))):
        xd[k] = v[comp, :, e.x(i), :]
    if last:
        back, tmp = refs[13:]
        tmp[0] = rate
        tmp[1] = state
        count = nx // back.shape[0]
        for k in range(back.shape[0]):
            for q in range(2):
                for z in range(tmp.shape[1]):
                    back[k, q * count : (q + 1) * count, tile(z)] = tmp[
                        q, z, k * count : (k + 1) * count, :
                    ]
        pad = back.shape[1] - 2 * count
        if pad:
            back[:, 2 * count :, :] = jnp.zeros((back.shape[0], pad, back.shape[2]), F32)


def stress_edges_body(nx, ny, last, rows, *refs):
    s_in, w, xl, xh, yl, yh, minus, plus, traction = refs[:9]
    del s_in
    e = Edges(nx, ny)
    fxl, fxh, fyl, fyh = sides()
    position = lax.axis_index("normal")
    members = lax.axis_size("normal")
    on_minus = position == members // 2 - 1
    on_plus = position == members // 2
    if last:
        recv, s, out, slip, state, sem = refs[9:]
    else:
        s, xu, xd, yu, yd = refs[9:]
    a = [xl[k] * fxl for k in range(4)]
    b = [xh[k] * fxh for k in range(5)]
    for i, value in minus_edges(nx, a[0:2], b[0:1]):
        add_rows(s, SXX, w, e.x(i), 3.0, value)
        add_rows(s, SYY, w, e.x(i), 1.0, value)
        add_rows(s, SZZ, w, e.x(i), 1.0, value)
    for i, value in plus_edges(nx, a[2:3], b[1:3]):
        add_rows(s, SXY, w, e.x(i), 1.0, value)
    for i, value in plus_edges(nx, a[3:4], b[3:5]):
        add_rows(s, SXZ, w, e.x(i), 1.0, value)
    a = [yl[k] * fyl for k in range(4)]
    b = [yh[k] * fyh for k in range(5)]
    a[2] = jnp.where(on_plus, minus[...], a[2])
    b[1] = jnp.where(on_minus, plus[...], b[1])
    for i, value in minus_edges(ny, a[0:2], b[0:1]):
        add_rows(s, SXX, w, e.y(i), 1.0, value)
        add_rows(s, SYY, w, e.y(i), 3.0, value)
        add_rows(s, SZZ, w, e.y(i), 1.0, value)
    for i, value in plus_edges(ny, a[2:3], b[1:3]):
        add_rows(s, SXY, w, e.y(i), 1.0, value)
    for i, value in plus_edges(ny, a[3:4], b[3:5]):
        add_rows(s, SYZ, w, e.y(i), 1.0, value)
    s[SXY, :, e.y(ny - 1), :] = jnp.where(on_minus, traction[...], s[SXY, :, e.y(ny - 1), :])
    if last:
        copies = []
        for c in range(6):
            copies += from_tiles(s.at[c], out.at[c], sem.at[c])
        for copy in copies:
            copy.start()
        slip[...] = recv[members // 2, 0:rows, :]
        state[...] = recv[members // 2, rows : 2 * rows, :]
        for copy in copies:
            copy.wait()
    else:
        pack_stress_x(s, e, xu, xd)
        pack_stress_y(s, e, yu, yd)


def own_body(state, mask, ids, out):
    rows = state.shape[0]
    block = jnp.concatenate((state[...], mask[...].astype(F32), ids[...].astype(F32)), 0)
    pad = out.shape[1] - 3 * rows
    if pad:
        block = jnp.concatenate((block, jnp.zeros((pad, block.shape[1]), F32)), 0)
    for k in range(out.shape[0]):
        out[k] = block


def parameters_body(rows, recv, table, st, par, tmp):
    for k in range(recv.shape[0]):
        at = slice(k * rows, (k + 1) * rows)
        for z in range(st.shape[0]):
            st[z, at, :] = recv[k, 0:rows, tile(z)]
            par[0, z, at, :] = recv[k, rows : 2 * rows, tile(z)]
            tmp[z, at, :] = recv[k, 2 * rows : 3 * rows, tile(z)]
    ids = tmp[...]
    for j in range(4):
        p = jnp.zeros_like(ids)
        for r in range(table.shape[1]):
            p = jnp.where(ids == float(r), table[j, r], p)
        par[1 + j] = p


def local(velocity, stress, modulus, buoyancy, fault_state, fault_mask, region_ids, friction_table):
    members = lax.axis_size("normal")
    _, nx, ny, nz = velocity.shape
    rows = fault_state.shape[0]
    flat, nt = nx * ny, nz // LANES
    vel_in = velocity.reshape(3, flat, nz)
    str_in = stress.reshape(6, flat, nz)
    mod_in = modulus.reshape(flat, nz)
    buo_in = buoyancy.reshape(flat, nz)
    dma = lambda n: pltpu.SemaphoreType.DMA((n, nt))
    stage_cost = pl.CostEstimate(flops=4_000_000_000, bytes_accessed=16_000_000, transcendentals=0)
    side_cost = pl.CostEstimate(flops=1_000_000, bytes_accessed=1_000_000, transcendentals=0)

    depth = -(-3 * rows // 8) * 8
    (spread,) = call(
        own_body, [VMEM] * 3, [((members, depth, nz), VMEM)],
        (fault_state, fault_mask, region_ids), cost=side_cost, name="own",
    )
    s, xu, xd, yu, yd = call(
        functools.partial(load_body, nx, ny), [ANY],
        [((6, nt, flat, LANES), VMEM), ((5, nt, ny, LANES), VMEM), ((4, nt, ny, LANES), VMEM),
         ((5, nt, nx, LANES), VMEM), ((4, nt, nx, LANES), VMEM)],
        (str_in,), scratch=[dma(6)], cost=side_cost, name="load",
    )
    recv = lax.all_to_all(spread, "normal", 0, 0, tiled=True)
    state, par = call(
        functools.partial(parameters_body, rows), [VMEM, SMEM],
        [((nt, nx, LANES), VMEM), ((5, nt, nx, LANES), VMEM)], (recv, friction_table),
        scratch=[pltpu.VMEM((nt, nx, LANES), F32)], cost=side_cost, name="parameters",
    )
    v = w = m = None
    for step in range(STEPS):
        first, last = step == 0, step == STEPS - 1
        xl, xh = shift_up(xu, "strike"), shift_down(xd, "strike")
        yl, yh = shift_up(yu, "normal"), shift_down(yd, "normal")
        if first:
            v, w = call(
                functools.partial(velocity_body, nx, ny, True), [VMEM, ANY, ANY],
                [((3, nt, flat, LANES), VMEM), ((nt, flat, LANES), VMEM)], (s, vel_in, buo_in),
                scratch=[dma(4)], cost=stage_cost, name="velocity_first",
            )
        else:
            (v,) = call(
                functools.partial(velocity_body, nx, ny, False),
                [VMEM] * 3, [((3, nt, flat, LANES), VMEM)], (s, v, w),
                aliases={1: 0}, cost=stage_cost, name="velocity",
            )
        v, yu, yd, mine, traction = call(
            functools.partial(velocity_edges_body, nx, ny), [VMEM] * 7,
            [((3, nt, flat, LANES), VMEM), ((4, nt, nx, LANES), VMEM), ((5, nt, nx, LANES), VMEM),
             ((nt, nx, LANES), VMEM), ((nt, nx, LANES), VMEM)],
            (v, w, s, xl, xh, yl, yh), aliases={0: 0}, cost=side_cost, name="velocity_edges",
        )
        other = swap_odd(mine, "normal")
        yl, yh = shift_up(yu, "normal"), shift_down(yd, "normal")
        back_depth = -(-2 * rows // 8) * 8
        outs = [((3, nt, flat, LANES), VMEM), ((4, nt, ny, LANES), VMEM), ((5, nt, ny, LANES), VMEM)]
        outs += [((nt, nx, LANES), VMEM)] * 4
        if last:
            outs.append(((members, back_depth, nz), VMEM))
        got = call(
            functools.partial(fault_body, nx, ny, last), [VMEM] * 6, outs,
            (mine, other, traction, par, state, v),
            scratch=[pltpu.VMEM((2, nt, nx, LANES), F32)] if last else [],
            aliases={5: 0}, cost=side_cost, name="fault",
        )
        v, xu, xd, state, minus, plus, trac_new = got[:7]
        xl, xh = shift_up(xu, "strike"), shift_down(xd, "strike")
        outs = [((6, nt, flat, LANES), VMEM)]
        if first:
            outs.append(((nt, flat, LANES), VMEM))
        if last:
            outs.append(((3, flat, nz), ANY))
        got_s = call(
            functools.partial(stress_body, nx, ny, first, last),
            [VMEM, VMEM, ANY if first else VMEM], outs, (v, s, mod_in if first else m),
            scratch=[dma(3)] if first or last else [], aliases={1: 0}, cost=stage_cost,
            name="stress",
        )
        s = got_s[0]
        if first:
            m = got_s[1]
        edge_in = (s, m, xl, xh, yl, yh, minus, plus, trac_new)
        if last:
            v_out = got_s[-1]
            recv = lax.all_to_all(got[7], "normal", 0, 0, tiled=True)
            _, s_out, slip, state_out = call(
                functools.partial(stress_edges_body, nx, ny, True, rows), [VMEM] * 10,
                [((6, nt, flat, LANES), VMEM), ((6, flat, nz), ANY), ((rows, nz), ANY_VMEM), ((rows, nz), ANY_VMEM)],
                edge_in + (recv,), scratch=[dma(6)], aliases={0: 0}, cost=side_cost,
                name="stress_edges_last",
            )
        else:
            s, xu, xd, yu, yd = call(
                functools.partial(stress_edges_body, nx, ny, False, rows), [VMEM] * 9,
                [((6, nt, flat, LANES), VMEM), ((5, nt, ny, LANES), VMEM), ((4, nt, ny, LANES), VMEM),
                 ((5, nt, nx, LANES), VMEM), ((4, nt, nx, LANES), VMEM)],
                edge_in, aliases={0: 0}, cost=side_cost, name="stress_edges",
            )
    return (
        v_out.reshape(3, nx, ny, nz),
        s_out.reshape(6, nx, ny, nz),
        slip,
        state_out,
    )


ANY_VMEM = pl.BlockSpec(memory_space=pltpu.MemorySpace.VMEM)


def solution(mesh):
    block = P(None, "strike", "normal", None)
    part = P("strike", "normal", None)
    row = P(("strike", "normal"), None)
    return jax.shard_map(
        local,
        mesh=mesh,
        in_specs=(block, block, part, part, row, row, row, P()),
        out_specs=(block, block, row, row),
        check_vma=False,
    )
```

```python
import functools

import jax
import jax.numpy as jnp
from jax import lax
from jax.experimental import pallas as pl
from jax.experimental.pallas import tpu as pltpu
from jax.sharding import PartitionSpec as P

STEPS = 2
NEWTON = 4

C1 = 9.0 / 8.0
C2 = -1.0 / 24.0
DT = 0.1
ETA = 1.0

F32 = jnp.float32
SXX, SYY, SZZ, SXY, SXZ, SYZ = range(6)


def shift_up(x, axis):
    count = lax.axis_size(axis)
    return lax.ppermute(x, axis, [(i, (i + 1) % count) for i in range(count)])


def shift_down(x, axis):
    count = lax.axis_size(axis)
    return lax.ppermute(x, axis, [((i + 1) % count, i) for i in range(count)])


def swap_odd(x, axis):
    count = lax.axis_size(axis)
    pairs = []
    for i in range(1, count, 2):
        j = (i + 1) % count
        pairs += [(i, j), (j, i)]
    return lax.ppermute(x, axis, pairs)


def swap(x, bit):
    count = lax.axis_size("normal")
    return lax.ppermute(x, "normal", [(i, i ^ bit) for i in range(count)])


VMEM = pl.BlockSpec(memory_space=pltpu.VMEM)
SMEM = pl.BlockSpec(memory_space=pltpu.SMEM)
HBM = pl.BlockSpec(memory_space=pltpu.HBM)


def call(body, ins, outs, args, scratch=(), aliases=None, cost=None, name=None):
    shapes = [
        pltpu.VMEM(shape, F32) if spec is VMEM else jax.ShapeDtypeStruct(shape, F32)
        for shape, spec in outs
    ]
    return pl.pallas_call(
        body,
        out_shape=shapes,
        in_specs=ins,
        out_specs=[spec for _, spec in outs],
        scratch_shapes=list(scratch),
        input_output_aliases=aliases or {},
        compiler_params=pltpu.CompilerParams(vmem_limit_bytes=16 << 20),
        cost_estimate=cost,
        name=name,
    )(*args)


LANES = 128


def masked(shape, offset, value):
    i = lax.broadcasted_iota(jnp.int32, shape, 0)
    n = shape[0]
    keep = i >= -offset if offset < 0 else i < n - offset
    return jnp.where(keep, jnp.asarray(value, F32), 0.0)


class Coefs:
    def __init__(self, ny):
        self.ny = ny
        self.t = {}
        for offset, value in ((-1, C1), (1, C2), (-2, C2), (1, C1), (2, C2), (-1, C2)):
            self.t[offset, value] = masked((ny, LANES), offset, value)
        self.lane = lax.broadcasted_iota(jnp.int32, (ny, LANES), 1)

    def y(self, f, offset, value):
        return pltpu.roll(f, (-offset) % self.ny, 0) * self.t[offset, value]

    def y_minus(self, fs):
        return [
            C1 * f - self.y(f, -1, C1) + self.y(f, 1, C2) - self.y(f, -2, C2) for f in fs
        ]

    def y_plus(self, fs):
        return [
            self.y(f, 1, C1) - C1 * f + self.y(f, 2, C2) - self.y(f, -1, C2) for f in fs
        ]

    def z(self, fs, offset):
        rolls = [pltpu.roll(f, (-offset) % LANES, 1) for f in fs]
        keep = self.lane < LANES - offset if offset > 0 else self.lane >= -offset
        out = []
        for k, r in enumerate(rolls):
            j = k + 1 if offset > 0 else k - 1
            out.append(jnp.where(keep, r, rolls[j] if 0 <= j < len(fs) else 0.0))
        return out

    def z_minus(self, fs):
        return [
            C1 * (f - b) + C2 * (c - d)
            for f, b, c, d in zip(fs, self.z(fs, -1), self.z(fs, 1), self.z(fs, -2))
        ]

    def z_plus(self, fs):
        return [
            C1 * (b - f) + C2 * (c - d)
            for f, b, c, d in zip(fs, self.z(fs, 1), self.z(fs, 2), self.z(fs, -1))
        ]


def add(*lists):
    return [functools.reduce(lambda p, q: p + q, parts) for parts in zip(*lists)]


def tile(k):
    return slice(k * LANES, (k + 1) * LANES)


def to_tiles(source, target, sems):
    return [
        pltpu.make_async_copy(source.at[:, tile(k)], target.at[k], sems.at[k])
        for k in range(target.shape[0])
    ]


def from_tiles(source, target, sems):
    return [
        pltpu.make_async_copy(source.at[k], target.at[:, tile(k)], sems.at[k])
        for k in range(source.shape[0])
    ]


def run(copies):
    for c in copies:
        c.start()
    for c in copies:
        c.wait()


MINUS = ((0, C1), (-1, -C1), (1, C2), (-2, -C2))
PLUS = ((1, C1), (0, -C1), (2, C2), (-1, -C2))


def slab(ref, comp, at):
    if comp is None:
        return [ref[k, at, :] for k in range(ref.shape[0])]
    return [ref[comp, k, at, :] for k in range(ref.shape[1])]


def x_terms(ref, comp, x, nx, ny, static, pairs):
    total = None
    for offset, coef in pairs:
        if static and not 0 <= x + offset < nx:
            continue
        start = (x + offset) * ny
        if not static:
            start = pl.multiple_of(start, 8)
        term = [coef * f for f in slab(ref, comp, pl.ds(start, ny))]
        total = term if total is None else add(total, term)
    return total


def over_x(nx, body):
    for x in (0, 1, nx - 2, nx - 1):
        body(x, True)

    def step(x, carry):
        body(x, False)
        return carry

    lax.fori_loop(2, nx - 2, step, 0)


def velocity_body(nx, ny, first, s, v_in, b_in, *refs):
    tiles = s.shape[1]
    if first:
        m_in, v, bd, md, sem = refs
        copies = to_tiles(b_in, bd, sem.at[3])
        for c in range(3):
            copies += to_tiles(v_in.at[c], v.at[c], sem.at[c])
        late = to_tiles(m_in, md, sem.at[4])
        for c in copies + late:
            c.start()
        for c in copies:
            c.wait()
    else:
        (v,) = refs
    cf = Coefs(ny)

    def body(x, static):
        start = x * ny if static else pl.multiple_of(x * ny, 8)
        at = pl.ds(start, ny)
        xt = functools.partial(x_terms, s, x=x, nx=nx, ny=ny, static=static)
        sxy, sxz, syz = slab(s, SXY, at), slab(s, SXZ, at), slab(s, SYZ, at)
        a = (
            add(xt(SXX, pairs=PLUS), cf.y_minus(sxy), cf.z_minus(sxz)),
            add(xt(SXY, pairs=MINUS), cf.y_plus(slab(s, SYY, at)), cf.z_minus(syz)),
            add(xt(SXZ, pairs=MINUS), cf.y_minus(syz), cf.z_plus(slab(s, SZZ, at))),
        )
        src = v if first else v_in
        for k in range(tiles):
            if first:
                w = DT * bd[k, at, :]
                bd[k, at, :] = w
            else:
                w = b_in[k, at, :]
            for c in range(3):
                v[c, k, at, :] = src[c, k, at, :] + w * a[c][k]

    over_x(nx, body)
    if first:
        for c in late:
            c.wait()


def stress_body(nx, ny, first, last, v, s_in, m_in, *refs):
    if last:
        yl, yh, minus, plus, traction, s, v_out, s_out, sem = refs
        md = m_in
        out = []
        for c in range(3):
            out += from_tiles(v.at[c], v_out.at[c], sem.at[c])
        for c in out:
            c.start()
        e = Edges(nx, ny)
        stress_y_terms(s, md, e, ny, yl, yh, minus, plus)
        s_in = s
    elif first:
        s, md = refs
    else:
        (s,) = refs
        md = m_in
    tiles = s.shape[1]
    cf = Coefs(ny)

    def body(x, static):
        start = x * ny if static else pl.multiple_of(x * ny, 8)
        at = pl.ds(start, ny)
        xt = functools.partial(x_terms, v, x=x, nx=nx, ny=ny, static=static)
        vx, vy, vz = slab(v, 0, at), slab(v, 1, at), slab(v, 2, at)
        exx = xt(0, pairs=MINUS)
        eyy = cf.y_minus(vy)
        ezz = cf.z_minus(vz)
        exy = add(xt(1, pairs=PLUS), cf.y_plus(vx))
        exz = add(xt(2, pairs=PLUS), cf.z_plus(vx))
        eyz = add(cf.z_plus(vy), cf.y_plus(vz))
        tr = add(exx, eyy, ezz)
        for k in range(tiles):
            if first:
                w = DT * m_in[k, at, :]
                md[k, at, :] = w
            else:
                w = md[k, at, :]
            s[SXX, k, at, :] = s_in[SXX, k, at, :] + w * (tr[k] + 2.0 * exx[k])
            s[SYY, k, at, :] = s_in[SYY, k, at, :] + w * (tr[k] + 2.0 * eyy[k])
            s[SZZ, k, at, :] = s_in[SZZ, k, at, :] + w * (tr[k] + 2.0 * ezz[k])
            s[SXY, k, at, :] = s_in[SXY, k, at, :] + w * exy[k]
            s[SXZ, k, at, :] = s_in[SXZ, k, at, :] + w * exz[k]
            s[SYZ, k, at, :] = s_in[SYZ, k, at, :] + w * eyz[k]

    if not last:
        over_x(nx, body)
        return

    for x in (0, 1, nx - 2, nx - 1):
        body(x, True)
    on_minus, _ = fault_side()

    def step(x, carry):
        body(x, False)
        return carry

    begin, width = 2, -(-(nx - 4) // 4)
    for stop in range(begin + width, nx - 2 + width, width):
        stop = min(stop, nx - 2)
        lax.fori_loop(begin, stop, step, 0)
        at = pl.ds(begin * ny + ny - 1, stop - begin, stride=ny)
        s[SXY, :, at, :] = jnp.where(on_minus, traction[:, begin:stop, :], s[SXY, :, at, :])
        span = pl.ds(begin * ny, (stop - begin) * ny)
        for c in range(6):
            for k in range(tiles):
                copy = pltpu.make_async_copy(
                    s.at[c, k, span], s_out.at[c, span, tile(k)], sem.at[3 + c, k]
                )
                copy.start()
                out.append(copy)
        begin = stop
    for c in out:
        c.wait()


class Edges:
    def __init__(self, nx, ny):
        self.nx, self.ny = nx, ny

    def x(self, i):
        return pl.ds(i * self.ny, self.ny)

    def y(self, i):
        return pl.ds(i, self.nx, stride=self.ny)


def minus_edges(n, low, high):
    return (
        (0, -C1 * low[1] - C2 * low[0]),
        (1, -C2 * low[1]),
        (n - 1, C2 * high[0]),
    )


def plus_edges(n, low, high):
    return (
        (0, -C2 * low[0]),
        (n - 1, C1 * high[0] + C2 * high[1]),
        (n - 2, C2 * high[0]),
    )


def sides():
    out = []
    for axis in ("strike", "normal"):
        i = lax.axis_index(axis)
        last = lax.axis_size(axis) - 1
        out += [jnp.where(i > 0, 1.0, 0.0).astype(F32), jnp.where(i < last, 1.0, 0.0).astype(F32)]
    return out


def fault_side():
    position = lax.axis_index("normal")
    half = lax.axis_size("normal") // 2
    return position == half - 1, position == half


def stress_x_terms(s, w, e, nx, xl, xh):
    low, high = sides()[:2]
    a = [xl[k] * low for k in range(4)]
    b = [xh[k] * high for k in range(5)]
    for i, value in minus_edges(nx, a[0:2], b[0:1]):
        add_rows(s, SXX, w, e.x(i), 3.0, value)
        add_rows(s, SYY, w, e.x(i), 1.0, value)
        add_rows(s, SZZ, w, e.x(i), 1.0, value)
    for i, value in plus_edges(nx, a[2:3], b[1:3]):
        add_rows(s, SXY, w, e.x(i), 1.0, value)
    for i, value in plus_edges(nx, a[3:4], b[3:5]):
        add_rows(s, SXZ, w, e.x(i), 1.0, value)


def stress_y_terms(s, w, e, ny, yl, yh, minus, plus):
    low, high = sides()[2:]
    on_minus, on_plus = fault_side()
    a = [yl[k] * low for k in range(4)]
    b = [yh[k] * high for k in range(5)]
    a[2] = jnp.where(on_plus, minus[...], a[2])
    b[1] = jnp.where(on_minus, plus[...], b[1])
    for i, value in minus_edges(ny, a[0:2], b[0:1]):
        add_rows(s, SXX, w, e.y(i), 1.0, value)
        add_rows(s, SYY, w, e.y(i), 3.0, value)
        add_rows(s, SZZ, w, e.y(i), 1.0, value)
    for i, value in plus_edges(ny, a[2:3], b[1:3]):
        add_rows(s, SXY, w, e.y(i), 1.0, value)
    for i, value in plus_edges(ny, a[3:4], b[3:5]):
        add_rows(s, SYZ, w, e.y(i), 1.0, value)


def add_rows(ref, comp, w, at, factor, value):
    ref[comp, :, at, :] = ref[comp, :, at, :] + w[:, at, :] * (factor * value if factor != 1.0 else value)


def pack_stress_x(s, e, up, down):
    nx = e.nx
    for k, (c, i) in enumerate(
        ((SXX, nx - 1), (SXY, nx - 2), (SXY, nx - 1), (SXZ, nx - 2), (SXZ, nx - 1))
    ):
        up[k] = s[c, :, e.x(i), :]
    for k, (c, i) in enumerate(((SXX, 0), (SXX, 1), (SXY, 0), (SXZ, 0))):
        down[k] = s[c, :, e.x(i), :]


def pack_stress_y(s, e, up, down):
    ny = e.ny
    for k, (c, i) in enumerate(
        ((SYY, ny - 1), (SXY, ny - 2), (SXY, ny - 1), (SYZ, ny - 2), (SYZ, ny - 1))
    ):
        up[k] = s[c, :, e.y(i), :]
    for k, (c, i) in enumerate(((SYY, 0), (SYY, 1), (SXY, 0), (SYZ, 0))):
        down[k] = s[c, :, e.y(i), :]


def load_body(nx, ny, stress, s, xu, xd, yu, yd, sem):
    e = Edges(nx, ny)
    order = (SXX, SXY, SXZ, SYY, SYZ, SZZ)
    copies = {c: to_tiles(stress.at[c], s.at[c], sem.at[c]) for c in order}

    def wait(*comps):
        for c in comps:
            for copy in copies[c]:
                copy.wait()

    for c in order:
        for copy in copies[c]:
            copy.start()
    wait(SXX, SXY, SXZ)
    pack_stress_x(s, e, xu, xd)
    wait(SYY, SYZ)
    pack_stress_y(s, e, yu, yd)
    wait(SZZ)


def velocity_edges_body(nx, ny, v_in, w, s, xl, xh, yl, yh, v, yu, yd, mine, traction):
    del v_in
    e = Edges(nx, ny)
    fxl, fxh, fyl, fyh = sides()
    a = [xl[k] * fxl for k in range(5)]
    b = [xh[k] * fxh for k in range(4)]
    for comp, terms in (
        (0, plus_edges(nx, a[0:1], b[0:2])),
        (1, minus_edges(nx, a[1:3], b[2:3])),
        (2, minus_edges(nx, a[3:5], b[3:4])),
    ):
        for i, value in terms:
            add_rows(v, comp, w, e.x(i), 1.0, value)
    a = [yl[k] * fyl for k in range(5)]
    b = [yh[k] * fyh for k in range(4)]
    for comp, terms in (
        (1, plus_edges(ny, a[0:1], b[0:2])),
        (0, minus_edges(ny, a[1:3], b[2:3])),
        (2, minus_edges(ny, a[3:5], b[3:4])),
    ):
        for i, value in terms:
            add_rows(v, comp, w, e.y(i), 1.0, value)
    odd = lax.rem(lax.axis_index("normal"), 2) == 1
    mine[...] = jnp.where(odd, v[0, :, e.y(ny - 1), :], v[0, :, e.y(0), :])
    traction[...] = jnp.where(odd, s[SXY, :, e.y(ny - 1), :], yl[2])
    for k, (c, i) in enumerate(((1, ny - 2), (1, ny - 1), (0, ny - 1), (2, ny - 1))):
        yu[k] = v[c, :, e.y(i), :]
    for k, (c, i) in enumerate(((1, 0), (0, 0), (0, 1), (2, 0), (2, 1))):
        yd[k] = v[c, :, e.y(i), :]


def inverse_sinh(values):
    magnitude = jnp.abs(values)
    root = jnp.sqrt(1.0 + magnitude * magnitude)
    result = jnp.log1p(magnitude + magnitude * magnitude / (1.0 + root))
    return jnp.where(values < 0.0, -result, result)


def fault_body(nx, ny, last, *refs):
    mine, other, traction, par, st_in, v_in, v, xu, xd, st, minus_o, plus_o, trac_o = refs[:13]
    del v_in
    e = Edges(nx, ny)
    position = lax.axis_index("normal")
    members = lax.axis_size("normal")
    odd = lax.rem(position, 2) == 1
    on_minus, on_plus = fault_side()
    m, o = mine[...], other[...]
    minus = jnp.where(odd, m, o)
    plus = jnp.where(odd, o, m)
    mask, a, b, inv_len, sigma = (par[k] for k in range(5))
    state = st_in[...]
    locked = traction[...] + ETA * (plus - minus)
    c = 0.5 * jnp.exp(state / a)
    weight = sigma * a
    rate = jnp.zeros_like(locked)
    for _ in range(NEWTON):
        arg = c * rate
        residue = locked - ETA * rate - weight * inverse_sinh(arg)
        slope = ETA + weight * c / jnp.sqrt(1.0 + arg * arg)
        rate = rate + residue / slope
    rate = rate * mask
    state = state + DT * inv_len * (jnp.exp(-state / b) - jnp.abs(rate))
    st[...] = state
    trac_o[...] = locked - ETA * rate
    middle = 0.5 * (minus + plus)
    minus = middle - 0.5 * rate
    plus = middle + 0.5 * rate
    minus_o[...] = minus
    plus_o[...] = plus
    v[0, :, e.y(ny - 1), :] = jnp.where(on_minus, minus, v[0, :, e.y(ny - 1), :])
    v[0, :, e.y(0), :] = jnp.where(on_plus, plus, v[0, :, e.y(0), :])
    for k, (comp, i) in enumerate(((0, nx - 2), (0, nx - 1), (1, nx - 1), (2, nx - 1))):
        xu[k] = v[comp, :, e.x(i), :]
    for k, (comp, i) in enumerate(((0, 0), (1, 0), (1, 1), (2, 0), (2, 1))):
        xd[k] = v[comp, :, e.x(i), :]
    if last:
        (back,) = refs[13:]
        half = nx // 2
        upper = position >= members // 2
        for q, value in enumerate((rate, state)):
            back[q] = jnp.where(upper, value[:, half:, :], value[:, :half, :])


def choose_body(holders, mine, got, out):
    out[...] = jnp.where(holds(holders), mine[...], got[...])


def holds(holders):
    position = lax.axis_index("normal")
    return functools.reduce(lambda p, q: p | q, [position == h for h in holders])


def stress_edges_body(nx, ny, s_in, w, xl, xh, yl, yh, minus, plus, traction, s, xu, xd, yu, yd):
    del s_in
    e = Edges(nx, ny)
    on_minus, _ = fault_side()
    stress_x_terms(s, w, e, nx, xl, xh)
    stress_y_terms(s, w, e, ny, yl, yh, minus, plus)
    s[SXY, :, e.y(ny - 1), :] = jnp.where(on_minus, traction[...], s[SXY, :, e.y(ny - 1), :])
    pack_stress_x(s, e, xu, xd)
    pack_stress_y(s, e, yu, yd)


def stress_last_body(nx, ny, rows, holders, s, w, xl, xh, traction, mine, got, o_in, out, slip, state, sem):
    del o_in
    e = Edges(nx, ny)
    on_minus, _ = fault_side()
    stress_x_terms(s, w, e, nx, xl, xh)
    copies = []
    for x in (0, 1, nx - 2, nx - 1):
        at = pl.ds(x * ny + ny - 1, 1)
        s[SXY, :, at, :] = jnp.where(on_minus, traction[:, x : x + 1, :], s[SXY, :, at, :])
    for j, x in enumerate((0, nx - 2)):
        span = pl.ds(x * ny, 2 * ny)
        for c in range(6):
            for k in range(s.shape[1]):
                copies.append(
                    pltpu.make_async_copy(
                        s.at[c, k, span], out.at[c, span, tile(k)], sem.at[j * 6 + c, k]
                    )
                )
    for c in copies:
        c.start()
    half = lax.axis_size("normal") // 2
    at = pl.ds(rows * lax.rem(lax.axis_index("normal"), half), rows)
    have = holds(holders)
    for k in range(s.shape[1]):
        slip[:, tile(k)] = jnp.where(have, mine[0, k, at, :], got[0, k, at, :])
        state[:, tile(k)] = jnp.where(have, mine[1, k, at, :], got[1, k, at, :])
    for c in copies:
        c.wait()


def own_body(state, mask, ids, out, st, mk, rg, sem):
    rows = state.shape[0]
    run(
        [
            pltpu.make_async_copy(a, b, sem.at[0, k])
            for k, (a, b) in enumerate(((state, st), (mask, mk), (ids, rg)))
        ]
    )
    out[0, 0:rows, :] = st[...]
    out[0, rows : 2 * rows, :] = mk[...].astype(F32)
    out[0, 2 * rows : 3 * rows, :] = rg[...].astype(F32)
    pad = out.shape[1] - 3 * rows
    if pad:
        out[0, 3 * rows :, :] = jnp.zeros((pad, out.shape[2]), F32)


def merge_body(bit, mine, got, out):
    upper = lax.rem(lax.axis_index("normal") // bit, 2) == 1
    n = mine.shape[0]
    a, b = mine[...], got[...]
    out[0:n] = jnp.where(upper, b, a)
    out[n : 2 * n] = jnp.where(upper, a, b)


def parameters_body(rows, mine, got, table, st, par, tmp):
    half = mine.shape[0]
    upper = lax.axis_index("normal") >= half
    for k in range(2 * half):
        at = slice(k * rows, (k + 1) * rows)
        a, b = (mine, got) if k < half else (got, mine)
        block = jnp.where(upper, b[k % half], a[k % half])
        for z in range(st.shape[0]):
            st[z, at, :] = block[0:rows, tile(z)]
            par[0, z, at, :] = block[rows : 2 * rows, tile(z)]
            tmp[z, at, :] = block[2 * rows : 3 * rows, tile(z)]
    ids = tmp[...]
    for j in range(4):
        p = jnp.zeros_like(ids)
        for r in range(table.shape[1]):
            p = jnp.where(ids == float(r), table[j, r], p)
        par[1 + j] = p


def local(velocity, stress, modulus, buoyancy, fault_state, fault_mask, region_ids, friction_table):
    members = lax.axis_size("normal")
    _, nx, ny, nz = velocity.shape
    rows = fault_state.shape[0]
    flat, nt = nx * ny, nz // LANES
    vel_in = velocity.reshape(3, flat, nz)
    str_in = stress.reshape(6, flat, nz)
    mod_in = modulus.reshape(flat, nz)
    buo_in = buoyancy.reshape(flat, nz)
    dma = lambda n: pltpu.SemaphoreType.DMA((n, nt))
    stage_cost = pl.CostEstimate(flops=4_000_000_000, bytes_accessed=16_000_000, transcendentals=0)
    side_cost = pl.CostEstimate(flops=1_000_000, bytes_accessed=1_000_000, transcendentals=0)

    depth = -(-3 * rows // 8) * 8
    (known,) = call(
        own_body, [HBM] * 3, [((1, depth, nz), VMEM)], (fault_state, fault_mask, region_ids),
        scratch=[pltpu.VMEM((rows, nz), F32)] + [pltpu.VMEM((rows, nz), jnp.int32)] * 2 + [dma(1)],
        cost=side_cost, name="own",
    )
    s, xu, xd, yu, yd = call(
        functools.partial(load_body, nx, ny), [HBM],
        [((6, nt, flat, LANES), VMEM), ((5, nt, ny, LANES), VMEM), ((4, nt, ny, LANES), VMEM),
         ((5, nt, nx, LANES), VMEM), ((4, nt, nx, LANES), VMEM)],
        (str_in,), scratch=[dma(6)], cost=side_cost, name="load",
    )
    bit = 1
    while 2 * bit < members:
        (known,) = call(
            functools.partial(merge_body, bit), [VMEM] * 2, [((2 * bit, depth, nz), VMEM)],
            (known, swap(known, bit)), cost=side_cost, name="merge",
        )
        bit *= 2
    state, par = call(
        functools.partial(parameters_body, rows), [VMEM, VMEM, SMEM],
        [((nt, nx, LANES), VMEM), ((5, nt, nx, LANES), VMEM)],
        (known, swap(known, bit), friction_table),
        scratch=[pltpu.VMEM((nt, nx, LANES), F32)], cost=side_cost, name="parameters",
    )
    block_v = ((3, nt, flat, LANES), VMEM)
    block_s = ((6, nt, flat, LANES), VMEM)
    block_1 = ((nt, flat, LANES), VMEM)
    row_1 = ((nt, nx, LANES), VMEM)
    v = w = m = None
    for step in range(STEPS):
        first, last = step == 0, step == STEPS - 1
        xl, xh = shift_up(xu, "strike"), shift_down(xd, "strike")
        yl, yh = shift_up(yu, "normal"), shift_down(yd, "normal")
        if first:
            v, w, m = call(
                functools.partial(velocity_body, nx, ny, True), [VMEM, HBM, HBM, HBM],
                [block_v, block_1, block_1], (s, vel_in, buo_in, mod_in),
                scratch=[dma(5)], cost=stage_cost, name="velocity_first",
            )
        else:
            (v,) = call(
                functools.partial(velocity_body, nx, ny, False), [VMEM] * 3, [block_v], (s, v, w),
                aliases={1: 0}, cost=stage_cost, name="velocity",
            )
        v, yu, yd, mine, traction = call(
            functools.partial(velocity_edges_body, nx, ny), [VMEM] * 7,
            [block_v, ((4, nt, nx, LANES), VMEM), ((5, nt, nx, LANES), VMEM), row_1, row_1],
            (v, w, s, xl, xh, yl, yh), aliases={0: 0}, cost=side_cost, name="velocity_edges",
        )
        other = swap_odd(mine, "normal")
        yl, yh = shift_up(yu, "normal"), shift_down(yd, "normal")
        outs = [block_v, ((4, nt, ny, LANES), VMEM), ((5, nt, ny, LANES), VMEM)] + [row_1] * 4
        if last:
            outs.append(((2, nt, nx // 2, LANES), VMEM))
        got = call(
            functools.partial(fault_body, nx, ny, last), [VMEM] * 6, outs,
            (mine, other, traction, par, state, v), aliases={5: 0}, cost=side_cost, name="fault",
        )
        v, xu, xd, state, minus, plus, trac_new = got[:7]
        xl, xh = shift_up(xu, "strike"), shift_down(xd, "strike")
        body = functools.partial(stress_body, nx, ny, first, last)
        if last:
            back, holders = got[7], [members // 2 - 1, members // 2]
            bit = members // 4
            while bit > 1:
                (back,) = call(
                    functools.partial(choose_body, tuple(holders)), [VMEM] * 2,
                    [((2, nt, nx // 2, LANES), VMEM)], (back, swap(back, bit)),
                    cost=side_cost, name="choose",
                )
                holders += [h ^ bit for h in holders]
                bit //= 2
            brought = swap(back, 1)
            s, v_out, s_out = call(
                body, [VMEM] * 8, [block_s, ((3, flat, nz), HBM), ((6, flat, nz), HBM)],
                (v, s, m, yl, yh, minus, plus, trac_new),
                scratch=[dma(9)], aliases={1: 0}, cost=stage_cost, name="stress_last",
            )
            s_out, slip, state_out = call(
                functools.partial(stress_last_body, nx, ny, rows, tuple(holders)),
                [VMEM] * 7 + [HBM], [((6, flat, nz), HBM), ((rows, nz), VMEM), ((rows, nz), VMEM)],
                (s, m, xl, xh, trac_new, back, brought, s_out), scratch=[dma(12)],
                aliases={7: 0}, cost=side_cost, name="edges_last",
            )
            continue
        if first:
            s, m = call(
                body, [VMEM] * 3, [block_s, block_1], (v, s, m), aliases={1: 0, 2: 1},
                cost=stage_cost, name="stress_first",
            )
        else:
            (s,) = call(
                body, [VMEM] * 3, [block_s], (v, s, m), aliases={1: 0}, cost=stage_cost,
                name="stress",
            )
        s, xu, xd, yu, yd = call(
            functools.partial(stress_edges_body, nx, ny), [VMEM] * 9,
            [block_s, ((5, nt, ny, LANES), VMEM), ((4, nt, ny, LANES), VMEM),
             ((5, nt, nx, LANES), VMEM), ((4, nt, nx, LANES), VMEM)],
            (s, m, xl, xh, yl, yh, minus, plus, trac_new), aliases={0: 0}, cost=side_cost,
            name="stress_edges",
        )
    return (
        v_out.reshape(3, nx, ny, nz),
        s_out.reshape(6, nx, ny, nz),
        slip,
        state_out,
    )


def solution(mesh):
    block = P(None, "strike", "normal", None)
    part = P("strike", "normal", None)
    row = P(("strike", "normal"), None)
    return jax.shard_map(
        local,
        mesh=mesh,
        in_specs=(block, block, part, part, row, row, row, P()),
        out_specs=(block, block, row, row),
        check_vma=False,
    )
```

```python
import functools

import jax
import jax.numpy as jnp
from jax import lax
from jax.experimental import pallas as pl
from jax.experimental.pallas import tpu as pltpu
from jax.sharding import PartitionSpec as P

STEPS = 2
NEWTON = 4

C1 = 9.0 / 8.0
C2 = -1.0 / 24.0
DT = 0.1
ETA = 1.0

F32 = jnp.float32
SXX, SYY, SZZ, SXY, SXZ, SYZ = range(6)


def shift_up(x, axis):
    count = lax.axis_size(axis)
    return lax.ppermute(x, axis, [(i, (i + 1) % count) for i in range(count)])


def shift_down(x, axis):
    count = lax.axis_size(axis)
    return lax.ppermute(x, axis, [((i + 1) % count, i) for i in range(count)])


def swap_odd(x, axis):
    count = lax.axis_size(axis)
    pairs = []
    for i in range(1, count, 2):
        j = (i + 1) % count
        pairs += [(i, j), (j, i)]
    return lax.ppermute(x, axis, pairs)


def swap(x, bit):
    count = lax.axis_size("normal")
    return lax.ppermute(x, "normal", [(i, i ^ bit) for i in range(count)])


VMEM = pl.BlockSpec(memory_space=pltpu.VMEM)
SMEM = pl.BlockSpec(memory_space=pltpu.SMEM)
HBM = pl.BlockSpec(memory_space=pltpu.HBM)


def call(body, ins, outs, args, scratch=(), aliases=None, cost=None, name=None):
    shapes = [
        pltpu.VMEM(shape, F32) if spec is VMEM else jax.ShapeDtypeStruct(shape, F32)
        for shape, spec in outs
    ]
    return pl.pallas_call(
        body,
        out_shape=shapes,
        in_specs=ins,
        out_specs=[spec for _, spec in outs],
        scratch_shapes=list(scratch),
        input_output_aliases=aliases or {},
        compiler_params=pltpu.CompilerParams(vmem_limit_bytes=16 << 20),
        cost_estimate=cost,
        name=name,
    )(*args)


LANES = 128


def masked(shape, offset, value):
    i = lax.broadcasted_iota(jnp.int32, shape, 0)
    n = shape[0]
    keep = i >= -offset if offset < 0 else i < n - offset
    return jnp.where(keep, jnp.asarray(value, F32), 0.0)


class Coefs:
    def __init__(self, ny):
        self.ny = ny
        self.t = {}
        for offset, value in ((-1, C1), (1, C2), (-2, C2), (1, C1), (2, C2), (-1, C2)):
            self.t[offset, value] = masked((ny, LANES), offset, value)
        self.lane = lax.broadcasted_iota(jnp.int32, (ny, LANES), 1)

    def y(self, f, offset, value):
        return pltpu.roll(f, (-offset) % self.ny, 0) * self.t[offset, value]

    def y_minus(self, fs):
        return [
            C1 * f - self.y(f, -1, C1) + self.y(f, 1, C2) - self.y(f, -2, C2) for f in fs
        ]

    def y_plus(self, fs):
        return [
            self.y(f, 1, C1) - C1 * f + self.y(f, 2, C2) - self.y(f, -1, C2) for f in fs
        ]

    def z(self, fs, offset):
        rolls = [pltpu.roll(f, (-offset) % LANES, 1) for f in fs]
        keep = self.lane < LANES - offset if offset > 0 else self.lane >= -offset
        out = []
        for k, r in enumerate(rolls):
            j = k + 1 if offset > 0 else k - 1
            out.append(jnp.where(keep, r, rolls[j] if 0 <= j < len(fs) else 0.0))
        return out

    def z_minus(self, fs):
        return [
            C1 * (f - b) + C2 * (c - d)
            for f, b, c, d in zip(fs, self.z(fs, -1), self.z(fs, 1), self.z(fs, -2))
        ]

    def z_plus(self, fs):
        return [
            C1 * (b - f) + C2 * (c - d)
            for f, b, c, d in zip(fs, self.z(fs, 1), self.z(fs, 2), self.z(fs, -1))
        ]


def add(*lists):
    return [functools.reduce(lambda p, q: p + q, parts) for parts in zip(*lists)]


def tile(k):
    return slice(k * LANES, (k + 1) * LANES)


def to_tiles(source, target, sems):
    return [
        pltpu.make_async_copy(source.at[:, tile(k)], target.at[k], sems.at[k])
        for k in range(target.shape[0])
    ]


def from_tiles(source, target, sems):
    return [
        pltpu.make_async_copy(source.at[k], target.at[:, tile(k)], sems.at[k])
        for k in range(source.shape[0])
    ]


def run(copies):
    for c in copies:
        c.start()
    for c in copies:
        c.wait()


MINUS = ((0, C1), (-1, -C1), (1, C2), (-2, -C2))
PLUS = ((1, C1), (0, -C1), (2, C2), (-1, -C2))


def slab(ref, comp, at):
    if comp is None:
        return [ref[k, at, :] for k in range(ref.shape[0])]
    return [ref[comp, k, at, :] for k in range(ref.shape[1])]


def x_terms(ref, comp, x, nx, ny, static, pairs):
    total = None
    for offset, coef in pairs:
        if static and not 0 <= x + offset < nx:
            continue
        start = (x + offset) * ny
        if not static:
            start = pl.multiple_of(start, 8)
        term = [coef * f for f in slab(ref, comp, pl.ds(start, ny))]
        total = term if total is None else add(total, term)
    return total


def over_x(nx, body):
    for x in (0, 1, nx - 2, nx - 1):
        body(x, True)

    def step(x, carry):
        body(x, False)
        return carry

    lax.fori_loop(2, nx - 2, step, 0)


def velocity_body(nx, ny, first, s, v_in, b_in, *refs):
    tiles = s.shape[1]
    if first:
        m_in, v, bd, md, sem = refs
        copies = to_tiles(b_in, bd, sem.at[3])
        for c in range(3):
            copies += to_tiles(v_in.at[c], v.at[c], sem.at[c])
        late = to_tiles(m_in, md, sem.at[4])
        for c in copies + late:
            c.start()
        for c in copies:
            c.wait()
    else:
        (v,) = refs
    cf = Coefs(ny)

    def body(x, static):
        start = x * ny if static else pl.multiple_of(x * ny, 8)
        at = pl.ds(start, ny)
        xt = functools.partial(x_terms, s, x=x, nx=nx, ny=ny, static=static)
        sxy, sxz, syz = slab(s, SXY, at), slab(s, SXZ, at), slab(s, SYZ, at)
        a = (
            add(xt(SXX, pairs=PLUS), cf.y_minus(sxy), cf.z_minus(sxz)),
            add(xt(SXY, pairs=MINUS), cf.y_plus(slab(s, SYY, at)), cf.z_minus(syz)),
            add(xt(SXZ, pairs=MINUS), cf.y_minus(syz), cf.z_plus(slab(s, SZZ, at))),
        )
        src = v if first else v_in
        for k in range(tiles):
            if first:
                w = DT * bd[k, at, :]
                bd[k, at, :] = w
            else:
                w = b_in[k, at, :]
            for c in range(3):
                v[c, k, at, :] = src[c, k, at, :] + w * a[c][k]

    over_x(nx, body)
    if first:
        for c in late:
            c.wait()


def stress_slabs(nx, ny, v, s_in, s, m_in, md):
    tiles = s.shape[1]
    cf = Coefs(ny)

    def body(x, static):
        start = x * ny if static else pl.multiple_of(x * ny, 8)
        at = pl.ds(start, ny)
        xt = functools.partial(x_terms, v, x=x, nx=nx, ny=ny, static=static)
        vx, vy, vz = slab(v, 0, at), slab(v, 1, at), slab(v, 2, at)
        exx = xt(0, pairs=MINUS)
        eyy = cf.y_minus(vy)
        ezz = cf.z_minus(vz)
        exy = add(xt(1, pairs=PLUS), cf.y_plus(vx))
        exz = add(xt(2, pairs=PLUS), cf.z_plus(vx))
        eyz = add(cf.z_plus(vy), cf.y_plus(vz))
        tr = add(exx, eyy, ezz)
        for k in range(tiles):
            w = m_in[k, at, :]
            if md is not None:
                w = DT * w
                md[k, at, :] = w
            s[SXX, k, at, :] = s_in[SXX, k, at, :] + w * (tr[k] + 2.0 * exx[k])
            s[SYY, k, at, :] = s_in[SYY, k, at, :] + w * (tr[k] + 2.0 * eyy[k])
            s[SZZ, k, at, :] = s_in[SZZ, k, at, :] + w * (tr[k] + 2.0 * ezz[k])
            s[SXY, k, at, :] = s_in[SXY, k, at, :] + w * exy[k]
            s[SXZ, k, at, :] = s_in[SXZ, k, at, :] + w * exz[k]
            s[SYZ, k, at, :] = s_in[SYZ, k, at, :] + w * eyz[k]

    return body


def stress_body(nx, ny, first, v, s_in, m_in, s, *md):
    over_x(nx, stress_slabs(nx, ny, v, s_in, s, m_in, md[0] if first else None))


def last_begin_body(nx, ny, v, s_in, m, back_in, s, back):
    del s_in
    body = stress_slabs(nx, ny, v, s, s, m, None)
    for x in (0, 1, nx - 2, nx - 1):
        body(x, True)
    back[...] = back_in[...]


def last_slabs_body(nx, ny, begin, end, first, v, s_in, m, traction, *refs):
    del s_in
    out = []
    if first:
        yl, yh, minus, plus, s, s_out, v_out, sem = refs
        for c in range(3):
            out += from_tiles(v.at[c], v_out.at[c], sem.at[6 + c])
        for c in out:
            c.start()
        stress_y_terms(s, m, Edges(nx, ny), ny, yl, yh, minus, plus)
    else:
        _, s, s_out, sem = refs
    body = stress_slabs(nx, ny, v, s, s, m, None)
    on_minus, _ = fault_side()

    def step(x, carry):
        body(x, False)
        return carry

    width = -(-(end - begin) // 2)
    while begin < end:
        stop = min(begin + width, end)
        lax.fori_loop(begin, stop, step, 0)
        at = pl.ds(begin * ny + ny - 1, stop - begin, stride=ny)
        s[SXY, :, at, :] = jnp.where(on_minus, traction[:, begin:stop, :], s[SXY, :, at, :])
        span = pl.ds(begin * ny, (stop - begin) * ny)
        for c in range(6):
            for k in range(s.shape[1]):
                copy = pltpu.make_async_copy(
                    s.at[c, k, span], s_out.at[c, span, tile(k)], sem.at[c, k]
                )
                copy.start()
                out.append(copy)
        begin = stop
    for c in out:
        c.wait()


class Edges:
    def __init__(self, nx, ny):
        self.nx, self.ny = nx, ny

    def x(self, i):
        return pl.ds(i * self.ny, self.ny)

    def y(self, i):
        return pl.ds(i, self.nx, stride=self.ny)


def minus_edges(n, low, high):
    return (
        (0, -C1 * low[1] - C2 * low[0]),
        (1, -C2 * low[1]),
        (n - 1, C2 * high[0]),
    )


def plus_edges(n, low, high):
    return (
        (0, -C2 * low[0]),
        (n - 1, C1 * high[0] + C2 * high[1]),
        (n - 2, C2 * high[0]),
    )


def sides():
    out = []
    for axis in ("strike", "normal"):
        i = lax.axis_index(axis)
        last = lax.axis_size(axis) - 1
        out += [jnp.where(i > 0, 1.0, 0.0).astype(F32), jnp.where(i < last, 1.0, 0.0).astype(F32)]
    return out


def fault_side():
    position = lax.axis_index("normal")
    half = lax.axis_size("normal") // 2
    return position == half - 1, position == half


def stress_x_terms(s, w, e, nx, xl, xh):
    low, high = sides()[:2]
    a = [xl[k] * low for k in range(4)]
    b = [xh[k] * high for k in range(5)]
    for i, value in minus_edges(nx, a[0:2], b[0:1]):
        add_rows(s, SXX, w, e.x(i), 3.0, value)
        add_rows(s, SYY, w, e.x(i), 1.0, value)
        add_rows(s, SZZ, w, e.x(i), 1.0, value)
    for i, value in plus_edges(nx, a[2:3], b[1:3]):
        add_rows(s, SXY, w, e.x(i), 1.0, value)
    for i, value in plus_edges(nx, a[3:4], b[3:5]):
        add_rows(s, SXZ, w, e.x(i), 1.0, value)


def stress_y_terms(s, w, e, ny, yl, yh, minus, plus):
    low, high = sides()[2:]
    on_minus, on_plus = fault_side()
    a = [yl[k] * low for k in range(4)]
    b = [yh[k] * high for k in range(5)]
    a[2] = jnp.where(on_plus, minus[...], a[2])
    b[1] = jnp.where(on_minus, plus[...], b[1])
    for i, value in minus_edges(ny, a[0:2], b[0:1]):
        add_rows(s, SXX, w, e.y(i), 1.0, value)
        add_rows(s, SYY, w, e.y(i), 3.0, value)
        add_rows(s, SZZ, w, e.y(i), 1.0, value)
    for i, value in plus_edges(ny, a[2:3], b[1:3]):
        add_rows(s, SXY, w, e.y(i), 1.0, value)
    for i, value in plus_edges(ny, a[3:4], b[3:5]):
        add_rows(s, SYZ, w, e.y(i), 1.0, value)


def add_rows(ref, comp, w, at, factor, value):
    ref[comp, :, at, :] = ref[comp, :, at, :] + w[:, at, :] * (factor * value if factor != 1.0 else value)


def pack_stress_x(s, e, up, down):
    nx = e.nx
    for k, (c, i) in enumerate(
        ((SXX, nx - 1), (SXY, nx - 2), (SXY, nx - 1), (SXZ, nx - 2), (SXZ, nx - 1))
    ):
        up[k] = s[c, :, e.x(i), :]
    for k, (c, i) in enumerate(((SXX, 0), (SXX, 1), (SXY, 0), (SXZ, 0))):
        down[k] = s[c, :, e.x(i), :]


def pack_stress_y(s, e, up, down):
    ny = e.ny
    for k, (c, i) in enumerate(
        ((SYY, ny - 1), (SXY, ny - 2), (SXY, ny - 1), (SYZ, ny - 2), (SYZ, ny - 1))
    ):
        up[k] = s[c, :, e.y(i), :]
    for k, (c, i) in enumerate(((SYY, 0), (SYY, 1), (SXY, 0), (SYZ, 0))):
        down[k] = s[c, :, e.y(i), :]


def load_body(nx, ny, stress, s, xu, xd, yu, yd, sem):
    e = Edges(nx, ny)
    order = (SXX, SXY, SXZ, SYY, SYZ, SZZ)
    copies = {c: to_tiles(stress.at[c], s.at[c], sem.at[c]) for c in order}

    def wait(*comps):
        for c in comps:
            for copy in copies[c]:
                copy.wait()

    for c in order:
        for copy in copies[c]:
            copy.start()
    wait(SXX, SXY, SXZ)
    pack_stress_x(s, e, xu, xd)
    wait(SYY, SYZ)
    pack_stress_y(s, e, yu, yd)
    wait(SZZ)


def velocity_edges_body(nx, ny, v_in, w, s, xl, xh, yl, yh, v, mine, traction):
    del v_in
    e = Edges(nx, ny)
    fxl, fxh, fyl, fyh = sides()
    a = [xl[k] * fxl for k in range(5)]
    b = [xh[k] * fxh for k in range(4)]
    for comp, terms in (
        (0, plus_edges(nx, a[0:1], b[0:2])),
        (1, minus_edges(nx, a[1:3], b[2:3])),
        (2, minus_edges(nx, a[3:5], b[3:4])),
    ):
        for i, value in terms:
            add_rows(v, comp, w, e.x(i), 1.0, value)
    a = [yl[k] * fyl for k in range(5)]
    b = [yh[k] * fyh for k in range(4)]
    for comp, terms in (
        (1, plus_edges(ny, a[0:1], b[0:2])),
        (0, minus_edges(ny, a[1:3], b[2:3])),
        (2, minus_edges(ny, a[3:5], b[3:4])),
    ):
        for i, value in terms:
            add_rows(v, comp, w, e.y(i), 1.0, value)
    odd = lax.rem(lax.axis_index("normal"), 2) == 1
    mine[...] = jnp.where(odd, v[0, :, e.y(ny - 1), :], v[0, :, e.y(0), :])
    traction[...] = jnp.where(odd, s[SXY, :, e.y(ny - 1), :], yl[2])


def pack_velocity_y_body(nx, ny, v, yu, yd):
    e = Edges(nx, ny)
    for k, (c, i) in enumerate(((1, ny - 2), (1, ny - 1), (0, ny - 1), (2, ny - 1))):
        yu[k] = v[c, :, e.y(i), :]
    for k, (c, i) in enumerate(((1, 0), (0, 0), (0, 1), (2, 0), (2, 1))):
        yd[k] = v[c, :, e.y(i), :]


def inverse_sinh(values):
    magnitude = jnp.abs(values)
    root = jnp.sqrt(1.0 + magnitude * magnitude)
    result = jnp.log1p(magnitude + magnitude * magnitude / (1.0 + root))
    return jnp.where(values < 0.0, -result, result)


def fault_body(nx, ny, last, *refs):
    mine, other, traction, par, st_in, v_in, v, xu, xd, st, minus_o, plus_o, trac_o = refs[:13]
    del v_in
    e = Edges(nx, ny)
    position = lax.axis_index("normal")
    members = lax.axis_size("normal")
    odd = lax.rem(position, 2) == 1
    on_minus, on_plus = fault_side()
    m, o = mine[...], other[...]
    minus = jnp.where(odd, m, o)
    plus = jnp.where(odd, o, m)
    mask, a, b, inv_len, sigma = (par[k] for k in range(5))
    state = st_in[...]
    locked = traction[...] + ETA * (plus - minus)
    c = 0.5 * jnp.exp(state / a)
    weight = sigma * a
    rate = jnp.zeros_like(locked)
    for _ in range(NEWTON):
        arg = c * rate
        residue = locked - ETA * rate - weight * inverse_sinh(arg)
        slope = ETA + weight * c / jnp.sqrt(1.0 + arg * arg)
        rate = rate + residue / slope
    rate = rate * mask
    state = state + DT * inv_len * (jnp.exp(-state / b) - jnp.abs(rate))
    st[...] = state
    trac_o[...] = locked - ETA * rate
    middle = 0.5 * (minus + plus)
    minus = middle - 0.5 * rate
    plus = middle + 0.5 * rate
    minus_o[...] = minus
    plus_o[...] = plus
    v[0, :, e.y(ny - 1), :] = jnp.where(on_minus, minus, v[0, :, e.y(ny - 1), :])
    v[0, :, e.y(0), :] = jnp.where(on_plus, plus, v[0, :, e.y(0), :])
    for k, (comp, i) in enumerate(((0, nx - 2), (0, nx - 1), (1, nx - 1), (2, nx - 1))):
        xu[k] = v[comp, :, e.x(i), :]
    for k, (comp, i) in enumerate(((0, 0), (1, 0), (1, 1), (2, 0), (2, 1))):
        xd[k] = v[comp, :, e.x(i), :]
    if last:
        (back,) = refs[13:]
        half = nx // 2
        upper = position >= members // 2
        for q, value in enumerate((rate, state)):
            back[q] = jnp.where(upper, value[:, half:, :], value[:, :half, :])


def choose_body(holders, mine, got, out):
    out[...] = jnp.where(holds(holders), mine[...], got[...])


def holds(holders):
    position = lax.axis_index("normal")
    return functools.reduce(lambda p, q: p | q, [position == h for h in holders])


def stress_edges_body(nx, ny, s_in, w, xl, xh, yl, yh, minus, plus, traction, s, xu, xd, yu, yd):
    del s_in
    e = Edges(nx, ny)
    on_minus, _ = fault_side()
    stress_x_terms(s, w, e, nx, xl, xh)
    stress_y_terms(s, w, e, ny, yl, yh, minus, plus)
    s[SXY, :, e.y(ny - 1), :] = jnp.where(on_minus, traction[...], s[SXY, :, e.y(ny - 1), :])
    pack_stress_x(s, e, xu, xd)
    pack_stress_y(s, e, yu, yd)


def stress_last_body(
    nx, ny, rows, holders, s, w, xl, xh, traction, mine, got, o_in, out, slip, state, own, sem
):
    del o_in
    e = Edges(nx, ny)
    on_minus, _ = fault_side()
    stress_x_terms(s, w, e, nx, xl, xh)
    copies = []
    for x in (0, 1, nx - 2, nx - 1):
        at = pl.ds(x * ny + ny - 1, 1)
        s[SXY, :, at, :] = jnp.where(on_minus, traction[:, x : x + 1, :], s[SXY, :, at, :])
    for j, x in enumerate((0, nx - 2)):
        span = pl.ds(x * ny, 2 * ny)
        for c in range(6):
            for k in range(s.shape[1]):
                copies.append(
                    pltpu.make_async_copy(
                        s.at[c, k, span], out.at[c, span, tile(k)], sem.at[j * 6 + c, k]
                    )
                )
    for c in copies:
        c.start()
    half = lax.axis_size("normal") // 2
    at = pl.ds(rows * lax.rem(lax.axis_index("normal"), half), rows)
    have = holds(holders)
    for k in range(s.shape[1]):
        for q in range(2):
            own[q, :, tile(k)] = jnp.where(have, mine[q, k, at, :], got[q, k, at, :])
    for q, target in enumerate((slip, state)):
        copy = pltpu.make_async_copy(own.at[q], target, sem.at[12, q])
        copy.start()
        copies.append(copy)
    for c in copies:
        c.wait()


def own_body(state, mask, ids, out, st, mk, rg, sem):
    rows = state.shape[0]
    run(
        [
            pltpu.make_async_copy(a, b, sem.at[0, k])
            for k, (a, b) in enumerate(((state, st), (mask, mk), (ids, rg)))
        ]
    )
    out[0, 0:rows, :] = st[...]
    out[0, rows : 2 * rows, :] = mk[...].astype(F32)
    out[0, 2 * rows : 3 * rows, :] = rg[...].astype(F32)
    pad = out.shape[1] - 3 * rows
    if pad:
        out[0, 3 * rows :, :] = jnp.zeros((pad, out.shape[2]), F32)


def merge_body(bit, mine, got, out):
    upper = lax.rem(lax.axis_index("normal") // bit, 2) == 1
    n = mine.shape[0]
    a, b = mine[...], got[...]
    out[0:n] = jnp.where(upper, b, a)
    out[n : 2 * n] = jnp.where(upper, a, b)


def parameters_body(rows, mine, got, table, st, par, tmp):
    half = mine.shape[0]
    upper = lax.axis_index("normal") >= half
    for k in range(2 * half):
        at = slice(k * rows, (k + 1) * rows)
        a, b = (mine, got) if k < half else (got, mine)
        block = jnp.where(upper, b[k % half], a[k % half])
        for z in range(st.shape[0]):
            st[z, at, :] = block[0:rows, tile(z)]
            par[0, z, at, :] = block[rows : 2 * rows, tile(z)]
            tmp[z, at, :] = block[2 * rows : 3 * rows, tile(z)]
    ids = tmp[...]
    for j in range(4):
        p = jnp.zeros_like(ids)
        for r in range(table.shape[1]):
            p = jnp.where(ids == float(r), table[j, r], p)
        par[1 + j] = p


def local(velocity, stress, modulus, buoyancy, fault_state, fault_mask, region_ids, friction_table):
    members = lax.axis_size("normal")
    _, nx, ny, nz = velocity.shape
    rows = fault_state.shape[0]
    flat, nt = nx * ny, nz // LANES
    pin = lambda x: pltpu.with_memory_space_constraint(x, pltpu.HBM)
    vel_in = pin(velocity.reshape(3, flat, nz))
    str_in = pin(stress.reshape(6, flat, nz))
    mod_in = pin(modulus.reshape(flat, nz))
    buo_in = pin(buoyancy.reshape(flat, nz))
    fault_in = (pin(fault_state), pin(fault_mask), pin(region_ids))
    dma = lambda n: pltpu.SemaphoreType.DMA((n, nt))
    stage_cost = pl.CostEstimate(flops=4_000_000_000, bytes_accessed=16_000_000, transcendentals=0)
    part_cost = pl.CostEstimate(flops=2_000_000_000, bytes_accessed=8_000_000, transcendentals=0)
    side_cost = pl.CostEstimate(flops=1_000_000, bytes_accessed=1_000_000, transcendentals=0)

    depth = -(-3 * rows // 8) * 8
    (known,) = call(
        own_body, [HBM] * 3, [((1, depth, nz), VMEM)], fault_in,
        scratch=[pltpu.VMEM((rows, nz), F32)] + [pltpu.VMEM((rows, nz), jnp.int32)] * 2 + [dma(1)],
        cost=side_cost, name="own",
    )
    s, xu, xd, yu, yd = call(
        functools.partial(load_body, nx, ny), [HBM],
        [((6, nt, flat, LANES), VMEM), ((5, nt, ny, LANES), VMEM), ((4, nt, ny, LANES), VMEM),
         ((5, nt, nx, LANES), VMEM), ((4, nt, nx, LANES), VMEM)],
        (str_in,), scratch=[dma(6)], cost=side_cost, name="load",
    )
    tie = lax.optimization_barrier

    def merge(known, got, bit):
        return call(
            functools.partial(merge_body, bit), [VMEM] * 2, [((2 * bit, depth, nz), VMEM)],
            (known, got), cost=side_cost, name="merge",
        )[0]

    got = swap(known, 1)
    known, got, xu, xd, yu, yd = tie((known, got, xu, xd, yu, yd))
    known = merge(known, got, 1)
    known = merge(known, swap(known, 2), 2)
    bit = 4
    block_v = ((3, nt, flat, LANES), VMEM)
    block_s = ((6, nt, flat, LANES), VMEM)
    block_1 = ((nt, flat, LANES), VMEM)
    row_1 = ((nt, nx, LANES), VMEM)
    v = w = m = None
    for step in range(STEPS):
        first, last = step == 0, step == STEPS - 1
        xl, xh = shift_up(xu, "strike"), shift_down(xd, "strike")
        yl, yh = shift_up(yu, "normal"), shift_down(yd, "normal")
        if first:
            v, w, m = call(
                functools.partial(velocity_body, nx, ny, True), [VMEM, HBM, HBM, HBM],
                [block_v, block_1, block_1], (s, vel_in, buo_in, mod_in),
                scratch=[dma(5)], cost=stage_cost, name="velocity_first",
            )
            while 2 * bit < members:
                known = merge(known, swap(known, bit), bit)
                bit *= 2
            known, v = tie((known, v))
            state, par = call(
                functools.partial(parameters_body, rows), [VMEM, VMEM, SMEM],
                [((nt, nx, LANES), VMEM), ((5, nt, nx, LANES), VMEM)],
                (known, swap(known, bit), friction_table),
                scratch=[pltpu.VMEM((nt, nx, LANES), F32)], cost=side_cost, name="parameters",
            )
        else:
            (v,) = call(
                functools.partial(velocity_body, nx, ny, False), [VMEM] * 3, [block_v], (s, v, w),
                aliases={1: 0}, cost=stage_cost, name="velocity",
            )
        v, mine, traction = call(
            functools.partial(velocity_edges_body, nx, ny), [VMEM] * 7, [block_v, row_1, row_1],
            (v, w, s, xl, xh, yl, yh), aliases={0: 0}, cost=side_cost, name="velocity_edges",
        )
        other = swap_odd(mine, "normal")
        yu, yd = call(
            functools.partial(pack_velocity_y_body, nx, ny), [VMEM],
            [((4, nt, nx, LANES), VMEM), ((5, nt, nx, LANES), VMEM)], (v,), cost=side_cost,
            name="pack_normal",
        )
        if not last:
            yl, yh = shift_up(yu, "normal"), shift_down(yd, "normal")
        outs = [block_v, ((4, nt, ny, LANES), VMEM), ((5, nt, ny, LANES), VMEM)] + [row_1] * 4
        if last:
            outs.append(((2, nt, nx // 2, LANES), VMEM))
        got = call(
            functools.partial(fault_body, nx, ny, last), [VMEM] * 6, outs,
            (mine, other, traction, par, state, v), aliases={5: 0}, cost=side_cost, name="fault",
        )
        v, xu, xd, state, minus, plus, trac_new = got[:7]
        if last:
            xu, xd, yu, yd = tie((xu, xd, yu, yd))
            yl, yh = shift_up(yu, "normal"), shift_down(yd, "normal")
        xl, xh = shift_up(xu, "strike"), shift_down(xd, "strike")
        body = functools.partial(stress_body, nx, ny, first)
        if last:
            half_rows = ((2, nt, nx // 2, LANES), VMEM)
            back, holders = got[7], [members // 2 - 1, members // 2]
            s, back = call(
                functools.partial(last_begin_body, nx, ny), [VMEM] * 4, [block_s, half_rows],
                (v, s, m, back), aliases={1: 0}, cost=side_cost,
                name="last_begin",
            )
            edges, bits = [2], []
            bit = members // 4
            while bit >= 1:
                bits.append(bit)
                bit //= 2
            parts = max(len(bits) - 1, 1)
            for j in range(parts):
                edges.append(2 + (nx - 4) * (j + 1) // parts)
            s_out = v_out = None
            for j, bit in enumerate(bits):
                came = swap(back, bit)
                if j < parts:
                    outs = [block_s, ((6, flat, nz), HBM)]
                    ins = [VMEM] * 4
                    args = [v, s, m, trac_new]
                    aliases = {1: 0}
                    if j == 0:
                        ins, args = ins + [VMEM] * 4, args + [yl, yh, minus, plus]
                        outs.append(((3, flat, nz), HBM))
                    else:
                        ins, args = ins + [HBM], args + [s_out]
                        aliases[4] = 1
                    parts_out = call(
                        functools.partial(
                            last_slabs_body, nx, ny, edges[j], edges[j + 1], j == 0
                        ),
                        ins, outs, args, scratch=[dma(9)], aliases=aliases, cost=part_cost,
                        name=f"last_slabs_{j}",
                    )
                    s, s_out = parts_out[:2]
                    if j == 0:
                        v_out = parts_out[2]
                if j < len(bits) - 1:
                    came, s = tie((came, s))
                    (back,) = call(
                        functools.partial(choose_body, tuple(holders)), [VMEM] * 2, [half_rows],
                        (back, came), cost=side_cost, name="choose",
                    )
                    holders += [h ^ bit for h in holders]
            s_out, slip, state_out = call(
                functools.partial(stress_last_body, nx, ny, rows, tuple(holders)),
                [VMEM] * 7 + [HBM],
                [((6, flat, nz), HBM), ((rows, nz), HBM), ((rows, nz), HBM)],
                (s, m, xl, xh, trac_new, back, came, s_out),
                scratch=[pltpu.VMEM((2, rows, nz), F32), dma(13)],
                aliases={7: 0}, cost=side_cost, name="edges_last",
            )
            continue
        if first:
            s, m = call(
                body, [VMEM] * 3, [block_s, block_1], (v, s, m), aliases={1: 0, 2: 1},
                cost=stage_cost, name="stress_first",
            )
        else:
            (s,) = call(
                body, [VMEM] * 3, [block_s], (v, s, m), aliases={1: 0}, cost=stage_cost,
                name="stress",
            )
        s, xu, xd, yu, yd = call(
            functools.partial(stress_edges_body, nx, ny), [VMEM] * 9,
            [block_s, ((5, nt, ny, LANES), VMEM), ((4, nt, ny, LANES), VMEM),
             ((5, nt, nx, LANES), VMEM), ((4, nt, nx, LANES), VMEM)],
            (s, m, xl, xh, yl, yh, minus, plus, trac_new), aliases={0: 0}, cost=side_cost,
            name="stress_edges",
        )
    return (
        v_out.reshape(3, nx, ny, nz),
        s_out.reshape(6, nx, ny, nz),
        slip,
        state_out,
    )


def solution(mesh):
    block = P(None, "strike", "normal", None)
    part = P("strike", "normal", None)
    row = P(("strike", "normal"), None)
    return jax.shard_map(
        local,
        mesh=mesh,
        in_specs=(block, block, part, part, row, row, row, P()),
        out_specs=(block, block, row, row),
        check_vma=False,
    )
```

```python
import functools

import jax
import jax.numpy as jnp
from jax import lax
from jax.experimental import pallas as pl
from jax.experimental.pallas import tpu as pltpu
from jax.sharding import PartitionSpec as P

STEPS = 2
NEWTON = 4

C2 = -1.0 / 24.0
RATIO = (9.0 / 8.0) / C2
DT = 0.1
STEP = DT * C2
ETA = 1.0

F32 = jnp.float32
SXX, SYY, SZZ, SXY, SXZ, SYZ = range(6)


def shift_up(x, axis):
    count = lax.axis_size(axis)
    return lax.ppermute(x, axis, [(i, (i + 1) % count) for i in range(count)])


def shift_down(x, axis):
    count = lax.axis_size(axis)
    return lax.ppermute(x, axis, [((i + 1) % count, i) for i in range(count)])


def swap_odd(x, axis):
    count = lax.axis_size(axis)
    pairs = []
    for i in range(1, count, 2):
        j = (i + 1) % count
        pairs += [(i, j), (j, i)]
    return lax.ppermute(x, axis, pairs)


def swap(x, bit):
    count = lax.axis_size("normal")
    return lax.ppermute(x, "normal", [(i, i ^ bit) for i in range(count)])


VMEM = pl.BlockSpec(memory_space=pltpu.VMEM)
SMEM = pl.BlockSpec(memory_space=pltpu.SMEM)
HBM = pl.BlockSpec(memory_space=pltpu.HBM)


def call(body, ins, outs, args, scratch=(), aliases=None, cost=None, name=None):
    shapes = [
        pltpu.VMEM(shape, F32) if spec is VMEM else jax.ShapeDtypeStruct(shape, F32)
        for shape, spec in outs
    ]
    return pl.pallas_call(
        body,
        out_shape=shapes,
        in_specs=ins,
        out_specs=[spec for _, spec in outs],
        scratch_shapes=list(scratch),
        input_output_aliases=aliases or {},
        compiler_params=pltpu.CompilerParams(vmem_limit_bytes=16 << 20),
        cost_estimate=cost,
        name=name,
    )(*args)


SUB, LANES = 8, 128


class Shifts:
    def __init__(self, ny):
        self.count = ny // SUB
        self.row = lax.broadcasted_iota(jnp.int32, (SUB, LANES), 0)
        self.lane = lax.broadcasted_iota(jnp.int32, (SUB, LANES), 1)

    def rows(self, here, ref, comp, slab, offset):
        edge = offset > 0
        keep = self.row < SUB - offset if edge else self.row >= -offset
        outer = self.count - 1 if edge else 0
        if here.static:
            turned = [[pltpu.roll(f, (-offset) % SUB, 0) for f in fs] for fs in slab]
            out = []
            for fs in turned:
                line = []
                for h, f in enumerate(fs):
                    j = h + 1 if edge else h - 1
                    line.append(jnp.where(keep, f, 0.0 if h == outer else fs[j]))
                out.append(line)
            return out
        return [
            [jnp.where(keep, f, 0.0) if h == outer else f for h, f in enumerate(fs)]
            for fs in here.load(ref, comp, 0, offset)
        ]

    def y_minus(self, here, ref, comp, slab):
        near = [self.rows(here, ref, comp, slab, o) for o in (-1, 1, -2)]
        return each(lambda f, b, c, d: RATIO * (f - b) + (c - d), slab, *near)

    def y_plus(self, here, ref, comp, slab):
        near = [self.rows(here, ref, comp, slab, o) for o in (1, 2, -1)]
        return each(lambda f, b, c, d: RATIO * (b - f) + (c - d), slab, *near)

    def lines(self, f, slab):
        columns = [f([fs[h] for fs in slab]) for h in range(self.count)]
        return [[column[k] for column in columns] for k in range(len(slab))]

    def z_minus(self, slab):
        def line(fs):
            n, lane = len(fs), self.lane
            r = [pltpu.roll(f, LANES - 1, 1) for f in fs]
            p = [jnp.where(lane < LANES - 1, r[k], r[k + 1] if k + 1 < n else 0.0) for k in range(n)]
            w = [RATIO * p[k] + fs[k] for k in range(n)]
            end = jnp.where(lane == LANES - 1, RATIO * r[0], 0.0)
            w[-1] = jnp.where(lane < LANES - 2, w[-1], end)
            q = [pltpu.roll(x, 2, 1) for x in w]
            return [RATIO * fs[k] + p[k] - jnp.where(lane >= 2, q[k], q[k - 1]) for k in range(n)]

        return self.lines(line, slab)

    def z_plus(self, slab):
        def line(fs):
            n, lane = len(fs), self.lane
            r = [pltpu.roll(f, 1, 1) for f in fs]
            m = [jnp.where(lane >= 1, r[k], r[k - 1] if k else 0.0) for k in range(n)]
            w = [RATIO * m[k] + fs[k] for k in range(n)]
            w[0] = jnp.where(lane >= 2, w[0], jnp.where(lane == 0, RATIO * r[-1], 0.0))
            q = [pltpu.roll(x, LANES - 2, 1) for x in w]
            return [
                jnp.where(lane < LANES - 2, q[k], q[(k + 1) % n]) - (RATIO * fs[k] + m[k])
                for k in range(n)
            ]

        return self.lines(line, slab)


def each(f, *slabs):
    return [[f(*pieces) for pieces in zip(*lines)] for lines in zip(*slabs)]


def add(*slabs):
    return each(lambda *parts: functools.reduce(lambda p, q: p + q, parts), *slabs)


def tile(k):
    return slice(k * LANES, (k + 1) * LANES)


def to_tiles(source, target, sems):
    return [
        pltpu.make_async_copy(source.at[:, tile(k)], target.at[k], sems.at[k])
        for k in range(target.shape[0])
    ]


def from_tiles(source, target, sems):
    return [
        pltpu.make_async_copy(source.at[k], target.at[:, tile(k)], sems.at[k])
        for k in range(source.shape[0])
    ]


def run(copies):
    for c in copies:
        c.start()
    for c in copies:
        c.wait()


class Slabs:
    def __init__(self, x, nx, ny, static):
        self.x, self.nx, self.ny, self.static = x, nx, ny, static

    def at(self, h, offset=0, row=0):
        start = (self.x + offset) * self.ny + h * SUB
        if not self.static:
            start = pl.multiple_of(start, SUB)
        return pl.ds(start + row, SUB)

    def load(self, ref, comp, offset=0, row=0):
        return [
            [ref[comp, k, self.at(h, offset, row), :] for h in range(self.ny // SUB)]
            for k in range(ref.shape[1])
        ]

    def near(self, ref, comp, offset):
        if self.static and not 0 <= self.x + offset < self.nx:
            return None
        return self.load(ref, comp, offset)

    def difference(self, ref, comp, a, b, c, d):
        total = None
        for p, q, factor in ((a, b, RATIO), (c, d, None)):
            p, q = self.near(ref, comp, p), self.near(ref, comp, q)
            if p is None and q is None:
                continue
            if p is None:
                term = each(lambda f: -f, q)
            else:
                term = p if q is None else each(lambda f, g: f - g, p, q)
            if factor is not None:
                term = each(lambda f: factor * f, term)
            total = term if total is None else add(total, term)
        return total

    def minus(self, ref, comp):
        return self.difference(ref, comp, 0, -1, 1, -2)

    def plus(self, ref, comp):
        return self.difference(ref, comp, 1, 0, 2, -1)


def run_slabs(begin, end, body):
    def step(i, carry):
        body(begin + 2 * i, False)
        body(begin + 2 * i + 1, False)
        return carry

    lax.fori_loop(0, (end - begin) // 2, step, 0)
    if (end - begin) % 2:
        body(end - 1, True)


def over_x(nx, body, parts=1, before=None):
    for j in range(parts):
        begin, end = nx * j // parts, nx * (j + 1) // parts
        if before is not None:
            before(j)
        first, last = max(begin, 2), min(end, nx - 2)
        for x in range(begin, first):
            body(x, True)
        run_slabs(first, last, body)
        for x in range(last, end):
            body(x, True)


LOADS = 4


def velocity_body(nx, ny, first, s, v_in, b_in, *refs):
    tiles = s.shape[1]
    before = None
    if first:
        m_in, v, bd, md, sem = refs
        loads = []
        for j in range(LOADS):
            at = pl.ds(nx * j // LOADS * ny, nx // LOADS * ny)
            pairs = [(b_in, bd)] + [(v_in.at[c], v.at[c]) for c in range(3)]
            loads.append(
                [
                    pltpu.make_async_copy(p.at[at, tile(k)], q.at[k, at], sem.at[4 * j + i, k])
                    for i, (p, q) in enumerate(pairs)
                    for k in range(tiles)
                ]
            )
        late = to_tiles(m_in, md, sem.at[4 * LOADS])
        for c in sum(loads, []) + late:
            c.start()

        def before(j):
            for c in loads[j]:
                c.wait()

    else:
        (v,) = refs
    sh = Shifts(ny)

    def body(x, static):
        here = Slabs(x, nx, ny, static)
        sxy, sxz, syz = here.load(s, SXY), here.load(s, SXZ), here.load(s, SYZ)
        syy = here.load(s, SYY)
        a = (
            add(here.plus(s, SXX), sh.y_minus(here, s, SXY, sxy), sh.z_minus(sxz)),
            add(here.minus(s, SXY), sh.y_plus(here, s, SYY, syy), sh.z_minus(syz)),
            add(here.minus(s, SXZ), sh.y_minus(here, s, SYZ, syz), sh.z_plus(here.load(s, SZZ))),
        )
        for k in range(tiles):
            for h in range(ny // SUB):
                at = here.at(h)
                if first:
                    w = STEP * bd[k, at, :]
                    bd[k, at, :] = w
                else:
                    w = b_in[k, at, :]
                for c in range(3):
                    v[c, k, at, :] = v[c, k, at, :] + w * a[c][k][h]

    over_x(nx, body, LOADS if first else 1, before)
    if first:
        for c in late:
            c.wait()


def stress_slabs(nx, ny, v, s, m_in, md):
    sh = Shifts(ny)

    def body(x, static):
        here = Slabs(x, nx, ny, static)
        vx, vy, vz = here.load(v, 0), here.load(v, 1), here.load(v, 2)
        exx, eyy, ezz = here.minus(v, 0), sh.y_minus(here, v, 1, vy), sh.z_minus(vz)
        exy = add(here.plus(v, 1), sh.y_plus(here, v, 0, vx))
        exz = add(here.plus(v, 2), sh.z_plus(vx))
        eyz = add(sh.z_plus(vy), sh.y_plus(here, v, 2, vz))
        tr = add(exx, eyy, ezz)
        for k in range(s.shape[1]):
            for h in range(ny // SUB):
                at = here.at(h)
                w = m_in[k, at, :]
                if md is not None:
                    w = STEP * w
                    md[k, at, :] = w
                for c, e in ((SXX, exx), (SYY, eyy), (SZZ, ezz)):
                    s[c, k, at, :] = s[c, k, at, :] + w * (tr[k][h] + 2.0 * e[k][h])
                for c, e in ((SXY, exy), (SXZ, exz), (SYZ, eyz)):
                    s[c, k, at, :] = s[c, k, at, :] + w * e[k][h]

    return body


def stress_body(nx, ny, first, v, s_in, m_in, s, *md):
    del s_in
    over_x(nx, stress_slabs(nx, ny, v, s, m_in, md[0] if first else None))


def last_begin_body(nx, ny, v, s_in, m, back_in, s, back):
    del s_in
    body = stress_slabs(nx, ny, v, s, m, None)
    for x in (0, 1, nx - 2, nx - 1):
        body(x, True)
    back[...] = back_in[...]


def last_slabs_body(nx, ny, begin, end, first, v, s_in, m, traction, *refs):
    del s_in
    out = []
    if first:
        yl, yh, minus, plus, s, s_out, v_out, sem = refs
        for c in range(3):
            out += from_tiles(v.at[c], v_out.at[c], sem.at[6 + c])
        for c in out:
            c.start()
        stress_y_terms(s, m, Edges(nx, ny), ny, yl, yh, minus, plus)
    else:
        _, s, s_out, sem = refs
    body = stress_slabs(nx, ny, v, s, m, None)
    on_minus, _ = fault_side()

    width = -(-(end - begin) // 4) * 2
    while begin < end:
        stop = min(begin + width, end)
        run_slabs(begin, stop, body)
        at = pl.ds(begin * ny + ny - 1, stop - begin, stride=ny)
        s[SXY, :, at, :] = jnp.where(on_minus, traction[:, begin:stop, :], s[SXY, :, at, :])
        span = pl.ds(begin * ny, (stop - begin) * ny)
        for c in range(6):
            for k in range(s.shape[1]):
                copy = pltpu.make_async_copy(
                    s.at[c, k, span], s_out.at[c, span, tile(k)], sem.at[c, k]
                )
                copy.start()
                out.append(copy)
        begin = stop
    for c in out:
        c.wait()


class Edges:
    def __init__(self, nx, ny):
        self.nx, self.ny = nx, ny

    def x(self, i):
        return pl.ds(i * self.ny, self.ny)

    def y(self, i):
        return pl.ds(i, self.nx, stride=self.ny)


def minus_edges(n, low, high):
    return (
        (0, -RATIO * low[1] - low[0]),
        (1, -low[1]),
        (n - 1, high[0]),
    )


def plus_edges(n, low, high):
    return (
        (0, -low[0]),
        (n - 1, RATIO * high[0] + high[1]),
        (n - 2, high[0]),
    )


def sides():
    out = []
    for axis in ("strike", "normal"):
        i = lax.axis_index(axis)
        last = lax.axis_size(axis) - 1
        out += [jnp.where(i > 0, 1.0, 0.0).astype(F32), jnp.where(i < last, 1.0, 0.0).astype(F32)]
    return out


def fault_side():
    position = lax.axis_index("normal")
    half = lax.axis_size("normal") // 2
    return position == half - 1, position == half


def stress_x_terms(s, w, e, nx, xl, xh):
    low, high = sides()[:2]
    a = [xl[k] * low for k in range(4)]
    b = [xh[k] * high for k in range(5)]
    for i, value in minus_edges(nx, a[0:2], b[0:1]):
        add_rows(s, SXX, w, e.x(i), 3.0, value)
        add_rows(s, SYY, w, e.x(i), 1.0, value)
        add_rows(s, SZZ, w, e.x(i), 1.0, value)
    for i, value in plus_edges(nx, a[2:3], b[1:3]):
        add_rows(s, SXY, w, e.x(i), 1.0, value)
    for i, value in plus_edges(nx, a[3:4], b[3:5]):
        add_rows(s, SXZ, w, e.x(i), 1.0, value)


def stress_y_terms(s, w, e, ny, yl, yh, minus, plus):
    low, high = sides()[2:]
    on_minus, on_plus = fault_side()
    a = [yl[k] * low for k in range(4)]
    b = [yh[k] * high for k in range(5)]
    a[2] = jnp.where(on_plus, minus[...], a[2])
    b[1] = jnp.where(on_minus, plus[...], b[1])
    for i, value in minus_edges(ny, a[0:2], b[0:1]):
        add_rows(s, SXX, w, e.y(i), 1.0, value)
        add_rows(s, SYY, w, e.y(i), 3.0, value)
        add_rows(s, SZZ, w, e.y(i), 1.0, value)
    for i, value in plus_edges(ny, a[2:3], b[1:3]):
        add_rows(s, SXY, w, e.y(i), 1.0, value)
    for i, value in plus_edges(ny, a[3:4], b[3:5]):
        add_rows(s, SYZ, w, e.y(i), 1.0, value)


def add_rows(ref, comp, w, at, factor, value):
    ref[comp, :, at, :] = ref[comp, :, at, :] + w[:, at, :] * (factor * value if factor != 1.0 else value)


def pack_stress_x(s, e, up, down):
    nx = e.nx
    for k, (c, i) in enumerate(
        ((SXX, nx - 1), (SXY, nx - 2), (SXY, nx - 1), (SXZ, nx - 2), (SXZ, nx - 1))
    ):
        up[k] = s[c, :, e.x(i), :]
    for k, (c, i) in enumerate(((SXX, 0), (SXX, 1), (SXY, 0), (SXZ, 0))):
        down[k] = s[c, :, e.x(i), :]


def pack_stress_y(s, e, up, down):
    ny = e.ny
    for k, (c, i) in enumerate(
        ((SYY, ny - 1), (SXY, ny - 2), (SXY, ny - 1), (SYZ, ny - 2), (SYZ, ny - 1))
    ):
        up[k] = s[c, :, e.y(i), :]
    for k, (c, i) in enumerate(((SYY, 0), (SYY, 1), (SXY, 0), (SYZ, 0))):
        down[k] = s[c, :, e.y(i), :]


def load_body(nx, ny, stress, s, xu, xd, yu, yd, sem):
    e = Edges(nx, ny)
    order = (SXX, SXY, SXZ, SYY, SYZ, SZZ)
    copies = {c: to_tiles(stress.at[c], s.at[c], sem.at[c]) for c in order}

    def wait(*comps):
        for c in comps:
            for copy in copies[c]:
                copy.wait()

    for c in order:
        for copy in copies[c]:
            copy.start()
    wait(SXX, SXY, SXZ)
    pack_stress_x(s, e, xu, xd)
    wait(SYY, SYZ)
    pack_stress_y(s, e, yu, yd)
    wait(SZZ)


def velocity_edges_body(nx, ny, v_in, w, s, xl, xh, yl, yh, v, mine, traction):
    del v_in
    e = Edges(nx, ny)
    fxl, fxh, fyl, fyh = sides()
    a = [xl[k] * fxl for k in range(5)]
    b = [xh[k] * fxh for k in range(4)]
    for comp, terms in (
        (0, plus_edges(nx, a[0:1], b[0:2])),
        (1, minus_edges(nx, a[1:3], b[2:3])),
        (2, minus_edges(nx, a[3:5], b[3:4])),
    ):
        for i, value in terms:
            add_rows(v, comp, w, e.x(i), 1.0, value)
    a = [yl[k] * fyl for k in range(5)]
    b = [yh[k] * fyh for k in range(4)]
    for comp, terms in (
        (1, plus_edges(ny, a[0:1], b[0:2])),
        (0, minus_edges(ny, a[1:3], b[2:3])),
        (2, minus_edges(ny, a[3:5], b[3:4])),
    ):
        for i, value in terms:
            add_rows(v, comp, w, e.y(i), 1.0, value)
    odd = lax.rem(lax.axis_index("normal"), 2) == 1
    mine[...] = jnp.where(odd, v[0, :, e.y(ny - 1), :], v[0, :, e.y(0), :])
    traction[...] = jnp.where(odd, s[SXY, :, e.y(ny - 1), :], yl[2])


def pack_velocity_y_body(nx, ny, v, yu, yd):
    e = Edges(nx, ny)
    for k, (c, i) in enumerate(((1, ny - 2), (1, ny - 1), (0, ny - 1), (2, ny - 1))):
        yu[k] = v[c, :, e.y(i), :]
    for k, (c, i) in enumerate(((1, 0), (0, 0), (0, 1), (2, 0), (2, 1))):
        yd[k] = v[c, :, e.y(i), :]


def inverse_sinh(values):
    magnitude = jnp.abs(values)
    root = jnp.sqrt(1.0 + magnitude * magnitude)
    result = jnp.log1p(magnitude + magnitude * magnitude / (1.0 + root))
    return jnp.where(values < 0.0, -result, result)


def fault_body(nx, ny, last, *refs):
    mine, other, traction, par, st_in, v_in, v, xu, xd, st, minus_o, plus_o, trac_o = refs[:13]
    del v_in
    e = Edges(nx, ny)
    position = lax.axis_index("normal")
    members = lax.axis_size("normal")
    odd = lax.rem(position, 2) == 1
    on_minus, on_plus = fault_side()
    m, o = mine[...], other[...]
    minus = jnp.where(odd, m, o)
    plus = jnp.where(odd, o, m)
    mask, a, b, inv_len, sigma = (par[k] for k in range(5))
    state = st_in[...]
    locked = traction[...] + ETA * (plus - minus)
    c = 0.5 * jnp.exp(state / a)
    weight = sigma * a
    rate = jnp.zeros_like(locked)
    for _ in range(NEWTON):
        arg = c * rate
        residue = locked - ETA * rate - weight * inverse_sinh(arg)
        slope = ETA + weight * c / jnp.sqrt(1.0 + arg * arg)
        rate = rate + residue / slope
    rate = rate * mask
    state = state + DT * inv_len * (jnp.exp(-state / b) - jnp.abs(rate))
    st[...] = state
    trac_o[...] = locked - ETA * rate
    middle = 0.5 * (minus + plus)
    minus = middle - 0.5 * rate
    plus = middle + 0.5 * rate
    minus_o[...] = minus
    plus_o[...] = plus
    v[0, :, e.y(ny - 1), :] = jnp.where(on_minus, minus, v[0, :, e.y(ny - 1), :])
    v[0, :, e.y(0), :] = jnp.where(on_plus, plus, v[0, :, e.y(0), :])
    for k, (comp, i) in enumerate(((0, nx - 2), (0, nx - 1), (1, nx - 1), (2, nx - 1))):
        xu[k] = v[comp, :, e.x(i), :]
    for k, (comp, i) in enumerate(((0, 0), (1, 0), (1, 1), (2, 0), (2, 1))):
        xd[k] = v[comp, :, e.x(i), :]
    if last:
        (back,) = refs[13:]
        half = nx // 2
        upper = position >= members // 2
        for q, value in enumerate((rate, state)):
            back[q] = jnp.where(upper, value[:, half:, :], value[:, :half, :])


def choose_body(holders, mine, got, out):
    out[...] = jnp.where(holds(holders), mine[...], got[...])


def holds(holders):
    position = lax.axis_index("normal")
    return functools.reduce(lambda p, q: p | q, [position == h for h in holders])


def stress_edges_body(nx, ny, s_in, w, xl, xh, yl, yh, minus, plus, traction, s, xu, xd, yu, yd):
    del s_in
    e = Edges(nx, ny)
    on_minus, _ = fault_side()
    stress_x_terms(s, w, e, nx, xl, xh)
    stress_y_terms(s, w, e, ny, yl, yh, minus, plus)
    s[SXY, :, e.y(ny - 1), :] = jnp.where(on_minus, traction[...], s[SXY, :, e.y(ny - 1), :])
    pack_stress_x(s, e, xu, xd)
    pack_stress_y(s, e, yu, yd)


def stress_last_body(
    nx, ny, rows, holders, s, w, xl, xh, traction, mine, got, o_in, out, slip, state, own, sem
):
    del o_in
    e = Edges(nx, ny)
    on_minus, _ = fault_side()
    stress_x_terms(s, w, e, nx, xl, xh)
    copies = []
    for x in (0, 1, nx - 2, nx - 1):
        at = pl.ds(x * ny + ny - 1, 1)
        s[SXY, :, at, :] = jnp.where(on_minus, traction[:, x : x + 1, :], s[SXY, :, at, :])
    for j, x in enumerate((0, nx - 2)):
        span = pl.ds(x * ny, 2 * ny)
        for c in range(6):
            for k in range(s.shape[1]):
                copies.append(
                    pltpu.make_async_copy(
                        s.at[c, k, span], out.at[c, span, tile(k)], sem.at[j * 6 + c, k]
                    )
                )
    for c in copies:
        c.start()
    half = lax.axis_size("normal") // 2
    at = pl.ds(rows * lax.rem(lax.axis_index("normal"), half), rows)
    have = holds(holders)
    for k in range(s.shape[1]):
        for q in range(2):
            own[q, :, tile(k)] = jnp.where(have, mine[q, k, at, :], got[q, k, at, :])
    for q, target in enumerate((slip, state)):
        copy = pltpu.make_async_copy(own.at[q], target, sem.at[12, q])
        copy.start()
        copies.append(copy)
    for c in copies:
        c.wait()


def own_body(state, mask, ids, out, st, mk, rg, sem):
    rows = state.shape[0]
    run(
        [
            pltpu.make_async_copy(a, b, sem.at[0, k])
            for k, (a, b) in enumerate(((state, st), (mask, mk), (ids, rg)))
        ]
    )
    out[0, 0:rows, :] = st[...]
    out[0, rows : 2 * rows, :] = mk[...].astype(F32)
    out[0, 2 * rows : 3 * rows, :] = rg[...].astype(F32)
    pad = out.shape[1] - 3 * rows
    if pad:
        out[0, 3 * rows :, :] = jnp.zeros((pad, out.shape[2]), F32)


def merge_body(bit, mine, got, out):
    upper = lax.rem(lax.axis_index("normal") // bit, 2) == 1
    n = mine.shape[0]
    a, b = mine[...], got[...]
    out[0:n] = jnp.where(upper, b, a)
    out[n : 2 * n] = jnp.where(upper, a, b)


def parameters_body(rows, mine, got, table, st, par, tmp):
    half = mine.shape[0]
    upper = lax.axis_index("normal") >= half
    for k in range(2 * half):
        at = slice(k * rows, (k + 1) * rows)
        a, b = (mine, got) if k < half else (got, mine)
        block = jnp.where(upper, b[k % half], a[k % half])
        for z in range(st.shape[0]):
            st[z, at, :] = block[0:rows, tile(z)]
            par[0, z, at, :] = block[rows : 2 * rows, tile(z)]
            tmp[z, at, :] = block[2 * rows : 3 * rows, tile(z)]
    ids = tmp[...]
    for j in range(4):
        p = jnp.zeros_like(ids)
        for r in range(table.shape[1]):
            p = jnp.where(ids == float(r), table[j, r], p)
        par[1 + j] = p


def local(velocity, stress, modulus, buoyancy, fault_state, fault_mask, region_ids, friction_table):
    members = lax.axis_size("normal")
    _, nx, ny, nz = velocity.shape
    rows = fault_state.shape[0]
    flat, nt = nx * ny, nz // LANES
    pin = lambda x: pltpu.with_memory_space_constraint(x, pltpu.HBM)
    vel_in = pin(velocity.reshape(3, flat, nz))
    str_in = pin(stress.reshape(6, flat, nz))
    mod_in = pin(modulus.reshape(flat, nz))
    buo_in = pin(buoyancy.reshape(flat, nz))
    fault_in = (pin(fault_state), pin(fault_mask), pin(region_ids))
    dma = lambda n: pltpu.SemaphoreType.DMA((n, nt))
    stage_cost = pl.CostEstimate(flops=4_000_000_000, bytes_accessed=16_000_000, transcendentals=0)
    part_cost = pl.CostEstimate(flops=2_000_000_000, bytes_accessed=8_000_000, transcendentals=0)
    side_cost = pl.CostEstimate(flops=1_000_000, bytes_accessed=1_000_000, transcendentals=0)

    depth = -(-3 * rows // 8) * 8
    (known,) = call(
        own_body, [HBM] * 3, [((1, depth, nz), VMEM)], fault_in,
        scratch=[pltpu.VMEM((rows, nz), F32)] + [pltpu.VMEM((rows, nz), jnp.int32)] * 2 + [dma(1)],
        cost=side_cost, name="own",
    )
    s, xu, xd, yu, yd = call(
        functools.partial(load_body, nx, ny), [HBM],
        [((6, nt, flat, LANES), VMEM), ((5, nt, ny, LANES), VMEM), ((4, nt, ny, LANES), VMEM),
         ((5, nt, nx, LANES), VMEM), ((4, nt, nx, LANES), VMEM)],
        (str_in,), scratch=[dma(6)], cost=side_cost, name="load",
    )
    tie = lax.optimization_barrier

    def merge(known, got, bit):
        return call(
            functools.partial(merge_body, bit), [VMEM] * 2, [((2 * bit, depth, nz), VMEM)],
            (known, got), cost=side_cost, name="merge",
        )[0]

    got = swap(known, 1)
    known, got, xu, xd, yu, yd = tie((known, got, xu, xd, yu, yd))
    known = merge(known, got, 1)
    known = merge(known, swap(known, 2), 2)
    bit = 4
    block_v = ((3, nt, flat, LANES), VMEM)
    block_s = ((6, nt, flat, LANES), VMEM)
    block_1 = ((nt, flat, LANES), VMEM)
    row_1 = ((nt, nx, LANES), VMEM)
    v = w = m = None
    for step in range(STEPS):
        first, last = step == 0, step == STEPS - 1
        xl, xh = shift_up(xu, "strike"), shift_down(xd, "strike")
        yl, yh = shift_up(yu, "normal"), shift_down(yd, "normal")
        if first:
            v, w, m = call(
                functools.partial(velocity_body, nx, ny, True), [VMEM, HBM, HBM, HBM],
                [block_v, block_1, block_1], (s, vel_in, buo_in, mod_in),
                scratch=[dma(4 * LOADS + 1)], cost=stage_cost, name="velocity_first",
            )
            while 2 * bit < members:
                known = merge(known, swap(known, bit), bit)
                bit *= 2
            known, v = tie((known, v))
            state, par = call(
                functools.partial(parameters_body, rows), [VMEM, VMEM, SMEM],
                [((nt, nx, LANES), VMEM), ((5, nt, nx, LANES), VMEM)],
                (known, swap(known, bit), friction_table),
                scratch=[pltpu.VMEM((nt, nx, LANES), F32)], cost=side_cost, name="parameters",
            )
        else:
            (v,) = call(
                functools.partial(velocity_body, nx, ny, False), [VMEM] * 3, [block_v], (s, v, w),
                aliases={1: 0}, cost=stage_cost, name="velocity",
            )
        v, mine, traction = call(
            functools.partial(velocity_edges_body, nx, ny), [VMEM] * 7, [block_v, row_1, row_1],
            (v, w, s, xl, xh, yl, yh), aliases={0: 0}, cost=side_cost, name="velocity_edges",
        )
        other = swap_odd(mine, "normal")
        yu, yd = call(
            functools.partial(pack_velocity_y_body, nx, ny), [VMEM],
            [((4, nt, nx, LANES), VMEM), ((5, nt, nx, LANES), VMEM)], (v,), cost=side_cost,
            name="pack_normal",
        )
        yl, yh = shift_up(yu, "normal"), shift_down(yd, "normal")
        outs = [block_v, ((4, nt, ny, LANES), VMEM), ((5, nt, ny, LANES), VMEM)] + [row_1] * 4
        if last:
            outs.append(((2, nt, nx // 2, LANES), VMEM))
        got = call(
            functools.partial(fault_body, nx, ny, last), [VMEM] * 6, outs,
            (mine, other, traction, par, state, v), aliases={5: 0}, cost=side_cost, name="fault",
        )
        v, xu, xd, state, minus, plus, trac_new = got[:7]
        xl, xh = shift_up(xu, "strike"), shift_down(xd, "strike")
        body = functools.partial(stress_body, nx, ny, first)
        if last:
            half_rows = ((2, nt, nx // 2, LANES), VMEM)
            back, holders = got[7], [members // 2 - 1, members // 2]
            s, back = call(
                functools.partial(last_begin_body, nx, ny), [VMEM] * 4, [block_s, half_rows],
                (v, s, m, back), aliases={1: 0}, cost=stage_cost,
                name="last_begin",
            )
            edges, bits = [2], []
            bit = members // 4
            while bit >= 1:
                bits.append(bit)
                bit //= 2
            parts = max(len(bits) - 1, 1)
            for j in range(parts):
                edges.append(2 + (nx - 4) * (j + 1) // parts)
            s_out = v_out = None
            for j, bit in enumerate(bits):
                came = swap(back, bit)
                if j < parts:
                    outs = [block_s, ((6, flat, nz), HBM)]
                    ins = [VMEM] * 4
                    args = [v, s, m, trac_new]
                    aliases = {1: 0}
                    if j == 0:
                        ins, args = ins + [VMEM] * 4, args + [yl, yh, minus, plus]
                        outs.append(((3, flat, nz), HBM))
                    else:
                        ins, args = ins + [HBM], args + [s_out]
                        aliases[4] = 1
                    parts_out = call(
                        functools.partial(
                            last_slabs_body, nx, ny, edges[j], edges[j + 1], j == 0
                        ),
                        ins, outs, args, scratch=[dma(9)], aliases=aliases, cost=part_cost,
                        name=f"last_slabs_{j}",
                    )
                    s, s_out = parts_out[:2]
                    if j == 0:
                        v_out = parts_out[2]
                if j < len(bits) - 1:
                    came, s = tie((came, s))
                    (back,) = call(
                        functools.partial(choose_body, tuple(holders)), [VMEM] * 2, [half_rows],
                        (back, came), cost=side_cost, name="choose",
                    )
                    holders += [h ^ bit for h in holders]
            s_out, slip, state_out = call(
                functools.partial(stress_last_body, nx, ny, rows, tuple(holders)),
                [VMEM] * 7 + [HBM],
                [((6, flat, nz), HBM), ((rows, nz), HBM), ((rows, nz), HBM)],
                (s, m, xl, xh, trac_new, back, came, s_out),
                scratch=[pltpu.VMEM((2, rows, nz), F32), dma(13)],
                aliases={7: 0}, cost=side_cost, name="edges_last",
            )
            continue
        if first:
            s, m = call(
                body, [VMEM] * 3, [block_s, block_1], (v, s, m), aliases={1: 0, 2: 1},
                cost=stage_cost, name="stress_first",
            )
        else:
            (s,) = call(
                body, [VMEM] * 3, [block_s], (v, s, m), aliases={1: 0}, cost=stage_cost,
                name="stress",
            )
        s, xu, xd, yu, yd = call(
            functools.partial(stress_edges_body, nx, ny), [VMEM] * 9,
            [block_s, ((5, nt, ny, LANES), VMEM), ((4, nt, ny, LANES), VMEM),
             ((5, nt, nx, LANES), VMEM), ((4, nt, nx, LANES), VMEM)],
            (s, m, xl, xh, yl, yh, minus, plus, trac_new), aliases={0: 0}, cost=side_cost,
            name="stress_edges",
        )
    return (
        v_out.reshape(3, nx, ny, nz),
        s_out.reshape(6, nx, ny, nz),
        slip,
        state_out,
    )


def solution(mesh):
    block = P(None, "strike", "normal", None)
    part = P("strike", "normal", None)
    row = P(("strike", "normal"), None)
    return jax.shard_map(
        local,
        mesh=mesh,
        in_specs=(block, block, part, part, row, row, row, P()),
        out_specs=(block, block, row, row),
        check_vma=False,
    )
```

```python
import functools

import jax
import jax.numpy as jnp
from jax import lax
from jax.experimental import pallas as pl
from jax.experimental.pallas import tpu as pltpu
from jax.sharding import PartitionSpec as P

STEPS = 2
NEWTON = 4

C2 = -1.0 / 24.0
RATIO = (9.0 / 8.0) / C2
DT = 0.1
STEP = DT * C2
ETA = 1.0

F32 = jnp.float32
SXX, SYY, SZZ, SXY, SXZ, SYZ = range(6)


def shift_up(x, axis):
    count = lax.axis_size(axis)
    return lax.ppermute(x, axis, [(i, (i + 1) % count) for i in range(count)])


def shift_down(x, axis):
    count = lax.axis_size(axis)
    return lax.ppermute(x, axis, [((i + 1) % count, i) for i in range(count)])


def swap_odd(x, axis):
    count = lax.axis_size(axis)
    pairs = []
    for i in range(1, count, 2):
        j = (i + 1) % count
        pairs += [(i, j), (j, i)]
    return lax.ppermute(x, axis, pairs)


def swap(x, bit):
    count = lax.axis_size("normal")
    return lax.ppermute(x, "normal", [(i, i ^ bit) for i in range(count)])


VMEM = pl.BlockSpec(memory_space=pltpu.VMEM)
SMEM = pl.BlockSpec(memory_space=pltpu.SMEM)
HBM = pl.BlockSpec(memory_space=pltpu.HBM)


def call(body, ins, outs, args, scratch=(), aliases=None, cost=None, name=None):
    shapes = [
        pltpu.VMEM(shape, F32) if spec is VMEM else jax.ShapeDtypeStruct(shape, F32)
        for shape, spec in outs
    ]
    return pl.pallas_call(
        body,
        out_shape=shapes,
        in_specs=ins,
        out_specs=[spec for _, spec in outs],
        scratch_shapes=list(scratch),
        input_output_aliases=aliases or {},
        compiler_params=pltpu.CompilerParams(vmem_limit_bytes=16 << 20),
        cost_estimate=cost,
        name=name,
    )(*args)


SUB, LANES = 8, 128


class Shifts:
    def __init__(self, ny):
        self.count = ny // SUB
        self.row = lax.broadcasted_iota(jnp.int32, (SUB, LANES), 0)
        self.lane = lax.broadcasted_iota(jnp.int32, (SUB, LANES), 1)

    def rows(self, here, ref, comp, slab, offset):
        edge = offset > 0
        keep = self.row < SUB - offset if edge else self.row >= -offset
        outer = self.count - 1 if edge else 0
        if here.static:
            turned = [[pltpu.roll(f, (-offset) % SUB, 0) for f in fs] for fs in slab]
            out = []
            for fs in turned:
                line = []
                for h, f in enumerate(fs):
                    j = h + 1 if edge else h - 1
                    line.append(jnp.where(keep, f, 0.0 if h == outer else fs[j]))
                out.append(line)
            return out
        return [
            [jnp.where(keep, f, 0.0) if h == outer else f for h, f in enumerate(fs)]
            for fs in here.load(ref, comp, 0, offset)
        ]

    def y_minus(self, here, ref, comp, slab):
        near = [self.rows(here, ref, comp, slab, o) for o in (-1, 1, -2)]
        return each(lambda f, b, c, d: RATIO * (f - b) + (c - d), slab, *near)

    def y_plus(self, here, ref, comp, slab):
        near = [self.rows(here, ref, comp, slab, o) for o in (1, 2, -1)]
        return each(lambda f, b, c, d: RATIO * (b - f) + (c - d), slab, *near)

    def lines(self, f, slab):
        columns = [f([fs[h] for fs in slab]) for h in range(self.count)]
        return [[column[k] for column in columns] for k in range(len(slab))]

    def z_minus(self, slab):
        def line(fs):
            n, lane = len(fs), self.lane
            r = [pltpu.roll(f, LANES - 1, 1) for f in fs]
            p = [jnp.where(lane < LANES - 1, r[k], r[k + 1] if k + 1 < n else 0.0) for k in range(n)]
            w = [RATIO * p[k] + fs[k] for k in range(n)]
            end = jnp.where(lane == LANES - 1, RATIO * r[0], 0.0)
            w[-1] = jnp.where(lane < LANES - 2, w[-1], end)
            q = [pltpu.roll(x, 2, 1) for x in w]
            return [RATIO * fs[k] + p[k] - jnp.where(lane >= 2, q[k], q[k - 1]) for k in range(n)]

        return self.lines(line, slab)

    def z_plus(self, slab):
        def line(fs):
            n, lane = len(fs), self.lane
            r = [pltpu.roll(f, 1, 1) for f in fs]
            m = [jnp.where(lane >= 1, r[k], r[k - 1] if k else 0.0) for k in range(n)]
            w = [RATIO * m[k] + fs[k] for k in range(n)]
            w[0] = jnp.where(lane >= 2, w[0], jnp.where(lane == 0, RATIO * r[-1], 0.0))
            q = [pltpu.roll(x, LANES - 2, 1) for x in w]
            return [
                jnp.where(lane < LANES - 2, q[k], q[(k + 1) % n]) - (RATIO * fs[k] + m[k])
                for k in range(n)
            ]

        return self.lines(line, slab)


def each(f, *slabs):
    return [[f(*pieces) for pieces in zip(*lines)] for lines in zip(*slabs)]


def add(*slabs):
    return each(lambda *parts: functools.reduce(lambda p, q: p + q, parts), *slabs)


def tile(k):
    return slice(k * LANES, (k + 1) * LANES)


def to_tiles(source, target, sems):
    return [
        pltpu.make_async_copy(source.at[:, tile(k)], target.at[k], sems.at[k])
        for k in range(target.shape[0])
    ]


def from_tiles(source, target, sems):
    return [
        pltpu.make_async_copy(source.at[k], target.at[:, tile(k)], sems.at[k])
        for k in range(source.shape[0])
    ]


def run(copies):
    for c in copies:
        c.start()
    for c in copies:
        c.wait()


class Slabs:
    def __init__(self, x, nx, ny, static):
        self.x, self.nx, self.ny, self.static = x, nx, ny, static

    def at(self, h, offset=0, row=0):
        start = (self.x + offset) * self.ny + h * SUB
        if not self.static:
            start = pl.multiple_of(start, SUB)
        return pl.ds(start + row, SUB)

    def load(self, ref, comp, offset=0, row=0):
        return [
            [ref[comp, k, self.at(h, offset, row), :] for h in range(self.ny // SUB)]
            for k in range(ref.shape[1])
        ]

    def near(self, ref, comp, offset):
        if self.static and not 0 <= self.x + offset < self.nx:
            return None
        return self.load(ref, comp, offset)

    def difference(self, ref, comp, a, b, c, d):
        total = None
        for p, q, factor in ((a, b, RATIO), (c, d, None)):
            p, q = self.near(ref, comp, p), self.near(ref, comp, q)
            if p is None and q is None:
                continue
            if p is None:
                term = each(lambda f: -f, q)
            else:
                term = p if q is None else each(lambda f, g: f - g, p, q)
            if factor is not None:
                term = each(lambda f: factor * f, term)
            total = term if total is None else add(total, term)
        return total

    def minus(self, ref, comp):
        return self.difference(ref, comp, 0, -1, 1, -2)

    def plus(self, ref, comp):
        return self.difference(ref, comp, 1, 0, 2, -1)


def run_slabs(begin, end, body):
    def step(i, carry):
        body(begin + 2 * i, False)
        body(begin + 2 * i + 1, False)
        return carry

    lax.fori_loop(0, (end - begin) // 2, step, 0)
    if (end - begin) % 2:
        body(end - 1, True)


def over_x(nx, body, parts=1, before=None):
    for j in range(parts):
        begin, end = nx * j // parts, nx * (j + 1) // parts
        if before is not None:
            before(j)
        first, last = max(begin, 2), min(end, nx - 2)
        for x in range(begin, first):
            body(x, True)
        run_slabs(first, last, body)
        for x in range(last, end):
            body(x, True)


LOADS = 4


def velocity_body(nx, ny, first, s, v_in, b_in, *refs):
    tiles = s.shape[1]
    before = None
    if first:
        m_in, v, bd, md, sem = refs
        loads = []
        for j in range(LOADS):
            at = pl.ds(nx * j // LOADS * ny, nx // LOADS * ny)
            pairs = [(b_in, bd)] + [(v_in.at[c], v.at[c]) for c in range(3)]
            loads.append(
                [
                    pltpu.make_async_copy(p.at[at, tile(k)], q.at[k, at], sem.at[4 * j + i, k])
                    for i, (p, q) in enumerate(pairs)
                    for k in range(tiles)
                ]
            )
        late = to_tiles(m_in, md, sem.at[4 * LOADS])
        for c in sum(loads, []) + late:
            c.start()

        def before(j):
            for c in loads[j]:
                c.wait()

    else:
        (v,) = refs
    sh = Shifts(ny)

    def body(x, static):
        here = Slabs(x, nx, ny, static)
        sxy, sxz, syz = here.load(s, SXY), here.load(s, SXZ), here.load(s, SYZ)
        syy = here.load(s, SYY)
        a = (
            add(here.plus(s, SXX), sh.y_minus(here, s, SXY, sxy), sh.z_minus(sxz)),
            add(here.minus(s, SXY), sh.y_plus(here, s, SYY, syy), sh.z_minus(syz)),
            add(here.minus(s, SXZ), sh.y_minus(here, s, SYZ, syz), sh.z_plus(here.load(s, SZZ))),
        )
        for k in range(tiles):
            for h in range(ny // SUB):
                at = here.at(h)
                if first:
                    w = STEP * bd[k, at, :]
                    bd[k, at, :] = w
                else:
                    w = b_in[k, at, :]
                for c in range(3):
                    v[c, k, at, :] = v[c, k, at, :] + w * a[c][k][h]

    over_x(nx, body, LOADS if first else 1, before)
    if first:
        for c in late:
            c.wait()


def stress_slabs(nx, ny, v, s, m_in, md):
    sh = Shifts(ny)

    def body(x, static):
        here = Slabs(x, nx, ny, static)
        vx, vy, vz = here.load(v, 0), here.load(v, 1), here.load(v, 2)
        exx, eyy, ezz = here.minus(v, 0), sh.y_minus(here, v, 1, vy), sh.z_minus(vz)
        exy = add(here.plus(v, 1), sh.y_plus(here, v, 0, vx))
        exz = add(here.plus(v, 2), sh.z_plus(vx))
        eyz = add(sh.z_plus(vy), sh.y_plus(here, v, 2, vz))
        tr = add(exx, eyy, ezz)
        for k in range(s.shape[1]):
            for h in range(ny // SUB):
                at = here.at(h)
                w = m_in[k, at, :]
                if md is not None:
                    w = STEP * w
                    md[k, at, :] = w
                for c, e in ((SXX, exx), (SYY, eyy), (SZZ, ezz)):
                    s[c, k, at, :] = s[c, k, at, :] + w * (tr[k][h] + 2.0 * e[k][h])
                for c, e in ((SXY, exy), (SXZ, exz), (SYZ, eyz)):
                    s[c, k, at, :] = s[c, k, at, :] + w * e[k][h]

    return body


def stress_body(nx, ny, first, v, s_in, m_in, s, *md):
    del s_in
    over_x(nx, stress_slabs(nx, ny, v, s, m_in, md[0] if first else None))


def slabs_out(ny, begin, end, s, out, sems):
    span = pl.ds(begin * ny, (end - begin) * ny)
    return [
        pltpu.make_async_copy(s.at[c, k, span], out.at[c, span, tile(k)], sems.at[c, k])
        for c in range(s.shape[0])
        for k in range(s.shape[1])
    ]


def last_slabs_body(nx, ny, part, before, begin, end, v, s_in, m, traction, *refs):
    del s_in
    e = Edges(nx, ny)
    on_minus, _ = fault_side()

    def fault_rows(begin, end):
        at = pl.ds(begin * ny + ny - 1, end - begin, stride=ny)
        s[SXY, :, at, :] = jnp.where(on_minus, traction[:, begin:end, :], s[SXY, :, at, :])

    if part == 0:
        s, v_out, sem = refs
        out = []
        for c in range(3):
            out += from_tiles(v.at[c], v_out.at[c], sem.at[c])
        for c in out:
            c.start()
    else:
        s, s_out, sem = refs[-3:]
        if part == 1:
            stress_y_terms(s, m, e, ny, *refs[:4])
            fault_rows(before, begin)
        out = slabs_out(ny, before, begin, s, s_out, sem)
        for c in out:
            c.start()
    body = stress_slabs(nx, ny, v, s, m, None)
    if part == 0:
        for x in (0, 1, nx - 2, nx - 1):
            body(x, True)
    run_slabs(begin, end, body)
    if part > 0:
        fault_rows(begin, end)
    for c in out:
        c.wait()


class Edges:
    def __init__(self, nx, ny):
        self.nx, self.ny = nx, ny

    def x(self, i):
        return pl.ds(i * self.ny, self.ny)

    def y(self, i):
        return pl.ds(i, self.nx, stride=self.ny)


def minus_edges(n, low, high):
    return (
        (0, -RATIO * low[1] - low[0]),
        (1, -low[1]),
        (n - 1, high[0]),
    )


def plus_edges(n, low, high):
    return (
        (0, -low[0]),
        (n - 1, RATIO * high[0] + high[1]),
        (n - 2, high[0]),
    )


def sides():
    out = []
    for axis in ("strike", "normal"):
        i = lax.axis_index(axis)
        last = lax.axis_size(axis) - 1
        out += [jnp.where(i > 0, 1.0, 0.0).astype(F32), jnp.where(i < last, 1.0, 0.0).astype(F32)]
    return out


def fault_side():
    position = lax.axis_index("normal")
    half = lax.axis_size("normal") // 2
    return position == half - 1, position == half


def stress_x_terms(s, w, e, nx, xl, xh):
    low, high = sides()[:2]
    a = [xl[k] * low for k in range(4)]
    b = [xh[k] * high for k in range(5)]
    for i, value in minus_edges(nx, a[0:2], b[0:1]):
        add_rows(s, SXX, w, e.x(i), 3.0, value)
        add_rows(s, SYY, w, e.x(i), 1.0, value)
        add_rows(s, SZZ, w, e.x(i), 1.0, value)
    for i, value in plus_edges(nx, a[2:3], b[1:3]):
        add_rows(s, SXY, w, e.x(i), 1.0, value)
    for i, value in plus_edges(nx, a[3:4], b[3:5]):
        add_rows(s, SXZ, w, e.x(i), 1.0, value)


def stress_y_terms(s, w, e, ny, yl, yh, minus, plus):
    low, high = sides()[2:]
    on_minus, on_plus = fault_side()
    a = [yl[k] * low for k in range(4)]
    b = [yh[k] * high for k in range(5)]
    a[2] = jnp.where(on_plus, minus[...], a[2])
    b[1] = jnp.where(on_minus, plus[...], b[1])
    for i, value in minus_edges(ny, a[0:2], b[0:1]):
        add_rows(s, SXX, w, e.y(i), 1.0, value)
        add_rows(s, SYY, w, e.y(i), 3.0, value)
        add_rows(s, SZZ, w, e.y(i), 1.0, value)
    for i, value in plus_edges(ny, a[2:3], b[1:3]):
        add_rows(s, SXY, w, e.y(i), 1.0, value)
    for i, value in plus_edges(ny, a[3:4], b[3:5]):
        add_rows(s, SYZ, w, e.y(i), 1.0, value)


def add_rows(ref, comp, w, at, factor, value):
    ref[comp, :, at, :] = ref[comp, :, at, :] + w[:, at, :] * (factor * value if factor != 1.0 else value)


def pack_stress_x(s, e, up, down):
    nx = e.nx
    for k, (c, i) in enumerate(
        ((SXX, nx - 1), (SXY, nx - 2), (SXY, nx - 1), (SXZ, nx - 2), (SXZ, nx - 1))
    ):
        up[k] = s[c, :, e.x(i), :]
    for k, (c, i) in enumerate(((SXX, 0), (SXX, 1), (SXY, 0), (SXZ, 0))):
        down[k] = s[c, :, e.x(i), :]


def pack_stress_y(s, e, up, down):
    ny = e.ny
    for k, (c, i) in enumerate(
        ((SYY, ny - 1), (SXY, ny - 2), (SXY, ny - 1), (SYZ, ny - 2), (SYZ, ny - 1))
    ):
        up[k] = s[c, :, e.y(i), :]
    for k, (c, i) in enumerate(((SYY, 0), (SYY, 1), (SXY, 0), (SYZ, 0))):
        down[k] = s[c, :, e.y(i), :]


def load_body(nx, ny, stress, s, xu, xd, yu, yd, sem):
    e = Edges(nx, ny)
    order = (SXX, SXY, SXZ, SYY, SYZ, SZZ)
    copies = {c: to_tiles(stress.at[c], s.at[c], sem.at[c]) for c in order}

    def wait(*comps):
        for c in comps:
            for copy in copies[c]:
                copy.wait()

    for c in order:
        for copy in copies[c]:
            copy.start()
    wait(SXX, SXY, SXZ)
    pack_stress_x(s, e, xu, xd)
    wait(SYY, SYZ)
    pack_stress_y(s, e, yu, yd)
    wait(SZZ)


def velocity_edges_body(nx, ny, v_in, w, s, xl, xh, yl, yh, v, mine, traction):
    del v_in
    e = Edges(nx, ny)
    fxl, fxh, fyl, fyh = sides()
    a = [xl[k] * fxl for k in range(5)]
    b = [xh[k] * fxh for k in range(4)]
    for comp, terms in (
        (0, plus_edges(nx, a[0:1], b[0:2])),
        (1, minus_edges(nx, a[1:3], b[2:3])),
        (2, minus_edges(nx, a[3:5], b[3:4])),
    ):
        for i, value in terms:
            add_rows(v, comp, w, e.x(i), 1.0, value)
    a = [yl[k] * fyl for k in range(5)]
    b = [yh[k] * fyh for k in range(4)]
    for comp, terms in (
        (1, plus_edges(ny, a[0:1], b[0:2])),
        (0, minus_edges(ny, a[1:3], b[2:3])),
        (2, minus_edges(ny, a[3:5], b[3:4])),
    ):
        for i, value in terms:
            add_rows(v, comp, w, e.y(i), 1.0, value)
    odd = lax.rem(lax.axis_index("normal"), 2) == 1
    mine[...] = jnp.where(odd, v[0, :, e.y(ny - 1), :], v[0, :, e.y(0), :])
    traction[...] = jnp.where(odd, s[SXY, :, e.y(ny - 1), :], yl[2])


def pack_velocity_y_body(nx, ny, v, yu, yd):
    e = Edges(nx, ny)
    for k, (c, i) in enumerate(((1, ny - 2), (1, ny - 1), (0, ny - 1), (2, ny - 1))):
        yu[k] = v[c, :, e.y(i), :]
    for k, (c, i) in enumerate(((1, 0), (0, 0), (0, 1), (2, 0), (2, 1))):
        yd[k] = v[c, :, e.y(i), :]


def inverse_sinh(values):
    magnitude = jnp.abs(values)
    root = jnp.sqrt(1.0 + magnitude * magnitude)
    result = jnp.log1p(magnitude + magnitude * magnitude / (1.0 + root))
    return jnp.where(values < 0.0, -result, result)


def fault_body(nx, ny, last, *refs):
    mine, other, traction, par, st_in, v_in, v, xu, xd, st, minus_o, plus_o, trac_o = refs[:13]
    del v_in
    e = Edges(nx, ny)
    position = lax.axis_index("normal")
    members = lax.axis_size("normal")
    odd = lax.rem(position, 2) == 1
    on_minus, on_plus = fault_side()
    m, o = mine[...], other[...]
    minus = jnp.where(odd, m, o)
    plus = jnp.where(odd, o, m)
    mask, a, b, inv_len, sigma = (par[k] for k in range(5))
    state = st_in[...]
    locked = traction[...] + ETA * (plus - minus)
    c = 0.5 * jnp.exp(state / a)
    weight = sigma * a
    rate = jnp.zeros_like(locked)
    for _ in range(NEWTON):
        arg = c * rate
        residue = locked - ETA * rate - weight * inverse_sinh(arg)
        slope = ETA + weight * c / jnp.sqrt(1.0 + arg * arg)
        rate = rate + residue / slope
    rate = rate * mask
    state = state + DT * inv_len * (jnp.exp(-state / b) - jnp.abs(rate))
    st[...] = state
    trac_o[...] = locked - ETA * rate
    middle = 0.5 * (minus + plus)
    minus = middle - 0.5 * rate
    plus = middle + 0.5 * rate
    minus_o[...] = minus
    plus_o[...] = plus
    v[0, :, e.y(ny - 1), :] = jnp.where(on_minus, minus, v[0, :, e.y(ny - 1), :])
    v[0, :, e.y(0), :] = jnp.where(on_plus, plus, v[0, :, e.y(0), :])
    for k, (comp, i) in enumerate(((0, nx - 2), (0, nx - 1), (1, nx - 1), (2, nx - 1))):
        xu[k] = v[comp, :, e.x(i), :]
    for k, (comp, i) in enumerate(((0, 0), (1, 0), (1, 1), (2, 0), (2, 1))):
        xd[k] = v[comp, :, e.x(i), :]
    if last:
        (back,) = refs[13:]
        half = nx // 2
        upper = position >= members // 2
        for q, value in enumerate((rate, state)):
            back[q] = jnp.where(upper, value[:, half:, :], value[:, :half, :])


def choose_body(holders, mine, got, out):
    out[...] = jnp.where(holds(holders), mine[...], got[...])


def holds(holders):
    position = lax.axis_index("normal")
    return functools.reduce(lambda p, q: p | q, [position == h for h in holders])


def stress_edges_body(nx, ny, s_in, w, xl, xh, yl, yh, minus, plus, traction, s, xu, xd, yu, yd):
    del s_in
    e = Edges(nx, ny)
    on_minus, _ = fault_side()
    stress_x_terms(s, w, e, nx, xl, xh)
    stress_y_terms(s, w, e, ny, yl, yh, minus, plus)
    s[SXY, :, e.y(ny - 1), :] = jnp.where(on_minus, traction[...], s[SXY, :, e.y(ny - 1), :])
    pack_stress_x(s, e, xu, xd)
    pack_stress_y(s, e, yu, yd)


def stress_last_body(
    nx, ny, rows, begin, holders, s, w, xl, xh, traction, mine, got, o_in, out, slip, state, own, sem
):
    del o_in
    e = Edges(nx, ny)
    early = slabs_out(ny, begin, nx - 2, s, out, sem)
    for c in early:
        c.start()
    on_minus, _ = fault_side()
    stress_x_terms(s, w, e, nx, xl, xh)
    copies = []
    for x in (0, 1, nx - 2, nx - 1):
        at = pl.ds(x * ny + ny - 1, 1)
        s[SXY, :, at, :] = jnp.where(on_minus, traction[:, x : x + 1, :], s[SXY, :, at, :])
    for j, x in enumerate((0, nx - 2)):
        span = pl.ds(x * ny, 2 * ny)
        for c in range(6):
            for k in range(s.shape[1]):
                copies.append(
                    pltpu.make_async_copy(
                        s.at[c, k, span], out.at[c, span, tile(k)], sem.at[6 + j * 6 + c, k]
                    )
                )
    for c in copies:
        c.start()
    half = lax.axis_size("normal") // 2
    at = pl.ds(rows * lax.rem(lax.axis_index("normal"), half), rows)
    have = holds(holders)
    for k in range(s.shape[1]):
        for q in range(2):
            own[q, :, tile(k)] = jnp.where(have, mine[q, k, at, :], got[q, k, at, :])
    for q, target in enumerate((slip, state)):
        copy = pltpu.make_async_copy(own.at[q], target, sem.at[18, q])
        copy.start()
        copies.append(copy)
    for c in early + copies:
        c.wait()


def own_body(state, mask, ids, out, st, mk, rg, sem):
    rows = state.shape[0]
    run(
        [
            pltpu.make_async_copy(a, b, sem.at[0, k])
            for k, (a, b) in enumerate(((state, st), (mask, mk), (ids, rg)))
        ]
    )
    out[0, 0:rows, :] = st[...]
    out[0, rows : 2 * rows, :] = mk[...].astype(F32)
    out[0, 2 * rows : 3 * rows, :] = rg[...].astype(F32)
    pad = out.shape[1] - 3 * rows
    if pad:
        out[0, 3 * rows :, :] = jnp.zeros((pad, out.shape[2]), F32)


def merge_body(bit, mine, got, out):
    upper = lax.rem(lax.axis_index("normal") // bit, 2) == 1
    n = mine.shape[0]
    a, b = mine[...], got[...]
    out[0:n] = jnp.where(upper, b, a)
    out[n : 2 * n] = jnp.where(upper, a, b)


def parameters_body(rows, mine, got, table, st, par, tmp):
    half = mine.shape[0]
    upper = lax.axis_index("normal") >= half
    for k in range(2 * half):
        at = slice(k * rows, (k + 1) * rows)
        a, b = (mine, got) if k < half else (got, mine)
        block = jnp.where(upper, b[k % half], a[k % half])
        for z in range(st.shape[0]):
            st[z, at, :] = block[0:rows, tile(z)]
            par[0, z, at, :] = block[rows : 2 * rows, tile(z)]
            tmp[z, at, :] = block[2 * rows : 3 * rows, tile(z)]
    ids = tmp[...]
    for j in range(4):
        p = jnp.zeros_like(ids)
        for r in range(table.shape[1]):
            p = jnp.where(ids == float(r), table[j, r], p)
        par[1 + j] = p


def local(velocity, stress, modulus, buoyancy, fault_state, fault_mask, region_ids, friction_table):
    members = lax.axis_size("normal")
    _, nx, ny, nz = velocity.shape
    rows = fault_state.shape[0]
    flat, nt = nx * ny, nz // LANES
    pin = lambda x: pltpu.with_memory_space_constraint(x, pltpu.HBM)
    vel_in = pin(velocity.reshape(3, flat, nz))
    str_in = pin(stress.reshape(6, flat, nz))
    mod_in = pin(modulus.reshape(flat, nz))
    buo_in = pin(buoyancy.reshape(flat, nz))
    fault_in = (pin(fault_state), pin(fault_mask), pin(region_ids))
    dma = lambda n: pltpu.SemaphoreType.DMA((n, nt))
    stage_cost = pl.CostEstimate(flops=4_000_000_000, bytes_accessed=16_000_000, transcendentals=0)
    part_cost = pl.CostEstimate(flops=2_000_000_000, bytes_accessed=8_000_000, transcendentals=0)
    side_cost = pl.CostEstimate(flops=1_000_000, bytes_accessed=1_000_000, transcendentals=0)

    depth = -(-3 * rows // 8) * 8
    (known,) = call(
        own_body, [HBM] * 3, [((1, depth, nz), VMEM)], fault_in,
        scratch=[pltpu.VMEM((rows, nz), F32)] + [pltpu.VMEM((rows, nz), jnp.int32)] * 2 + [dma(1)],
        cost=side_cost, name="own",
    )
    s, xu, xd, yu, yd = call(
        functools.partial(load_body, nx, ny), [HBM],
        [((6, nt, flat, LANES), VMEM), ((5, nt, ny, LANES), VMEM), ((4, nt, ny, LANES), VMEM),
         ((5, nt, nx, LANES), VMEM), ((4, nt, nx, LANES), VMEM)],
        (str_in,), scratch=[dma(6)], cost=side_cost, name="load",
    )
    tie = lax.optimization_barrier

    def merge(known, got, bit):
        return call(
            functools.partial(merge_body, bit), [VMEM] * 2, [((2 * bit, depth, nz), VMEM)],
            (known, got), cost=side_cost, name="merge",
        )[0]

    got = swap(known, 1)
    known, got, xu, xd, yu, yd = tie((known, got, xu, xd, yu, yd))
    known = merge(known, got, 1)
    known = merge(known, swap(known, 2), 2)
    bit = 4
    block_v = ((3, nt, flat, LANES), VMEM)
    block_s = ((6, nt, flat, LANES), VMEM)
    block_1 = ((nt, flat, LANES), VMEM)
    row_1 = ((nt, nx, LANES), VMEM)
    v = w = m = None
    for step in range(STEPS):
        first, last = step == 0, step == STEPS - 1
        xl, xh = shift_up(xu, "strike"), shift_down(xd, "strike")
        yl, yh = shift_up(yu, "normal"), shift_down(yd, "normal")
        if first:
            v, w, m = call(
                functools.partial(velocity_body, nx, ny, True), [VMEM, HBM, HBM, HBM],
                [block_v, block_1, block_1], (s, vel_in, buo_in, mod_in),
                scratch=[dma(4 * LOADS + 1)], cost=stage_cost, name="velocity_first",
            )
            while 2 * bit < members:
                known = merge(known, swap(known, bit), bit)
                bit *= 2
            known, v = tie((known, v))
            state, par = call(
                functools.partial(parameters_body, rows), [VMEM, VMEM, SMEM],
                [((nt, nx, LANES), VMEM), ((5, nt, nx, LANES), VMEM)],
                (known, swap(known, bit), friction_table),
                scratch=[pltpu.VMEM((nt, nx, LANES), F32)], cost=side_cost, name="parameters",
            )
        else:
            (v,) = call(
                functools.partial(velocity_body, nx, ny, False), [VMEM] * 3, [block_v], (s, v, w),
                aliases={1: 0}, cost=stage_cost, name="velocity",
            )
        v, mine, traction = call(
            functools.partial(velocity_edges_body, nx, ny), [VMEM] * 7, [block_v, row_1, row_1],
            (v, w, s, xl, xh, yl, yh), aliases={0: 0}, cost=side_cost, name="velocity_edges",
        )
        other = swap_odd(mine, "normal")
        yu, yd = call(
            functools.partial(pack_velocity_y_body, nx, ny), [VMEM],
            [((4, nt, nx, LANES), VMEM), ((5, nt, nx, LANES), VMEM)], (v,), cost=side_cost,
            name="pack_normal",
        )
        yl, yh = shift_up(yu, "normal"), shift_down(yd, "normal")
        outs = [block_v, ((4, nt, ny, LANES), VMEM), ((5, nt, ny, LANES), VMEM)] + [row_1] * 4
        if last:
            outs.append(((2, nt, nx // 2, LANES), VMEM))
        got = call(
            functools.partial(fault_body, nx, ny, last), [VMEM] * 6, outs,
            (mine, other, traction, par, state, v), aliases={5: 0}, cost=side_cost, name="fault",
        )
        v, xu, xd, state, minus, plus, trac_new = got[:7]
        xl, xh = shift_up(xu, "strike"), shift_down(xd, "strike")
        body = functools.partial(stress_body, nx, ny, first)
        if last:
            half_rows = ((2, nt, nx // 2, LANES), VMEM)
            block_out = ((6, flat, nz), HBM)
            cuts = [2, 2 + (nx - 4) // 6 * 2 + 2, nx - 2 - (nx - 4) // 6 * 2, nx - 2]
            holders = [members // 2 - 1, members // 2]
            bit = members // 4
            back, s_out = got[7], None
            came = swap(back, bit)
            for part in range(3):
                ins, args, aliases, outs = [VMEM] * 4, [v, s, m, trac_new], {1: 0}, [block_s]
                if part == 0:
                    outs += [((3, flat, nz), HBM)]
                elif part == 1:
                    ins, args = ins + [VMEM] * 4, args + [yl, yh, minus, plus]
                    outs += [block_out]
                else:
                    ins, args = ins + [HBM], args + [s_out]
                    outs += [block_out]
                    aliases[4] = 1
                body = functools.partial(
                    last_slabs_body, nx, ny, part, cuts[part - 1] if part else None, cuts[part],
                    cuts[part + 1],
                )
                done = call(
                    body, ins, outs, args, scratch=[dma(3 if part == 0 else 6)], aliases=aliases,
                    cost=part_cost if part else stage_cost, name=f"last_slabs_{part}",
                )
                s = done[0]
                if part == 0:
                    v_out = done[1]
                else:
                    s_out = done[1]
                if bit > 1:
                    came, s = tie((came, s))
                    (back,) = call(
                        functools.partial(choose_body, tuple(holders)), [VMEM] * 2, [half_rows],
                        (back, came), cost=side_cost, name="choose",
                    )
                    holders += [h ^ bit for h in holders]
                    bit //= 2
                    came = swap(back, bit)
            s_out, slip, state_out = call(
                functools.partial(stress_last_body, nx, ny, rows, cuts[2], tuple(holders)),
                [VMEM] * 7 + [HBM], [block_out, ((rows, nz), HBM), ((rows, nz), HBM)],
                (s, m, xl, xh, trac_new, back, came, s_out),
                scratch=[pltpu.VMEM((2, rows, nz), F32), dma(19)],
                aliases={7: 0}, cost=side_cost, name="edges_last",
            )
            continue
        if first:
            s, m = call(
                body, [VMEM] * 3, [block_s, block_1], (v, s, m), aliases={1: 0, 2: 1},
                cost=stage_cost, name="stress_first",
            )
        else:
            (s,) = call(
                body, [VMEM] * 3, [block_s], (v, s, m), aliases={1: 0}, cost=stage_cost,
                name="stress",
            )
        s, xu, xd, yu, yd = call(
            functools.partial(stress_edges_body, nx, ny), [VMEM] * 9,
            [block_s, ((5, nt, ny, LANES), VMEM), ((4, nt, ny, LANES), VMEM),
             ((5, nt, nx, LANES), VMEM), ((4, nt, nx, LANES), VMEM)],
            (s, m, xl, xh, yl, yh, minus, plus, trac_new), aliases={0: 0}, cost=side_cost,
            name="stress_edges",
        )
    return (
        v_out.reshape(3, nx, ny, nz),
        s_out.reshape(6, nx, ny, nz),
        slip,
        state_out,
    )


def solution(mesh):
    block = P(None, "strike", "normal", None)
    part = P("strike", "normal", None)
    row = P(("strike", "normal"), None)
    return jax.shard_map(
        local,
        mesh=mesh,
        in_specs=(block, block, part, part, row, row, row, P()),
        out_specs=(block, block, row, row),
        check_vma=False,
    )
```

```python
import functools

import jax
import jax.numpy as jnp
from jax import lax
from jax.experimental import pallas as pl
from jax.experimental.pallas import tpu as pltpu
from jax.sharding import PartitionSpec as P

STEPS = 2
NEWTON = 4

C2 = -1.0 / 24.0
RATIO = (9.0 / 8.0) / C2
DT = 0.1
STEP = DT * C2
ETA = 1.0

F32 = jnp.float32
SXX, SYY, SZZ, SXY, SXZ, SYZ = range(6)


def shift_up(x, axis):
    count = lax.axis_size(axis)
    return lax.ppermute(x, axis, [(i, (i + 1) % count) for i in range(count)])


def shift_down(x, axis):
    count = lax.axis_size(axis)
    return lax.ppermute(x, axis, [((i + 1) % count, i) for i in range(count)])


def swap_odd(x, axis):
    count = lax.axis_size(axis)
    pairs = []
    for i in range(1, count, 2):
        j = (i + 1) % count
        pairs += [(i, j), (j, i)]
    return lax.ppermute(x, axis, pairs)


def swap(x, bit):
    count = lax.axis_size("normal")
    return lax.ppermute(x, "normal", [(i, i ^ bit) for i in range(count)])


VMEM = pl.BlockSpec(memory_space=pltpu.VMEM)
SMEM = pl.BlockSpec(memory_space=pltpu.SMEM)
HBM = pl.BlockSpec(memory_space=pltpu.HBM)
ANY = pl.BlockSpec(memory_space=pl.ANY)


def call(body, ins, outs, args, scratch=(), aliases=None, cost=None, name=None):
    shapes = [
        pltpu.VMEM(shape, F32) if spec is VMEM else jax.ShapeDtypeStruct(shape, F32)
        for shape, spec in outs
    ]
    return pl.pallas_call(
        body,
        out_shape=shapes,
        in_specs=ins,
        out_specs=[spec for _, spec in outs],
        scratch_shapes=list(scratch),
        input_output_aliases=aliases or {},
        compiler_params=pltpu.CompilerParams(vmem_limit_bytes=16 << 20),
        cost_estimate=cost,
        name=name,
    )(*args)


SUB, LANES = 8, 128


class Shifts:
    def __init__(self, ny):
        self.count = ny // SUB
        self.row = lax.broadcasted_iota(jnp.int32, (SUB, LANES), 0)
        self.lane = lax.broadcasted_iota(jnp.int32, (SUB, LANES), 1)

    def rows(self, here, ref, comp, slab, offset):
        edge = offset > 0
        keep = self.row < SUB - offset if edge else self.row >= -offset
        outer = self.count - 1 if edge else 0
        if here.static:
            turned = [[pltpu.roll(f, (-offset) % SUB, 0) for f in fs] for fs in slab]
            out = []
            for fs in turned:
                line = []
                for h, f in enumerate(fs):
                    j = h + 1 if edge else h - 1
                    line.append(jnp.where(keep, f, 0.0 if h == outer else fs[j]))
                out.append(line)
            return out
        return [
            [jnp.where(keep, f, 0.0) if h == outer else f for h, f in enumerate(fs)]
            for fs in here.load(ref, comp, 0, offset)
        ]

    def y_minus(self, here, ref, comp, slab):
        near = [self.rows(here, ref, comp, slab, o) for o in (-1, 1, -2)]
        return each(lambda f, b, c, d: RATIO * (f - b) + (c - d), slab, *near)

    def y_plus(self, here, ref, comp, slab):
        near = [self.rows(here, ref, comp, slab, o) for o in (1, 2, -1)]
        return each(lambda f, b, c, d: RATIO * (b - f) + (c - d), slab, *near)

    def lines(self, f, slab):
        columns = [f([fs[h] for fs in slab]) for h in range(self.count)]
        return [[column[k] for column in columns] for k in range(len(slab))]

    def z_minus(self, slab):
        def line(fs):
            n, lane = len(fs), self.lane
            r = [pltpu.roll(f, LANES - 1, 1) for f in fs]
            p = [jnp.where(lane < LANES - 1, r[k], r[k + 1] if k + 1 < n else 0.0) for k in range(n)]
            w = [RATIO * p[k] + fs[k] for k in range(n)]
            end = jnp.where(lane == LANES - 1, RATIO * r[0], 0.0)
            w[-1] = jnp.where(lane < LANES - 2, w[-1], end)
            q = [pltpu.roll(x, 2, 1) for x in w]
            return [RATIO * fs[k] + p[k] - jnp.where(lane >= 2, q[k], q[k - 1]) for k in range(n)]

        return self.lines(line, slab)

    def z_plus(self, slab):
        def line(fs):
            n, lane = len(fs), self.lane
            r = [pltpu.roll(f, 1, 1) for f in fs]
            m = [jnp.where(lane >= 1, r[k], r[k - 1] if k else 0.0) for k in range(n)]
            w = [RATIO * m[k] + fs[k] for k in range(n)]
            w[0] = jnp.where(lane >= 2, w[0], jnp.where(lane == 0, RATIO * r[-1], 0.0))
            q = [pltpu.roll(x, LANES - 2, 1) for x in w]
            return [
                jnp.where(lane < LANES - 2, q[k], q[(k + 1) % n]) - (RATIO * fs[k] + m[k])
                for k in range(n)
            ]

        return self.lines(line, slab)


def each(f, *slabs):
    return [[f(*pieces) for pieces in zip(*lines)] for lines in zip(*slabs)]


def add(*slabs):
    return each(lambda *parts: functools.reduce(lambda p, q: p + q, parts), *slabs)


def tile(k):
    return slice(k * LANES, (k + 1) * LANES)


def to_tiles(source, target, sems):
    return [
        pltpu.make_async_copy(source.at[:, tile(k)], target.at[k], sems.at[k])
        for k in range(target.shape[0])
    ]


def from_tiles(source, target, sems):
    return [
        pltpu.make_async_copy(source.at[k], target.at[:, tile(k)], sems.at[k])
        for k in range(source.shape[0])
    ]


def run(copies):
    for c in copies:
        c.start()
    for c in copies:
        c.wait()


class Slabs:
    def __init__(self, x, nx, ny, static):
        self.x, self.nx, self.ny, self.static = x, nx, ny, static

    def at(self, h, offset=0, row=0):
        start = (self.x + offset) * self.ny + h * SUB
        if not self.static:
            start = pl.multiple_of(start, SUB)
        return pl.ds(start + row, SUB)

    def load(self, ref, comp, offset=0, row=0):
        return [
            [ref[comp, k, self.at(h, offset, row), :] for h in range(self.ny // SUB)]
            for k in range(ref.shape[1])
        ]

    def near(self, ref, comp, offset):
        if self.static and not 0 <= self.x + offset < self.nx:
            return None
        return self.load(ref, comp, offset)

    def difference(self, ref, comp, a, b, c, d):
        total = None
        for p, q, factor in ((a, b, RATIO), (c, d, None)):
            p, q = self.near(ref, comp, p), self.near(ref, comp, q)
            if p is None and q is None:
                continue
            if p is None:
                term = each(lambda f: -f, q)
            else:
                term = p if q is None else each(lambda f, g: f - g, p, q)
            if factor is not None:
                term = each(lambda f: factor * f, term)
            total = term if total is None else add(total, term)
        return total

    def minus(self, ref, comp):
        return self.difference(ref, comp, 0, -1, 1, -2)

    def plus(self, ref, comp):
        return self.difference(ref, comp, 1, 0, 2, -1)


def run_slabs(begin, end, body):
    def step(i, carry):
        body(begin + 2 * i, False)
        body(begin + 2 * i + 1, False)
        return carry

    lax.fori_loop(0, (end - begin) // 2, step, 0)
    if (end - begin) % 2:
        body(end - 1, True)


def over_x(nx, body, parts=1, before=None):
    for j in range(parts):
        begin, end = nx * j // parts, nx * (j + 1) // parts
        if before is not None:
            before(j)
        first, last = max(begin, 2), min(end, nx - 2)
        for x in range(begin, first):
            body(x, True)
        run_slabs(first, last, body)
        for x in range(last, end):
            body(x, True)


LOADS = 4


def velocity_body(nx, ny, first, s, v_in, b_in, *refs):
    tiles = s.shape[1]
    before = None
    if first:
        m_in, v, bd, md, sem = refs
        loads = []
        for j in range(LOADS):
            at = pl.ds(nx * j // LOADS * ny, nx // LOADS * ny)
            pairs = [(b_in, bd)] + [(v_in.at[c], v.at[c]) for c in range(3)]
            loads.append(
                [
                    pltpu.make_async_copy(p.at[at, tile(k)], q.at[k, at], sem.at[4 * j + i, k])
                    for i, (p, q) in enumerate(pairs)
                    for k in range(tiles)
                ]
            )
        late = to_tiles(m_in, md, sem.at[4 * LOADS])
        for c in sum(loads, []) + late:
            c.start()

        def before(j):
            for c in loads[j]:
                c.wait()

    else:
        (v,) = refs
    sh = Shifts(ny)

    def body(x, static):
        here = Slabs(x, nx, ny, static)
        sxy, sxz, syz = here.load(s, SXY), here.load(s, SXZ), here.load(s, SYZ)
        syy = here.load(s, SYY)
        a = (
            add(here.plus(s, SXX), sh.y_minus(here, s, SXY, sxy), sh.z_minus(sxz)),
            add(here.minus(s, SXY), sh.y_plus(here, s, SYY, syy), sh.z_minus(syz)),
            add(here.minus(s, SXZ), sh.y_minus(here, s, SYZ, syz), sh.z_plus(here.load(s, SZZ))),
        )
        for k in range(tiles):
            for h in range(ny // SUB):
                at = here.at(h)
                if first:
                    w = STEP * bd[k, at, :]
                    bd[k, at, :] = w
                else:
                    w = b_in[k, at, :]
                for c in range(3):
                    v[c, k, at, :] = v[c, k, at, :] + w * a[c][k][h]

    over_x(nx, body, LOADS if first else 1, before)
    if first:
        for c in late:
            c.wait()


def stress_slabs(nx, ny, v, s, m_in, md):
    sh = Shifts(ny)

    def body(x, static):
        here = Slabs(x, nx, ny, static)
        vx, vy, vz = here.load(v, 0), here.load(v, 1), here.load(v, 2)
        exx, eyy, ezz = here.minus(v, 0), sh.y_minus(here, v, 1, vy), sh.z_minus(vz)
        exy = add(here.plus(v, 1), sh.y_plus(here, v, 0, vx))
        exz = add(here.plus(v, 2), sh.z_plus(vx))
        eyz = add(sh.z_plus(vy), sh.y_plus(here, v, 2, vz))
        tr = add(exx, eyy, ezz)
        for k in range(s.shape[1]):
            for h in range(ny // SUB):
                at = here.at(h)
                w = m_in[k, at, :]
                if md is not None:
                    w = STEP * w
                    md[k, at, :] = w
                for c, e in ((SXX, exx), (SYY, eyy), (SZZ, ezz)):
                    s[c, k, at, :] = s[c, k, at, :] + w * (tr[k][h] + 2.0 * e[k][h])
                for c, e in ((SXY, exy), (SXZ, exz), (SYZ, eyz)):
                    s[c, k, at, :] = s[c, k, at, :] + w * e[k][h]

    return body


def stress_body(nx, ny, first, v, s_in, m_in, s, *md):
    del s_in
    over_x(nx, stress_slabs(nx, ny, v, s, m_in, md[0] if first else None))


def slabs_out(ny, begin, end, s, out, sems):
    span = pl.ds(begin * ny, (end - begin) * ny)
    return [
        pltpu.make_async_copy(s.at[c, k, span], out.at[c, span, tile(k)], sems.at[c, k])
        for c in range(s.shape[0])
        for k in range(s.shape[1])
    ]


def last_slabs_body(nx, ny, part, before, begin, end, v, s_in, m, traction, *refs):
    del s_in
    e = Edges(nx, ny)
    on_minus, _ = fault_side()

    def fault_rows(begin, end):
        at = pl.ds(begin * ny + ny - 1, end - begin, stride=ny)
        s[SXY, :, at, :] = jnp.where(on_minus, traction[:, begin:end, :], s[SXY, :, at, :])

    if part == 0:
        s, v_out, sem = refs
        out = []
        for c in range(3):
            out += from_tiles(v.at[c], v_out.at[c], sem.at[c])
        for c in out:
            c.start()
    else:
        s, s_out, sem = refs[-3:]
        if part == 1:
            stress_y_terms(s, m, e, ny, *refs[:4])
            fault_rows(before, begin)
        out = slabs_out(ny, before, begin, s, s_out, sem)
        for c in out:
            c.start()
    body = stress_slabs(nx, ny, v, s, m, None)
    if part == 0:
        for x in (0, 1, nx - 2, nx - 1):
            body(x, True)
    run_slabs(begin, end, body)
    if part > 0:
        fault_rows(begin, end)
    for c in out:
        c.wait()


class Edges:
    def __init__(self, nx, ny):
        self.nx, self.ny = nx, ny

    def x(self, i):
        return pl.ds(i * self.ny, self.ny)

    def y(self, i):
        return pl.ds(i, self.nx, stride=self.ny)


def minus_edges(n, low, high):
    return (
        (0, -RATIO * low[1] - low[0]),
        (1, -low[1]),
        (n - 1, high[0]),
    )


def plus_edges(n, low, high):
    return (
        (0, -low[0]),
        (n - 1, RATIO * high[0] + high[1]),
        (n - 2, high[0]),
    )


def sides():
    out = []
    for axis in ("strike", "normal"):
        i = lax.axis_index(axis)
        last = lax.axis_size(axis) - 1
        out += [jnp.where(i > 0, 1.0, 0.0).astype(F32), jnp.where(i < last, 1.0, 0.0).astype(F32)]
    return out


def fault_side():
    position = lax.axis_index("normal")
    half = lax.axis_size("normal") // 2
    return position == half - 1, position == half


def stress_x_terms(s, w, e, nx, xl, xh):
    low, high = sides()[:2]
    a = [xl[k] * low for k in range(4)]
    b = [xh[k] * high for k in range(5)]
    for i, value in minus_edges(nx, a[0:2], b[0:1]):
        add_rows(s, SXX, w, e.x(i), 3.0, value)
        add_rows(s, SYY, w, e.x(i), 1.0, value)
        add_rows(s, SZZ, w, e.x(i), 1.0, value)
    for i, value in plus_edges(nx, a[2:3], b[1:3]):
        add_rows(s, SXY, w, e.x(i), 1.0, value)
    for i, value in plus_edges(nx, a[3:4], b[3:5]):
        add_rows(s, SXZ, w, e.x(i), 1.0, value)


def stress_y_terms(s, w, e, ny, yl, yh, minus, plus):
    low, high = sides()[2:]
    on_minus, on_plus = fault_side()
    a = [yl[k] * low for k in range(4)]
    b = [yh[k] * high for k in range(5)]
    a[2] = jnp.where(on_plus, minus[...], a[2])
    b[1] = jnp.where(on_minus, plus[...], b[1])
    for i, value in minus_edges(ny, a[0:2], b[0:1]):
        add_rows(s, SXX, w, e.y(i), 1.0, value)
        add_rows(s, SYY, w, e.y(i), 3.0, value)
        add_rows(s, SZZ, w, e.y(i), 1.0, value)
    for i, value in plus_edges(ny, a[2:3], b[1:3]):
        add_rows(s, SXY, w, e.y(i), 1.0, value)
    for i, value in plus_edges(ny, a[3:4], b[3:5]):
        add_rows(s, SYZ, w, e.y(i), 1.0, value)


def add_rows(ref, comp, w, at, factor, value):
    ref[comp, :, at, :] = ref[comp, :, at, :] + w[:, at, :] * (factor * value if factor != 1.0 else value)


def pack_stress_x(s, e, up, down):
    nx = e.nx
    for k, (c, i) in enumerate(
        ((SXX, nx - 1), (SXY, nx - 2), (SXY, nx - 1), (SXZ, nx - 2), (SXZ, nx - 1))
    ):
        up[k] = s[c, :, e.x(i), :]
    for k, (c, i) in enumerate(((SXX, 0), (SXX, 1), (SXY, 0), (SXZ, 0))):
        down[k] = s[c, :, e.x(i), :]


def pack_stress_y(s, e, up, down):
    ny = e.ny
    for k, (c, i) in enumerate(
        ((SYY, ny - 1), (SXY, ny - 2), (SXY, ny - 1), (SYZ, ny - 2), (SYZ, ny - 1))
    ):
        up[k] = s[c, :, e.y(i), :]
    for k, (c, i) in enumerate(((SYY, 0), (SYY, 1), (SXY, 0), (SYZ, 0))):
        down[k] = s[c, :, e.y(i), :]


def load_body(nx, ny, stress, s, xu, xd, yu, yd, sem):
    e = Edges(nx, ny)
    order = (SXX, SXY, SXZ, SYY, SYZ, SZZ)
    copies = {c: to_tiles(stress.at[c], s.at[c], sem.at[c]) for c in order}

    def wait(*comps):
        for c in comps:
            for copy in copies[c]:
                copy.wait()

    for c in order:
        for copy in copies[c]:
            copy.start()
    wait(SXX, SXY, SXZ)
    pack_stress_x(s, e, xu, xd)
    wait(SYY, SYZ)
    pack_stress_y(s, e, yu, yd)
    wait(SZZ)


def velocity_edges_body(nx, ny, rows, v_in, w, s, xl, xh, yl, yh, *refs):
    del v_in
    v, mine, traction = refs[-3:]
    e = Edges(nx, ny)
    fxl, fxh, fyl, fyh = sides()
    a = [xl[k] * fxl for k in range(5)]
    b = [xh[k] * fxh for k in range(4)]
    for comp, terms in (
        (0, plus_edges(nx, a[0:1], b[0:2])),
        (1, minus_edges(nx, a[1:3], b[2:3])),
        (2, minus_edges(nx, a[3:5], b[3:4])),
    ):
        for i, value in terms:
            add_rows(v, comp, w, e.x(i), 1.0, value)
    a = [yl[k] * fyl for k in range(5)]
    b = [yh[k] * fyh for k in range(4)]
    for comp, terms in (
        (1, plus_edges(ny, a[0:1], b[0:2])),
        (0, minus_edges(ny, a[1:3], b[2:3])),
        (2, minus_edges(ny, a[3:5], b[3:4])),
    ):
        for i, value in terms:
            add_rows(v, comp, w, e.y(i), 1.0, value)
    odd = lax.rem(lax.axis_index("normal"), 2) == 1
    mine[:, 0:nx, :] = jnp.where(odd, v[0, :, e.y(ny - 1), :], v[0, :, e.y(0), :])
    if rows:
        known = refs[0]
        count = known.shape[0] * rows
        for k in range(known.shape[0]):
            for q in range(3):
                at = slice(nx + q * count + k * rows, nx + q * count + (k + 1) * rows)
                for z in range(mine.shape[0]):
                    mine[z, at, :] = known[k, q * rows : (q + 1) * rows, tile(z)]
    traction[...] = jnp.where(odd, s[SXY, :, e.y(ny - 1), :], yl[2])


def pack_velocity_y_body(nx, ny, v, yu, yd):
    e = Edges(nx, ny)
    for k, (c, i) in enumerate(((1, ny - 2), (1, ny - 1), (0, ny - 1), (2, ny - 1))):
        yu[k] = v[c, :, e.y(i), :]
    for k, (c, i) in enumerate(((1, 0), (0, 0), (0, 1), (2, 0), (2, 1))):
        yd[k] = v[c, :, e.y(i), :]


def inverse_sinh(values):
    magnitude = jnp.abs(values)
    root = jnp.sqrt(1.0 + magnitude * magnitude)
    result = jnp.log1p(magnitude + magnitude * magnitude / (1.0 + root))
    return jnp.where(values < 0.0, -result, result)


def fault_parameters(nx, mine, other, table, state, par):
    half = nx // 2
    upper = lax.axis_index("normal") >= lax.axis_size("normal") // 2
    full = []
    for q in range(3):
        at = slice(nx + q * half, nx + (q + 1) * half)
        a, b = mine[:, at, :], other[:, at, :]
        full.append(jnp.concatenate((jnp.where(upper, b, a), jnp.where(upper, a, b)), 1))
    state[...] = full[0]
    par[0] = full[1]
    for j in range(4):
        p = jnp.zeros_like(full[2])
        for r in range(table.shape[1]):
            p = jnp.where(full[2] == float(r), table[j, r], p)
        par[1 + j] = p


def fault_body(nx, ny, first, last, *refs):
    if first:
        mine, other, traction, table, v_in, v, xu, xd, st, minus_o, plus_o, trac_o, par = refs[:13]
        fault_parameters(nx, mine, other, table, st, par)
        st_in = st
    else:
        mine, other, traction, par, st_in, v_in, v, xu, xd, st, minus_o, plus_o, trac_o = refs[:13]
    del v_in
    e = Edges(nx, ny)
    position = lax.axis_index("normal")
    members = lax.axis_size("normal")
    odd = lax.rem(position, 2) == 1
    on_minus, on_plus = fault_side()
    m, o = mine[:, 0:nx, :], other[:, 0:nx, :]
    minus = jnp.where(odd, m, o)
    plus = jnp.where(odd, o, m)
    mask, a, b, inv_len, sigma = (par[k] for k in range(5))
    state = st_in[...]
    locked = traction[...] + ETA * (plus - minus)
    c = 0.5 * jnp.exp(state / a)
    weight = sigma * a
    rate = jnp.zeros_like(locked)
    for _ in range(NEWTON):
        arg = c * rate
        residue = locked - ETA * rate - weight * inverse_sinh(arg)
        slope = ETA + weight * c / jnp.sqrt(1.0 + arg * arg)
        rate = rate + residue / slope
    rate = rate * mask
    state = state + DT * inv_len * (jnp.exp(-state / b) - jnp.abs(rate))
    st[...] = state
    trac_o[...] = locked - ETA * rate
    middle = 0.5 * (minus + plus)
    minus = middle - 0.5 * rate
    plus = middle + 0.5 * rate
    minus_o[...] = minus
    plus_o[...] = plus
    v[0, :, e.y(ny - 1), :] = jnp.where(on_minus, minus, v[0, :, e.y(ny - 1), :])
    v[0, :, e.y(0), :] = jnp.where(on_plus, plus, v[0, :, e.y(0), :])
    for k, (comp, i) in enumerate(((0, nx - 2), (0, nx - 1), (1, nx - 1), (2, nx - 1))):
        xu[k] = v[comp, :, e.x(i), :]
    for k, (comp, i) in enumerate(((0, 0), (1, 0), (1, 1), (2, 0), (2, 1))):
        xd[k] = v[comp, :, e.x(i), :]
    if last:
        (back,) = refs[13:]
        half = nx // 2
        upper = position >= members // 2
        for q, value in enumerate((rate, state)):
            back[q] = jnp.where(upper, value[:, half:, :], value[:, :half, :])


def choose_body(holders, mine, got, out):
    out[...] = jnp.where(holds(holders), mine[...], got[...])


def holds(holders):
    position = lax.axis_index("normal")
    return functools.reduce(lambda p, q: p | q, [position == h for h in holders])


def stress_edges_body(nx, ny, s_in, w, xl, xh, yl, yh, minus, plus, traction, s, xu, xd, yu, yd):
    del s_in
    e = Edges(nx, ny)
    on_minus, _ = fault_side()
    stress_x_terms(s, w, e, nx, xl, xh)
    stress_y_terms(s, w, e, ny, yl, yh, minus, plus)
    s[SXY, :, e.y(ny - 1), :] = jnp.where(on_minus, traction[...], s[SXY, :, e.y(ny - 1), :])
    pack_stress_x(s, e, xu, xd)
    pack_stress_y(s, e, yu, yd)


def stress_last_body(
    nx, ny, rows, begin, holders, s, w, xl, xh, traction, mine, got, o_in, out, slip, state, own, sem
):
    del o_in
    e = Edges(nx, ny)
    early = slabs_out(ny, begin, nx - 2, s, out, sem)
    for c in early:
        c.start()
    on_minus, _ = fault_side()
    stress_x_terms(s, w, e, nx, xl, xh)
    copies = []
    for x in (0, 1, nx - 2, nx - 1):
        at = pl.ds(x * ny + ny - 1, 1)
        s[SXY, :, at, :] = jnp.where(on_minus, traction[:, x : x + 1, :], s[SXY, :, at, :])
    for j, x in enumerate((0, nx - 2)):
        span = pl.ds(x * ny, 2 * ny)
        for c in range(6):
            for k in range(s.shape[1]):
                copies.append(
                    pltpu.make_async_copy(
                        s.at[c, k, span], out.at[c, span, tile(k)], sem.at[6 + j * 6 + c, k]
                    )
                )
    for c in copies:
        c.start()
    half = lax.axis_size("normal") // 2
    at = pl.ds(rows * lax.rem(lax.axis_index("normal"), half), rows)
    have = holds(holders)
    for k in range(s.shape[1]):
        for q in range(2):
            own[q, :, tile(k)] = jnp.where(have, mine[q, k, at, :], got[q, k, at, :])
    for q, target in enumerate((slip, state)):
        copy = pltpu.make_async_copy(own.at[q], target, sem.at[18, q])
        copy.start()
        copies.append(copy)
    for c in early + copies:
        c.wait()


def own_body(state, mask, ids, out, st, mk, rg, sem):
    rows = state.shape[0]
    run(
        [
            pltpu.make_async_copy(a, b, sem.at[0, k])
            for k, (a, b) in enumerate(((state, st), (mask, mk), (ids, rg)))
        ]
    )
    out[0, 0:rows, :] = st[...]
    out[0, rows : 2 * rows, :] = mk[...].astype(F32)
    out[0, 2 * rows : 3 * rows, :] = rg[...].astype(F32)
    pad = out.shape[1] - 3 * rows
    if pad:
        out[0, 3 * rows :, :] = jnp.zeros((pad, out.shape[2]), F32)


def merge_body(bit, mine, got, out):
    upper = lax.rem(lax.axis_index("normal") // bit, 2) == 1
    n = mine.shape[0]
    a, b = mine[...], got[...]
    out[0:n] = jnp.where(upper, b, a)
    out[n : 2 * n] = jnp.where(upper, a, b)


def local(velocity, stress, modulus, buoyancy, fault_state, fault_mask, region_ids, friction_table):
    members = lax.axis_size("normal")
    _, nx, ny, nz = velocity.shape
    rows = fault_state.shape[0]
    flat, nt = nx * ny, nz // LANES
    pin = lambda x: pltpu.with_memory_space_constraint(x, pltpu.HBM)
    vel_in = velocity.reshape(3, flat, nz)
    str_in = pin(stress.reshape(6, flat, nz))
    mod_in = modulus.reshape(flat, nz)
    buo_in = buoyancy.reshape(flat, nz)
    fault_in = (pin(fault_state), pin(fault_mask), pin(region_ids))
    dma = lambda n: pltpu.SemaphoreType.DMA((n, nt))
    stage_cost = pl.CostEstimate(flops=4_000_000_000, bytes_accessed=16_000_000, transcendentals=0)
    part_cost = pl.CostEstimate(flops=2_000_000_000, bytes_accessed=8_000_000, transcendentals=0)
    side_cost = pl.CostEstimate(flops=1_000_000, bytes_accessed=1_000_000, transcendentals=0)

    depth = -(-3 * rows // 8) * 8
    (known,) = call(
        own_body, [HBM] * 3, [((1, depth, nz), VMEM)], fault_in,
        scratch=[pltpu.VMEM((rows, nz), F32)] + [pltpu.VMEM((rows, nz), jnp.int32)] * 2 + [dma(1)],
        cost=side_cost, name="own",
    )
    s, xu, xd, yu, yd = call(
        functools.partial(load_body, nx, ny), [HBM],
        [((6, nt, flat, LANES), VMEM), ((5, nt, ny, LANES), VMEM), ((4, nt, ny, LANES), VMEM),
         ((5, nt, nx, LANES), VMEM), ((4, nt, nx, LANES), VMEM)],
        (str_in,), scratch=[dma(6)], cost=side_cost, name="load",
    )
    tie = lax.optimization_barrier

    def merge(known, got, bit):
        return call(
            functools.partial(merge_body, bit), [VMEM] * 2, [((2 * bit, depth, nz), VMEM)],
            (known, got), cost=side_cost, name="merge",
        )[0]

    got = swap(known, 1)
    known, got, xu, xd, yu, yd = tie((known, got, xu, xd, yu, yd))
    known = merge(known, got, 1)
    known = merge(known, swap(known, 2), 2)
    bit = 4
    block_v = ((3, nt, flat, LANES), VMEM)
    block_s = ((6, nt, flat, LANES), VMEM)
    block_1 = ((nt, flat, LANES), VMEM)
    row_1 = ((nt, nx, LANES), VMEM)
    v = w = m = None
    for step in range(STEPS):
        first, last = step == 0, step == STEPS - 1
        xl, xh = shift_up(xu, "strike"), shift_down(xd, "strike")
        yl, yh = shift_up(yu, "normal"), shift_down(yd, "normal")
        if first:
            v, w, m = call(
                functools.partial(velocity_body, nx, ny, True), [VMEM, ANY, ANY, ANY],
                [block_v, block_1, block_1], (s, vel_in, buo_in, mod_in),
                scratch=[dma(4 * LOADS + 1)], cost=stage_cost, name="velocity_first",
            )
            while 2 * bit < members:
                known = merge(known, swap(known, bit), bit)
                bit *= 2
            known, v = tie((known, v))
        else:
            (v,) = call(
                functools.partial(velocity_body, nx, ny, False), [VMEM] * 3, [block_v], (s, v, w),
                aliases={1: 0}, cost=stage_cost, name="velocity",
            )
        extra = [known] if first else []
        sent = ((nt, nx + 3 * (nx // 2), LANES), VMEM) if first else row_1
        v, mine, traction = call(
            functools.partial(velocity_edges_body, nx, ny, rows if first else 0),
            [VMEM] * (7 + len(extra)), [block_v, sent, row_1], (v, w, s, xl, xh, yl, yh, *extra),
            aliases={0: 0}, cost=side_cost, name="velocity_edges",
        )
        other = swap_odd(mine, "normal")
        yu, yd = call(
            functools.partial(pack_velocity_y_body, nx, ny), [VMEM],
            [((4, nt, nx, LANES), VMEM), ((5, nt, nx, LANES), VMEM)], (v,), cost=side_cost,
            name="pack_normal",
        )
        yl, yh = shift_up(yu, "normal"), shift_down(yd, "normal")
        outs = [block_v, ((4, nt, ny, LANES), VMEM), ((5, nt, ny, LANES), VMEM)] + [row_1] * 4
        if last:
            outs.append(((2, nt, nx // 2, LANES), VMEM))
        elif first:
            outs.append(((5, nt, nx, LANES), VMEM))
        ins = [VMEM, VMEM, VMEM, SMEM, VMEM] if first else [VMEM] * 6
        args = (friction_table, v) if first else (par, state, v)
        got = call(
            functools.partial(fault_body, nx, ny, first, last), ins, outs,
            (mine, other, traction, *args), aliases={len(ins) - 1: 0}, cost=side_cost,
            name="fault",
        )
        if first:
            par = got[7]
        v, xu, xd, state, minus, plus, trac_new = got[:7]
        xl, xh = shift_up(xu, "strike"), shift_down(xd, "strike")
        body = functools.partial(stress_body, nx, ny, first)
        if last:
            half_rows = ((2, nt, nx // 2, LANES), VMEM)
            block_out = ((6, flat, nz), HBM)
            cuts = [2, 2 + (nx - 4) // 6 * 2 + 2, nx - 2 - (nx - 4) // 6 * 2, nx - 2]
            holders = [members // 2 - 1, members // 2]
            bit = members // 4
            back, s_out = got[7], None
            came = swap(back, bit)
            for part in range(3):
                ins, args, aliases, outs = [VMEM] * 4, [v, s, m, trac_new], {1: 0}, [block_s]
                if part == 0:
                    outs += [((3, flat, nz), HBM)]
                elif part == 1:
                    ins, args = ins + [VMEM] * 4, args + [yl, yh, minus, plus]
                    outs += [block_out]
                else:
                    ins, args = ins + [HBM], args + [s_out]
                    outs += [block_out]
                    aliases[4] = 1
                body = functools.partial(
                    last_slabs_body, nx, ny, part, cuts[part - 1] if part else None, cuts[part],
                    cuts[part + 1],
                )
                done = call(
                    body, ins, outs, args, scratch=[dma(3 if part == 0 else 6)], aliases=aliases,
                    cost=part_cost if part else stage_cost, name=f"last_slabs_{part}",
                )
                s = done[0]
                if part == 0:
                    v_out = done[1]
                else:
                    s_out = done[1]
                if bit > 1:
                    came, s = tie((came, s))
                    (back,) = call(
                        functools.partial(choose_body, tuple(holders)), [VMEM] * 2, [half_rows],
                        (back, came), cost=side_cost, name="choose",
                    )
                    holders += [h ^ bit for h in holders]
                    bit //= 2
                    came = swap(back, bit)
            s_out, slip, state_out = call(
                functools.partial(stress_last_body, nx, ny, rows, cuts[2], tuple(holders)),
                [VMEM] * 7 + [HBM], [block_out, ((rows, nz), HBM), ((rows, nz), HBM)],
                (s, m, xl, xh, trac_new, back, came, s_out),
                scratch=[pltpu.VMEM((2, rows, nz), F32), dma(19)],
                aliases={7: 0}, cost=side_cost, name="edges_last",
            )
            continue
        if first:
            s, m = call(
                body, [VMEM] * 3, [block_s, block_1], (v, s, m), aliases={1: 0, 2: 1},
                cost=stage_cost, name="stress_first",
            )
        else:
            (s,) = call(
                body, [VMEM] * 3, [block_s], (v, s, m), aliases={1: 0}, cost=stage_cost,
                name="stress",
            )
        s, xu, xd, yu, yd = call(
            functools.partial(stress_edges_body, nx, ny), [VMEM] * 9,
            [block_s, ((5, nt, ny, LANES), VMEM), ((4, nt, ny, LANES), VMEM),
             ((5, nt, nx, LANES), VMEM), ((4, nt, nx, LANES), VMEM)],
            (s, m, xl, xh, yl, yh, minus, plus, trac_new), aliases={0: 0}, cost=side_cost,
            name="stress_edges",
        )
    return (
        v_out.reshape(3, nx, ny, nz),
        s_out.reshape(6, nx, ny, nz),
        slip,
        state_out,
    )


def solution(mesh):
    block = P(None, "strike", "normal", None)
    part = P("strike", "normal", None)
    row = P(("strike", "normal"), None)
    return jax.shard_map(
        local,
        mesh=mesh,
        in_specs=(block, block, part, part, row, row, row, P()),
        out_specs=(block, block, row, row),
        check_vma=False,
    )
```

```python
import functools

import jax
import jax.numpy as jnp
from jax import lax
from jax.experimental import pallas as pl
from jax.experimental.pallas import tpu as pltpu
from jax.sharding import PartitionSpec as P

STEPS = 2
NEWTON = 4

C2 = -1.0 / 24.0
RATIO = (9.0 / 8.0) / C2
DT = 0.1
STEP = DT * C2
ETA = 1.0

F32 = jnp.float32
SXX, SYY, SZZ, SXY, SXZ, SYZ = range(6)


def shift_up(x, axis):
    count = lax.axis_size(axis)
    return lax.ppermute(x, axis, [(i, (i + 1) % count) for i in range(count)])


def shift_down(x, axis):
    count = lax.axis_size(axis)
    return lax.ppermute(x, axis, [((i + 1) % count, i) for i in range(count)])


def swap_odd(x, axis):
    count = lax.axis_size(axis)
    pairs = []
    for i in range(1, count, 2):
        j = (i + 1) % count
        pairs += [(i, j), (j, i)]
    return lax.ppermute(x, axis, pairs)


def swap(x, bit):
    count = lax.axis_size("normal")
    return lax.ppermute(x, "normal", [(i, i ^ bit) for i in range(count)])


VMEM = pl.BlockSpec(memory_space=pltpu.VMEM)
SMEM = pl.BlockSpec(memory_space=pltpu.SMEM)
HBM = pl.BlockSpec(memory_space=pltpu.HBM)
ANY = pl.BlockSpec(memory_space=pl.ANY)


def call(body, ins, outs, args, scratch=(), aliases=None, cost=None, name=None):
    shapes = [
        pltpu.VMEM(shape, F32) if spec is VMEM else jax.ShapeDtypeStruct(shape, F32)
        for shape, spec in outs
    ]
    return pl.pallas_call(
        body,
        out_shape=shapes,
        in_specs=ins,
        out_specs=[spec for _, spec in outs],
        scratch_shapes=list(scratch),
        input_output_aliases=aliases or {},
        compiler_params=pltpu.CompilerParams(vmem_limit_bytes=16 << 20),
        cost_estimate=cost,
        name=name,
    )(*args)


SUB, LANES = 8, 128


class Shifts:
    def __init__(self, ny):
        self.count = ny // SUB
        self.row = lax.broadcasted_iota(jnp.int32, (SUB, LANES), 0)
        self.lane = lax.broadcasted_iota(jnp.int32, (SUB, LANES), 1)

    def rows(self, here, ref, comp, slab, offset):
        edge = offset > 0
        keep = self.row < SUB - offset if edge else self.row >= -offset
        outer = self.count - 1 if edge else 0
        if here.static:
            turned = [[pltpu.roll(f, (-offset) % SUB, 0) for f in fs] for fs in slab]
            out = []
            for fs in turned:
                line = []
                for h, f in enumerate(fs):
                    j = h + 1 if edge else h - 1
                    line.append(jnp.where(keep, f, 0.0 if h == outer else fs[j]))
                out.append(line)
            return out
        return [
            [jnp.where(keep, f, 0.0) if h == outer else f for h, f in enumerate(fs)]
            for fs in here.load(ref, comp, 0, offset)
        ]

    def y_minus(self, here, ref, comp, slab):
        near = [self.rows(here, ref, comp, slab, o) for o in (-1, 1, -2)]
        return each(lambda f, b, c, d: RATIO * (f - b) + (c - d), slab, *near)

    def y_plus(self, here, ref, comp, slab):
        near = [self.rows(here, ref, comp, slab, o) for o in (1, 2, -1)]
        return each(lambda f, b, c, d: RATIO * (b - f) + (c - d), slab, *near)

    def lines(self, f, slab):
        columns = [f([fs[h] for fs in slab]) for h in range(self.count)]
        return [[column[k] for column in columns] for k in range(len(slab))]

    def z_minus(self, slab):
        def line(fs):
            n, lane = len(fs), self.lane
            r = [pltpu.roll(f, LANES - 1, 1) for f in fs]
            p = [jnp.where(lane < LANES - 1, r[k], r[k + 1] if k + 1 < n else 0.0) for k in range(n)]
            w = [RATIO * p[k] + fs[k] for k in range(n)]
            end = jnp.where(lane == LANES - 1, RATIO * r[0], 0.0)
            w[-1] = jnp.where(lane < LANES - 2, w[-1], end)
            q = [pltpu.roll(x, 2, 1) for x in w]
            return [RATIO * fs[k] + p[k] - jnp.where(lane >= 2, q[k], q[k - 1]) for k in range(n)]

        return self.lines(line, slab)

    def z_plus(self, slab):
        def line(fs):
            n, lane = len(fs), self.lane
            r = [pltpu.roll(f, 1, 1) for f in fs]
            m = [jnp.where(lane >= 1, r[k], r[k - 1] if k else 0.0) for k in range(n)]
            w = [RATIO * m[k] + fs[k] for k in range(n)]
            w[0] = jnp.where(lane >= 2, w[0], jnp.where(lane == 0, RATIO * r[-1], 0.0))
            q = [pltpu.roll(x, LANES - 2, 1) for x in w]
            return [
                jnp.where(lane < LANES - 2, q[k], q[(k + 1) % n]) - (RATIO * fs[k] + m[k])
                for k in range(n)
            ]

        return self.lines(line, slab)


def each(f, *slabs):
    return [[f(*pieces) for pieces in zip(*lines)] for lines in zip(*slabs)]


def add(*slabs):
    return each(lambda *parts: functools.reduce(lambda p, q: p + q, parts), *slabs)


def tile(k):
    return slice(k * LANES, (k + 1) * LANES)


def to_tiles(source, target, sems):
    return [
        pltpu.make_async_copy(source.at[:, tile(k)], target.at[k], sems.at[k])
        for k in range(target.shape[0])
    ]


def from_tiles(source, target, sems):
    return [
        pltpu.make_async_copy(source.at[k], target.at[:, tile(k)], sems.at[k])
        for k in range(source.shape[0])
    ]


def run(copies):
    for c in copies:
        c.start()
    for c in copies:
        c.wait()


class Slabs:
    def __init__(self, x, nx, ny, static):
        self.x, self.nx, self.ny, self.static = x, nx, ny, static

    def at(self, h, offset=0, row=0):
        start = (self.x + offset) * self.ny + h * SUB
        if not self.static:
            start = pl.multiple_of(start, SUB)
        return pl.ds(start + row, SUB)

    def load(self, ref, comp, offset=0, row=0):
        return [
            [ref[comp, k, self.at(h, offset, row), :] for h in range(self.ny // SUB)]
            for k in range(ref.shape[1])
        ]

    def near(self, ref, comp, offset):
        if self.static and not 0 <= self.x + offset < self.nx:
            return None
        return self.load(ref, comp, offset)

    def difference(self, ref, comp, a, b, c, d):
        total = None
        for p, q, factor in ((a, b, RATIO), (c, d, None)):
            p, q = self.near(ref, comp, p), self.near(ref, comp, q)
            if p is None and q is None:
                continue
            if p is None:
                term = each(lambda f: -f, q)
            else:
                term = p if q is None else each(lambda f, g: f - g, p, q)
            if factor is not None:
                term = each(lambda f: factor * f, term)
            total = term if total is None else add(total, term)
        return total

    def minus(self, ref, comp):
        return self.difference(ref, comp, 0, -1, 1, -2)

    def plus(self, ref, comp):
        return self.difference(ref, comp, 1, 0, 2, -1)


def run_slabs(begin, end, body):
    def step(i, carry):
        body(begin + 2 * i, False)
        body(begin + 2 * i + 1, False)
        return carry

    lax.fori_loop(0, (end - begin) // 2, step, 0)
    if (end - begin) % 2:
        body(end - 1, True)


def over_x(nx, body, parts=1, before=None):
    for j in range(parts):
        begin, end = nx * j // parts, nx * (j + 1) // parts
        if before is not None:
            before(j)
        first, last = max(begin, 2), min(end, nx - 2)
        for x in range(begin, first):
            body(x, True)
        run_slabs(first, last, body)
        for x in range(last, end):
            body(x, True)


LOADS = 2


def velocity_body(nx, ny, first, s, v_in, b_in, *refs):
    tiles = s.shape[1]
    before = None
    if first:
        m_in, v, bd, md, sem = refs
        loads = []
        for j in range(LOADS):
            at = pl.ds(nx * j // LOADS * ny, nx // LOADS * ny)
            pairs = [(b_in, bd)] + [(v_in.at[c], v.at[c]) for c in range(3)]
            loads.append(
                [
                    pltpu.make_async_copy(p.at[at, tile(k)], q.at[k, at], sem.at[4 * j + i, k])
                    for i, (p, q) in enumerate(pairs)
                    for k in range(tiles)
                ]
            )
        late = to_tiles(m_in, md, sem.at[4 * LOADS])
        for c in sum(loads, []) + late:
            c.start()

        def before(j):
            for c in loads[j]:
                c.wait()

    else:
        (v,) = refs
    sh = Shifts(ny)

    def body(x, static):
        here = Slabs(x, nx, ny, static)
        sxy, sxz, syz = here.load(s, SXY), here.load(s, SXZ), here.load(s, SYZ)
        syy = here.load(s, SYY)
        a = (
            add(here.plus(s, SXX), sh.y_minus(here, s, SXY, sxy), sh.z_minus(sxz)),
            add(here.minus(s, SXY), sh.y_plus(here, s, SYY, syy), sh.z_minus(syz)),
            add(here.minus(s, SXZ), sh.y_minus(here, s, SYZ, syz), sh.z_plus(here.load(s, SZZ))),
        )
        for k in range(tiles):
            for h in range(ny // SUB):
                at = here.at(h)
                if first:
                    w = STEP * bd[k, at, :]
                    bd[k, at, :] = w
                else:
                    w = b_in[k, at, :]
                for c in range(3):
                    v[c, k, at, :] = v[c, k, at, :] + w * a[c][k][h]

    over_x(nx, body, LOADS if first else 1, before)
    if first:
        for c in late:
            c.wait()


def stress_slabs(nx, ny, v, s, m_in, md):
    sh = Shifts(ny)

    def body(x, static):
        here = Slabs(x, nx, ny, static)
        vx, vy, vz = here.load(v, 0), here.load(v, 1), here.load(v, 2)
        exx, eyy, ezz = here.minus(v, 0), sh.y_minus(here, v, 1, vy), sh.z_minus(vz)
        exy = add(here.plus(v, 1), sh.y_plus(here, v, 0, vx))
        exz = add(here.plus(v, 2), sh.z_plus(vx))
        eyz = add(sh.z_plus(vy), sh.y_plus(here, v, 2, vz))
        tr = add(exx, eyy, ezz)
        for k in range(s.shape[1]):
            for h in range(ny // SUB):
                at = here.at(h)
                w = m_in[k, at, :]
                if md is not None:
                    w = STEP * w
                    md[k, at, :] = w
                for c, e in ((SXX, exx), (SYY, eyy), (SZZ, ezz)):
                    s[c, k, at, :] = s[c, k, at, :] + w * (tr[k][h] + 2.0 * e[k][h])
                for c, e in ((SXY, exy), (SXZ, exz), (SYZ, eyz)):
                    s[c, k, at, :] = s[c, k, at, :] + w * e[k][h]

    return body


def stress_body(nx, ny, first, v, s_in, m_in, s, *md):
    del s_in
    over_x(nx, stress_slabs(nx, ny, v, s, m_in, md[0] if first else None))


def slabs_out(ny, begin, end, s, out, sems):
    span = pl.ds(begin * ny, (end - begin) * ny)
    return [
        pltpu.make_async_copy(s.at[c, k, span], out.at[c, span, tile(k)], sems.at[c, k])
        for c in range(s.shape[0])
        for k in range(s.shape[1])
    ]


def last_slabs_body(nx, ny, part, before, begin, end, v, s_in, m, traction, *refs):
    del s_in
    e = Edges(nx, ny)
    on_minus, _ = fault_side()

    def fault_rows(begin, end):
        at = pl.ds(begin * ny + ny - 1, end - begin, stride=ny)
        s[SXY, :, at, :] = jnp.where(on_minus, traction[:, begin:end, :], s[SXY, :, at, :])

    if part == 0:
        s, v_out, sem = refs
        out = []
        for c in range(3):
            out += from_tiles(v.at[c], v_out.at[c], sem.at[c])
        for c in out:
            c.start()
    else:
        s, s_out, sem = refs[-3:]
        if part == 1:
            stress_y_terms(s, m, e, ny, *refs[:4])
            fault_rows(before, begin)
        out = slabs_out(ny, before, begin, s, s_out, sem)
        for c in out:
            c.start()
    body = stress_slabs(nx, ny, v, s, m, None)
    if part == 0:
        for x in (0, 1, nx - 2, nx - 1):
            body(x, True)
    run_slabs(begin, end, body)
    if part > 0:
        fault_rows(begin, end)
    for c in out:
        c.wait()


class Edges:
    def __init__(self, nx, ny):
        self.nx, self.ny = nx, ny

    def x(self, i):
        return pl.ds(i * self.ny, self.ny)

    def y(self, i):
        return pl.ds(i, self.nx, stride=self.ny)


def minus_edges(n, low, high):
    return (
        (0, -RATIO * low[1] - low[0]),
        (1, -low[1]),
        (n - 1, high[0]),
    )


def plus_edges(n, low, high):
    return (
        (0, -low[0]),
        (n - 1, RATIO * high[0] + high[1]),
        (n - 2, high[0]),
    )


def sides():
    out = []
    for axis in ("strike", "normal"):
        i = lax.axis_index(axis)
        last = lax.axis_size(axis) - 1
        out += [jnp.where(i > 0, 1.0, 0.0).astype(F32), jnp.where(i < last, 1.0, 0.0).astype(F32)]
    return out


def fault_side():
    position = lax.axis_index("normal")
    half = lax.axis_size("normal") // 2
    return position == half - 1, position == half


def stress_x_terms(s, w, e, nx, xl, xh):
    low, high = sides()[:2]
    a = [xl[k] * low for k in range(4)]
    b = [xh[k] * high for k in range(5)]
    for i, value in minus_edges(nx, a[0:2], b[0:1]):
        add_rows(s, SXX, w, e.x(i), 3.0, value)
        add_rows(s, SYY, w, e.x(i), 1.0, value)
        add_rows(s, SZZ, w, e.x(i), 1.0, value)
    for i, value in plus_edges(nx, a[2:3], b[1:3]):
        add_rows(s, SXY, w, e.x(i), 1.0, value)
    for i, value in plus_edges(nx, a[3:4], b[3:5]):
        add_rows(s, SXZ, w, e.x(i), 1.0, value)


def stress_y_terms(s, w, e, ny, yl, yh, minus, plus):
    low, high = sides()[2:]
    on_minus, on_plus = fault_side()
    a = [yl[k] * low for k in range(4)]
    b = [yh[k] * high for k in range(5)]
    a[2] = jnp.where(on_plus, minus[...], a[2])
    b[1] = jnp.where(on_minus, plus[...], b[1])
    for i, value in minus_edges(ny, a[0:2], b[0:1]):
        add_rows(s, SXX, w, e.y(i), 1.0, value)
        add_rows(s, SYY, w, e.y(i), 3.0, value)
        add_rows(s, SZZ, w, e.y(i), 1.0, value)
    for i, value in plus_edges(ny, a[2:3], b[1:3]):
        add_rows(s, SXY, w, e.y(i), 1.0, value)
    for i, value in plus_edges(ny, a[3:4], b[3:5]):
        add_rows(s, SYZ, w, e.y(i), 1.0, value)


def add_rows(ref, comp, w, at, factor, value):
    ref[comp, :, at, :] = ref[comp, :, at, :] + w[:, at, :] * (factor * value if factor != 1.0 else value)


def pack_stress_x(s, e, up, down):
    nx = e.nx
    for k, (c, i) in enumerate(
        ((SXX, nx - 1), (SXY, nx - 2), (SXY, nx - 1), (SXZ, nx - 2), (SXZ, nx - 1))
    ):
        up[k] = s[c, :, e.x(i), :]
    for k, (c, i) in enumerate(((SXX, 0), (SXX, 1), (SXY, 0), (SXZ, 0))):
        down[k] = s[c, :, e.x(i), :]


def pack_stress_y(s, e, up, down):
    ny = e.ny
    for k, (c, i) in enumerate(
        ((SYY, ny - 1), (SXY, ny - 2), (SXY, ny - 1), (SYZ, ny - 2), (SYZ, ny - 1))
    ):
        up[k] = s[c, :, e.y(i), :]
    for k, (c, i) in enumerate(((SYY, 0), (SYY, 1), (SXY, 0), (SYZ, 0))):
        down[k] = s[c, :, e.y(i), :]


def load_body(nx, ny, stress, s, xu, xd, yu, yd, sem):
    e = Edges(nx, ny)
    order = (SXX, SXY, SXZ, SYY, SYZ, SZZ)
    copies = {c: to_tiles(stress.at[c], s.at[c], sem.at[c]) for c in order}

    def wait(*comps):
        for c in comps:
            for copy in copies[c]:
                copy.wait()

    for c in order:
        for copy in copies[c]:
            copy.start()
    wait(SXX, SXY, SXZ)
    pack_stress_x(s, e, xu, xd)
    wait(SYY, SYZ)
    pack_stress_y(s, e, yu, yd)
    wait(SZZ)


def velocity_edges_body(nx, ny, rows, v_in, w, s, xl, xh, yl, yh, *refs):
    del v_in
    v, mine, traction = refs[-3:]
    e = Edges(nx, ny)
    fxl, fxh, fyl, fyh = sides()
    a = [xl[k] * fxl for k in range(5)]
    b = [xh[k] * fxh for k in range(4)]
    for comp, terms in (
        (0, plus_edges(nx, a[0:1], b[0:2])),
        (1, minus_edges(nx, a[1:3], b[2:3])),
        (2, minus_edges(nx, a[3:5], b[3:4])),
    ):
        for i, value in terms:
            add_rows(v, comp, w, e.x(i), 1.0, value)
    a = [yl[k] * fyl for k in range(5)]
    b = [yh[k] * fyh for k in range(4)]
    for comp, terms in (
        (1, plus_edges(ny, a[0:1], b[0:2])),
        (0, minus_edges(ny, a[1:3], b[2:3])),
        (2, minus_edges(ny, a[3:5], b[3:4])),
    ):
        for i, value in terms:
            add_rows(v, comp, w, e.y(i), 1.0, value)
    odd = lax.rem(lax.axis_index("normal"), 2) == 1
    mine[:, 0:nx, :] = jnp.where(odd, v[0, :, e.y(ny - 1), :], v[0, :, e.y(0), :])
    if rows:
        known = refs[0]
        count = known.shape[0] * rows
        for k in range(known.shape[0]):
            for q in range(3):
                at = slice(nx + q * count + k * rows, nx + q * count + (k + 1) * rows)
                for z in range(mine.shape[0]):
                    mine[z, at, :] = known[k, q * rows : (q + 1) * rows, tile(z)]
    traction[...] = jnp.where(odd, s[SXY, :, e.y(ny - 1), :], yl[2])


def pack_velocity_y_body(nx, ny, v, yu, yd):
    e = Edges(nx, ny)
    for k, (c, i) in enumerate(((1, ny - 2), (1, ny - 1), (0, ny - 1), (2, ny - 1))):
        yu[k] = v[c, :, e.y(i), :]
    for k, (c, i) in enumerate(((1, 0), (0, 0), (0, 1), (2, 0), (2, 1))):
        yd[k] = v[c, :, e.y(i), :]


def inverse_sinh(values):
    magnitude = jnp.abs(values)
    root = jnp.sqrt(1.0 + magnitude * magnitude)
    result = jnp.log1p(magnitude + magnitude * magnitude / (1.0 + root))
    return jnp.where(values < 0.0, -result, result)


def fault_parameters(nx, mine, other, table, state, par):
    half = nx // 2
    upper = lax.axis_index("normal") >= lax.axis_size("normal") // 2
    full = []
    for q in range(3):
        at = slice(nx + q * half, nx + (q + 1) * half)
        a, b = mine[:, at, :], other[:, at, :]
        full.append(jnp.concatenate((jnp.where(upper, b, a), jnp.where(upper, a, b)), 1))
    state[...] = full[0]
    par[0] = full[1]
    for j in range(4):
        p = jnp.zeros_like(full[2])
        for r in range(table.shape[1]):
            p = jnp.where(full[2] == float(r), table[j, r], p)
        par[1 + j] = p


def fault_body(nx, ny, first, last, *refs):
    if first:
        mine, other, traction, table, v_in, v, xu, xd, st, minus_o, plus_o, trac_o, par = refs[:13]
        fault_parameters(nx, mine, other, table, st, par)
        st_in = st
    else:
        mine, other, traction, par, st_in, v_in, v, xu, xd, st, minus_o, plus_o, trac_o = refs[:13]
    del v_in
    e = Edges(nx, ny)
    position = lax.axis_index("normal")
    members = lax.axis_size("normal")
    odd = lax.rem(position, 2) == 1
    on_minus, on_plus = fault_side()
    m, o = mine[:, 0:nx, :], other[:, 0:nx, :]
    minus = jnp.where(odd, m, o)
    plus = jnp.where(odd, o, m)
    mask, a, b, inv_len, sigma = (par[k] for k in range(5))
    state = st_in[...]
    locked = traction[...] + ETA * (plus - minus)
    c = 0.5 * jnp.exp(state / a)
    weight = sigma * a
    rate = jnp.zeros_like(locked)
    for _ in range(NEWTON):
        arg = c * rate
        residue = locked - ETA * rate - weight * inverse_sinh(arg)
        slope = ETA + weight * c / jnp.sqrt(1.0 + arg * arg)
        rate = rate + residue / slope
    rate = rate * mask
    state = state + DT * inv_len * (jnp.exp(-state / b) - jnp.abs(rate))
    st[...] = state
    trac_o[...] = locked - ETA * rate
    middle = 0.5 * (minus + plus)
    minus = middle - 0.5 * rate
    plus = middle + 0.5 * rate
    minus_o[...] = minus
    plus_o[...] = plus
    v[0, :, e.y(ny - 1), :] = jnp.where(on_minus, minus, v[0, :, e.y(ny - 1), :])
    v[0, :, e.y(0), :] = jnp.where(on_plus, plus, v[0, :, e.y(0), :])
    for k, (comp, i) in enumerate(((0, nx - 2), (0, nx - 1), (1, nx - 1), (2, nx - 1))):
        xu[k] = v[comp, :, e.x(i), :]
    for k, (comp, i) in enumerate(((0, 0), (1, 0), (1, 1), (2, 0), (2, 1))):
        xd[k] = v[comp, :, e.x(i), :]
    if last:
        (back,) = refs[13:]
        half = nx // 2
        upper = position >= members // 2
        for q, value in enumerate((rate, state)):
            back[q] = jnp.where(upper, value[:, half:, :], value[:, :half, :])


def choose_body(holders, mine, got, out):
    out[...] = jnp.where(holds(holders), mine[...], got[...])


def holds(holders):
    position = lax.axis_index("normal")
    return functools.reduce(lambda p, q: p | q, [position == h for h in holders])


def stress_edges_body(nx, ny, s_in, w, xl, xh, yl, yh, minus, plus, traction, s, xu, xd, yu, yd):
    del s_in
    e = Edges(nx, ny)
    on_minus, _ = fault_side()
    stress_x_terms(s, w, e, nx, xl, xh)
    stress_y_terms(s, w, e, ny, yl, yh, minus, plus)
    s[SXY, :, e.y(ny - 1), :] = jnp.where(on_minus, traction[...], s[SXY, :, e.y(ny - 1), :])
    pack_stress_x(s, e, xu, xd)
    pack_stress_y(s, e, yu, yd)


def stress_last_body(
    nx, ny, rows, begin, holders, s, w, xl, xh, traction, mine, got, o_in, out, slip, state, own, sem
):
    del o_in
    e = Edges(nx, ny)
    early = slabs_out(ny, begin, nx - 2, s, out, sem)
    for c in early:
        c.start()
    on_minus, _ = fault_side()
    stress_x_terms(s, w, e, nx, xl, xh)
    copies = []
    for x in (0, 1, nx - 2, nx - 1):
        at = pl.ds(x * ny + ny - 1, 1)
        s[SXY, :, at, :] = jnp.where(on_minus, traction[:, x : x + 1, :], s[SXY, :, at, :])
    for j, x in enumerate((0, nx - 2)):
        span = pl.ds(x * ny, 2 * ny)
        for c in range(6):
            for k in range(s.shape[1]):
                copies.append(
                    pltpu.make_async_copy(
                        s.at[c, k, span], out.at[c, span, tile(k)], sem.at[6 + j * 6 + c, k]
                    )
                )
    for c in copies:
        c.start()
    half = lax.axis_size("normal") // 2
    at = pl.ds(rows * lax.rem(lax.axis_index("normal"), half), rows)
    have = holds(holders)
    for k in range(s.shape[1]):
        for q in range(2):
            own[q, :, tile(k)] = jnp.where(have, mine[q, k, at, :], got[q, k, at, :])
    for q, target in enumerate((slip, state)):
        copy = pltpu.make_async_copy(own.at[q], target, sem.at[18, q])
        copy.start()
        copies.append(copy)
    for c in early + copies:
        c.wait()


def own_body(state, mask, ids, out, st, mk, rg, sem):
    rows = state.shape[0]
    run(
        [
            pltpu.make_async_copy(a, b, sem.at[0, k])
            for k, (a, b) in enumerate(((state, st), (mask, mk), (ids, rg)))
        ]
    )
    out[0, 0:rows, :] = st[...]
    out[0, rows : 2 * rows, :] = mk[...].astype(F32)
    out[0, 2 * rows : 3 * rows, :] = rg[...].astype(F32)
    pad = out.shape[1] - 3 * rows
    if pad:
        out[0, 3 * rows :, :] = jnp.zeros((pad, out.shape[2]), F32)


def merge_body(bit, mine, got, out):
    upper = lax.rem(lax.axis_index("normal") // bit, 2) == 1
    n = mine.shape[0]
    a, b = mine[...], got[...]
    out[0:n] = jnp.where(upper, b, a)
    out[n : 2 * n] = jnp.where(upper, a, b)


def local(velocity, stress, modulus, buoyancy, fault_state, fault_mask, region_ids, friction_table):
    members = lax.axis_size("normal")
    _, nx, ny, nz = velocity.shape
    rows = fault_state.shape[0]
    flat, nt = nx * ny, nz // LANES
    pin = lambda x: pltpu.with_memory_space_constraint(x, pltpu.HBM)
    vel_in = velocity.reshape(3, flat, nz)
    str_in = pin(stress.reshape(6, flat, nz))
    mod_in = modulus.reshape(flat, nz)
    buo_in = buoyancy.reshape(flat, nz)
    fault_in = (pin(fault_state), pin(fault_mask), pin(region_ids))
    dma = lambda n: pltpu.SemaphoreType.DMA((n, nt))
    stage_cost = pl.CostEstimate(flops=4_000_000_000, bytes_accessed=16_000_000, transcendentals=0)
    part_cost = pl.CostEstimate(flops=2_000_000_000, bytes_accessed=8_000_000, transcendentals=0)
    side_cost = pl.CostEstimate(flops=1_000_000, bytes_accessed=1_000_000, transcendentals=0)

    depth = -(-3 * rows // 8) * 8
    (known,) = call(
        own_body, [HBM] * 3, [((1, depth, nz), VMEM)], fault_in,
        scratch=[pltpu.VMEM((rows, nz), F32)] + [pltpu.VMEM((rows, nz), jnp.int32)] * 2 + [dma(1)],
        cost=side_cost, name="own",
    )
    s, xu, xd, yu, yd = call(
        functools.partial(load_body, nx, ny), [HBM],
        [((6, nt, flat, LANES), VMEM), ((5, nt, ny, LANES), VMEM), ((4, nt, ny, LANES), VMEM),
         ((5, nt, nx, LANES), VMEM), ((4, nt, nx, LANES), VMEM)],
        (str_in,), scratch=[dma(6)], cost=side_cost, name="load",
    )
    tie = lax.optimization_barrier

    def merge(known, got, bit):
        return call(
            functools.partial(merge_body, bit), [VMEM] * 2, [((2 * bit, depth, nz), VMEM)],
            (known, got), cost=side_cost, name="merge",
        )[0]

    got = swap(known, 1)
    known, got, xu, xd, yu, yd = tie((known, got, xu, xd, yu, yd))
    known = merge(known, got, 1)
    known = merge(known, swap(known, 2), 2)
    bit = 4
    block_v = ((3, nt, flat, LANES), VMEM)
    block_s = ((6, nt, flat, LANES), VMEM)
    block_1 = ((nt, flat, LANES), VMEM)
    row_1 = ((nt, nx, LANES), VMEM)
    v = w = m = None
    for step in range(STEPS):
        first, last = step == 0, step == STEPS - 1
        xl, xh = shift_up(xu, "strike"), shift_down(xd, "strike")
        yl, yh = shift_up(yu, "normal"), shift_down(yd, "normal")
        if first:
            v, w, m = call(
                functools.partial(velocity_body, nx, ny, True), [VMEM, ANY, ANY, ANY],
                [block_v, block_1, block_1], (s, vel_in, buo_in, mod_in),
                scratch=[dma(4 * LOADS + 1)], cost=stage_cost, name="velocity_first",
            )
            while 2 * bit < members:
                known = merge(known, swap(known, bit), bit)
                bit *= 2
            known, v = tie((known, v))
        else:
            (v,) = call(
                functools.partial(velocity_body, nx, ny, False), [VMEM] * 3, [block_v], (s, v, w),
                aliases={1: 0}, cost=stage_cost, name="velocity",
            )
        extra = [known] if first else []
        sent = ((nt, nx + 3 * (nx // 2), LANES), VMEM) if first else row_1
        v, mine, traction = call(
            functools.partial(velocity_edges_body, nx, ny, rows if first else 0),
            [VMEM] * (7 + len(extra)), [block_v, sent, row_1], (v, w, s, xl, xh, yl, yh, *extra),
            aliases={0: 0}, cost=side_cost, name="velocity_edges",
        )
        other = swap_odd(mine, "normal")
        yu, yd = call(
            functools.partial(pack_velocity_y_body, nx, ny), [VMEM],
            [((4, nt, nx, LANES), VMEM), ((5, nt, nx, LANES), VMEM)], (v,), cost=side_cost,
            name="pack_normal",
        )
        yl, yh = shift_up(yu, "normal"), shift_down(yd, "normal")
        outs = [block_v, ((4, nt, ny, LANES), VMEM), ((5, nt, ny, LANES), VMEM)] + [row_1] * 4
        if last:
            outs.append(((2, nt, nx // 2, LANES), VMEM))
        elif first:
            outs.append(((5, nt, nx, LANES), VMEM))
        ins = [VMEM, VMEM, VMEM, SMEM, VMEM] if first else [VMEM] * 6
        args = (friction_table, v) if first else (par, state, v)
        got = call(
            functools.partial(fault_body, nx, ny, first, last), ins, outs,
            (mine, other, traction, *args), aliases={len(ins) - 1: 0}, cost=side_cost,
            name="fault",
        )
        if first:
            par = got[7]
        v, xu, xd, state, minus, plus, trac_new = got[:7]
        xl, xh = shift_up(xu, "strike"), shift_down(xd, "strike")
        body = functools.partial(stress_body, nx, ny, first)
        if last:
            half_rows = ((2, nt, nx // 2, LANES), VMEM)
            block_out = ((6, flat, nz), HBM)
            cuts = [2, 2 + (nx - 4) // 6 * 2 + 2, nx - 2 - (nx - 4) // 6 * 2, nx - 2]
            holders = [members // 2 - 1, members // 2]
            bit = members // 4
            back, s_out = got[7], None
            came = swap(back, bit)
            for part in range(3):
                ins, args, aliases, outs = [VMEM] * 4, [v, s, m, trac_new], {1: 0}, [block_s]
                if part == 0:
                    outs += [((3, flat, nz), HBM)]
                elif part == 1:
                    ins, args = ins + [VMEM] * 4, args + [yl, yh, minus, plus]
                    outs += [block_out]
                else:
                    ins, args = ins + [HBM], args + [s_out]
                    outs += [block_out]
                    aliases[4] = 1
                body = functools.partial(
                    last_slabs_body, nx, ny, part, cuts[part - 1] if part else None, cuts[part],
                    cuts[part + 1],
                )
                done = call(
                    body, ins, outs, args, scratch=[dma(3 if part == 0 else 6)], aliases=aliases,
                    cost=part_cost if part else stage_cost, name=f"last_slabs_{part}",
                )
                s = done[0]
                if part == 0:
                    v_out = done[1]
                else:
                    s_out = done[1]
                if bit > 1:
                    came, s = tie((came, s))
                    (back,) = call(
                        functools.partial(choose_body, tuple(holders)), [VMEM] * 2, [half_rows],
                        (back, came), cost=side_cost, name="choose",
                    )
                    holders += [h ^ bit for h in holders]
                    bit //= 2
                    came = swap(back, bit)
            s_out, slip, state_out = call(
                functools.partial(stress_last_body, nx, ny, rows, cuts[2], tuple(holders)),
                [VMEM] * 7 + [HBM], [block_out, ((rows, nz), HBM), ((rows, nz), HBM)],
                (s, m, xl, xh, trac_new, back, came, s_out),
                scratch=[pltpu.VMEM((2, rows, nz), F32), dma(19)],
                aliases={7: 0}, cost=side_cost, name="edges_last",
            )
            continue
        if first:
            s, m = call(
                body, [VMEM] * 3, [block_s, block_1], (v, s, m), aliases={1: 0, 2: 1},
                cost=stage_cost, name="stress_first",
            )
        else:
            (s,) = call(
                body, [VMEM] * 3, [block_s], (v, s, m), aliases={1: 0}, cost=stage_cost,
                name="stress",
            )
        s, xu, xd, yu, yd = call(
            functools.partial(stress_edges_body, nx, ny), [VMEM] * 9,
            [block_s, ((5, nt, ny, LANES), VMEM), ((4, nt, ny, LANES), VMEM),
             ((5, nt, nx, LANES), VMEM), ((4, nt, nx, LANES), VMEM)],
            (s, m, xl, xh, yl, yh, minus, plus, trac_new), aliases={0: 0}, cost=side_cost,
            name="stress_edges",
        )
    return (
        v_out.reshape(3, nx, ny, nz),
        s_out.reshape(6, nx, ny, nz),
        slip,
        state_out,
    )


def solution(mesh):
    block = P(None, "strike", "normal", None)
    part = P("strike", "normal", None)
    row = P(("strike", "normal"), None)
    return jax.shard_map(
        local,
        mesh=mesh,
        in_specs=(block, block, part, part, row, row, row, P()),
        out_specs=(block, block, row, row),
        check_vma=False,
    )
```
